256 devices in a mesh: shot: 32 (over x_hi, z, core), depth: 8 (over x_lo, y).
Axes of the slice: x: 4 (x_hi: 2, x_lo: 2; x = x_hi * 2 + x_lo), y: 4, z: 8, core: 2. Of those that a mesh axis runs over, the one named last changes fastest.
Arguments:
- u_prev: float32 [32, 64, 128, 128], P('shot', None, 'depth'), may hold values from -8 to 8.5
- u_cur: float32 [32, 64, 128, 128], P('shot', None, 'depth'), may hold values from -8 to 8.5
- a_prev: float32 [32, 64, 128, 128], P('shot', None, 'depth'), may hold values from -8 to 8.5
- a_cur: float32 [32, 64, 128, 128], P('shot', None, 'depth'), may hold values from -8 to 8.5
- model: float32 [64, 128, 128], P('shot', 'depth'), may hold values from 0.03 to 0.09
- aniso_h: float32 [64, 128, 128], P('shot', 'depth'), may hold values from 0.7 to 1.5
- aniso_c: float32 [64, 128, 128], P('shot', 'depth'), may hold values from -0.5 to 0.5
- smooth_coef: float32 [64, 128, 128], P('shot', 'depth'), may hold values from 0.02 to 0.16
- bin_onehot: int32 [16, 16, 4], P(None, 'depth'), may hold values from 0 to 1, as said below
- shot_group: int32 [32], P('shot'), may hold values from 0 to 15
- src_cell: int32 [32], P('shot'), may hold values from 0 to 1048575
- rec_cell: int32 [32, 128], P('shot'), may hold values from 0 to 1048575
- src_wave: float32 [32, 3], P('shot'), may hold values from -6 to 6
- rec_data: float32 [32, 2, 128], P('shot'), may hold values from -6 to 6
Outputs:
- model_next: float32 [64, 128, 128], P('shot', 'depth')
- grad_dir: float32 [64, 128, 128], P('shot', 'depth')
- wave_next: float32 [32, 64, 128, 128], P('shot', None, 'depth')
The draws below stay inside these ranges and needn't reach their ends.
Inputs may be any that keep to these rules, and one draw needn't show every extreme that they name: `bin_onehot`: each entry along the last dimension is one-hot: exactly one 1 per row.
All inputs are finite; a program needn't handle non-finite values.
Results may differ from the reference program's by a relative error of at most 0.000092.
Values sent between devices are 32-bit elements; how exact they have to be, the bound alone decides.
No kernel may reach another device: no remote copies, remote signals or barrier semaphores. Data moves between devices by JAX's collectives and lax.ppermute only.
A program may use at most 64 MiB of HBM per device.

```python
import math
import jax
import jax.numpy as jnp
from jax import lax

NX = 64
NY = 128
NREC = 128
STEPS = 2
GROUPS = 16
BZ = 8
NBINS = 4
NZ = 128
SHOTS = 32
NBLK = 16


def wave_field(key, salt):
    key = jax.random.fold_in(key, salt)
    along_x = jnp.arange(NX, dtype=jnp.float32) / NX
    along_z = jnp.arange(NZ, dtype=jnp.float32) / NZ
    base = jnp.clip(jax.random.normal(key, (SHOTS, NX, NZ, NY), jnp.float32), -5.0, 5.0)
    growth = jnp.exp2(0.585 * along_x)[:, None, None] * jnp.exp2(0.585 * along_z)[None, :, None]
    return 0.5 * growth * base


def draw_u_prev(key, part):
    return wave_field(key, 11)


def draw_u_cur(key, part):
    return wave_field(key, 12)


def draw_a_prev(key, part):
    return wave_field(key, 13)


def draw_a_cur(key, part):
    return wave_field(key, 14)


def draw_bin_onehot(key, part):
    chosen = jax.random.randint(jax.random.fold_in(key, 21), (GROUPS, NBLK), 0, NBINS)
    return (chosen[:, :, None] == jnp.arange(NBINS, dtype=jnp.int32)).astype(jnp.int32)


def plant(values, rng, least, high):
    extent = values.shape
    spot = [jax.random.randint(jax.random.fold_in(rng, axis), (), 0, extent[axis]) for axis in range(len(extent))]
    values = values.at[tuple(spot)].set(least)
    longest = extent.index(max(extent))
    spot[longest] = (spot[longest] + 1) % extent[longest]
    return values.at[tuple(spot)].set(high)


def block_scale(own_key, dims, pieces, low, largest):
    level = 1.0
    for dim, blocks in pieces:
        steps = jax.random.uniform(jax.random.fold_in(jax.random.fold_in(own_key, 6), dim), (blocks,), jnp.float32, low / len(pieces), largest / len(pieces))
        level = level * jnp.repeat(jnp.exp(steps), dims[dim] // blocks).reshape((-1,) + (1,) * (len(dims) - 1 - dim))
    return level


def centred(own_key, extent, deviation, bound, pieces=(), kind=jnp.bfloat16):
    level = block_scale(own_key, extent, pieces, -0.22, 0.18) if pieces else 1.0
    values = jax.random.normal(own_key, extent, jnp.float32) * deviation * level
    return jnp.minimum(jnp.maximum(values, -bound), bound).astype(kind)


def setup_inputs(seed: int = 0) -> dict:
    keys = jax.random.split(jax.random.key(seed), 15)
    return {
        "u_prev": draw_u_prev(jax.random.fold_in(keys[14], 71), 0),
        "u_cur": draw_u_cur(jax.random.fold_in(keys[14], 71), 0),
        "a_prev": draw_a_prev(jax.random.fold_in(keys[14], 71), 0),
        "a_cur": draw_a_cur(jax.random.fold_in(keys[14], 71), 0),
        "model": jnp.clip(jnp.exp(math.log(0.09) - 1.09861235 * jax.random.uniform(keys[4], (NX, NZ, NY), jnp.float32) ** block_scale(keys[4], (NX, NZ, NY), ((0, 32), (1, 8)), -0.2, 0.2)), 0.03, 0.09),
        "aniso_h": jnp.clip(jnp.exp(math.log(1.5) - 0.7621401 * jax.random.uniform(keys[5], (NX, NZ, NY), jnp.float32) ** block_scale(keys[5], (NX, NZ, NY), ((0, 32), (1, 8)), -0.2, 0.2)), 0.7, 1.5),
        "aniso_c": jnp.clip(jax.random.uniform(keys[6], (NX, NZ, NY), jnp.float32, -0.5, 0.5) * block_scale(keys[6], (NX, NZ, NY), ((0, 32), (1, 8)), -0.4, 0.0), -0.5, 0.5),
        "smooth_coef": jnp.clip(0.02 + 0.14 * jax.random.uniform(keys[7], (NX, NZ, NY), jnp.float32) ** block_scale(keys[7], (NX, NZ, NY), ((0, 32), (1, 8)), -0.2, 0.2), 0.02, 0.16),
        "bin_onehot": draw_bin_onehot(jax.random.fold_in(keys[14], 71), 0),
        "shot_group": plant(jax.random.randint(keys[9], (SHOTS,), 0, GROUPS), jax.random.fold_in(keys[9], 1), 0, GROUPS - 1).astype(jnp.int32),
        "src_cell": plant(jax.random.randint(keys[10], (SHOTS,), 0, NX * NZ * NY), jax.random.fold_in(keys[10], 1), 0, (NX * NZ * NY) - 1).astype(jnp.int32),
        "rec_cell": plant(jax.random.randint(keys[11], (SHOTS, NREC), 0, NX * NZ * NY), jax.random.fold_in(keys[11], 1), 0, (NX * NZ * NY) - 1).astype(jnp.int32),
        "src_wave": centred(keys[12], (SHOTS, STEPS + 1), 1.0, 6.0, ((0, 32),), jnp.float32),
        "rec_data": centred(keys[13], (SHOTS, STEPS, NREC), 1.0, 6.0, ((0, 32),), jnp.float32),
    }


second_coef = (-205.0 / 72.0, 8.0 / 5.0, -1.0 / 5.0, 8.0 / 315.0, -1.0 / 560.0)
first_coef = (0.8, -0.2, 4.0 / 105.0, -1.0 / 280.0)

def pad_axis(field, axis, width):
    widths = [(0, 0)] * field.ndim
    widths[axis] = (width, width)
    return jnp.pad(field, widths)

def shifted(padded, axis, offset, count):
    return lax.slice_in_dim(padded, 4 + offset, 4 + offset + count, axis=axis)

def second_along(padded, axis, count):
    result = second_coef[0] * shifted(padded, axis, 0, count)
    for offset in range(1, 5):
        result = result + second_coef[offset] * (shifted(padded, axis, offset, count) + shifted(padded, axis, -offset, count))
    return result

def first_along(padded, axis, count):
    result = first_coef[0] * (shifted(padded, axis, 1, count) - shifted(padded, axis, -1, count))
    for offset in range(2, 5):
        result = result + first_coef[offset - 1] * (shifted(padded, axis, offset, count) - shifted(padded, axis, -offset, count))
    return result

def apply_operator(padded_z, aniso_h, aniso_c):
    ndim = padded_z.ndim
    axis_x, axis_z, axis_y = (ndim - 3, ndim - 2, ndim - 1)
    count_z = padded_z.shape[axis_z] - 8
    count_x = padded_z.shape[axis_x]
    count_y = padded_z.shape[axis_y]
    centre = lax.slice_in_dim(padded_z, 4, 4 + count_z, axis=axis_z)
    depth_two = second_along(padded_z, axis_z, count_z)
    depth_one = first_along(padded_z, axis_z, count_z)
    lateral = second_along(pad_axis(centre, axis_x, 4), axis_x, count_x) + second_along(pad_axis(centre, axis_y, 4), axis_y, count_y)
    crossing = first_along(pad_axis(depth_one, axis_x, 4), axis_x, count_x)
    return aniso_h * lateral + depth_two + aniso_c * crossing

def relax_once(padded, centre, coef):
    neighbours = padded[2:, 1:-1, 1:-1] + padded[:-2, 1:-1, 1:-1]
    neighbours = neighbours + padded[1:-1, 2:, 1:-1] + padded[1:-1, :-2, 1:-1]
    neighbours = neighbours + padded[1:-1, 1:-1, 2:] + padded[1:-1, 1:-1, :-2]
    return centre + coef * (neighbours - 6.0 * centre)

def reference(u_prev, u_cur, a_prev, a_cur, model, aniso_h, aniso_c, smooth_coef, bin_onehot, shot_group, src_cell, rec_cell, src_wave, rec_data):
    cells = NX * NZ * NY
    powers = jnp.exp2(-jnp.arange(NBINS).astype(u_cur.dtype))
    block_weight = lax.optimization_barrier(jnp.sum(bin_onehot.astype(u_cur.dtype) * powers, axis=2))
    shot_weight = jnp.repeat(block_weight[shot_group], BZ, axis=1)

    def operate(field):
        return apply_operator(pad_axis(field, 1, 4), aniso_h, aniso_c)

    def one_shot(carry, items):
        older, wave, adj_old, adjoint, source, amplitude, receivers, records, weight = items
        gradient = jnp.zeros_like(wave)
        for step_index in range(STEPS):
            applied = operate(wave)
            adj_applied = operate(adjoint)
            gradient = gradient + adjoint * applied
            src_field = jnp.zeros((cells,), wave.dtype).at[source].add(amplitude[step_index]).reshape(NX, NZ, NY)
            rec_field = jnp.zeros((cells,), wave.dtype).at[receivers].add(records[step_index]).reshape(NX, NZ, NY)
            next_wave = 2.0 * wave - older + model * applied + src_field
            next_adj = 2.0 * adjoint - adj_old + model * adj_applied + rec_field
            older, wave = (wave, next_wave)
            adj_old, adjoint = (adjoint, next_adj)
        carry = carry + weight[None, :, None] * gradient
        return (carry, (older, wave))
    summed, (earlier, latest) = lax.scan(one_shot, jnp.zeros((NX, NZ, NY), u_cur.dtype), (u_prev, u_cur, a_prev, a_cur, src_cell, src_wave, rec_cell, rec_data, shot_weight))
    smoothed = summed
    for sweep_index in range(2):
        smoothed = relax_once(jnp.pad(smoothed, 1), smoothed, smooth_coef)
    square_sum = jnp.sum(smoothed * smoothed)
    norm_scale = jnp.sqrt(square_sum / (NX * NZ * NY) + 1e-06)
    grad_dir = smoothed / norm_scale
    model_next = model * (1.0 - 0.25 * jnp.tanh(grad_dir))

    def final_step(items):
        older, wave, source, amplitude = items
        src_field = jnp.zeros((cells,), wave.dtype).at[source].add(amplitude[STEPS]).reshape(NX, NZ, NY)
        applied = apply_operator(pad_axis(wave, 1, 4), aniso_h, aniso_c)
        return 2.0 * wave - older + model_next * applied + src_field
    wave_next = lax.map(final_step, (earlier, latest, src_cell, src_wave))
    return (model_next, grad_dir, wave_next)
```

```python
import jax
import jax.numpy as jnp
from jax import lax
from jax.sharding import PartitionSpec as P

second_coef = (-205.0 / 72.0, 8.0 / 5.0, -1.0 / 5.0, 8.0 / 315.0, -1.0 / 560.0)
first_coef = (0.8, -0.2, 4.0 / 105.0, -1.0 / 280.0)


def pad_axis(field, axis, width):
    widths = [(0, 0)] * field.ndim
    widths[axis] = (width, width)
    return jnp.pad(field, widths)


def shifted(padded, axis, offset, count):
    return lax.slice_in_dim(padded, 4 + offset, 4 + offset + count, axis=axis)


def second_along(padded, axis, count):
    result = second_coef[0] * shifted(padded, axis, 0, count)
    for offset in range(1, 5):
        result = result + second_coef[offset] * (
            shifted(padded, axis, offset, count) + shifted(padded, axis, -offset, count)
        )
    return result


def first_along(padded, axis, count):
    result = first_coef[0] * (shifted(padded, axis, 1, count) - shifted(padded, axis, -1, count))
    for offset in range(2, 5):
        result = result + first_coef[offset - 1] * (
            shifted(padded, axis, offset, count) - shifted(padded, axis, -offset, count)
        )
    return result


def apply_operator(padded_z, aniso_h, aniso_c):
    ndim = padded_z.ndim
    axis_x, axis_z, axis_y = (ndim - 3, ndim - 2, ndim - 1)
    count_z = padded_z.shape[axis_z] - 8
    count_x = padded_z.shape[axis_x]
    count_y = padded_z.shape[axis_y]
    centre = lax.slice_in_dim(padded_z, 4, 4 + count_z, axis=axis_z)
    depth_two = second_along(padded_z, axis_z, count_z)
    depth_one = first_along(padded_z, axis_z, count_z)
    lateral = second_along(pad_axis(centre, axis_x, 4), axis_x, count_x) + second_along(
        pad_axis(centre, axis_y, 4), axis_y, count_y
    )
    crossing = first_along(pad_axis(depth_one, axis_x, 4), axis_x, count_x)
    return aniso_h * lateral + depth_two + aniso_c * crossing


def relax_once(padded, centre, coef):
    neighbours = padded[2:, 1:-1, 1:-1] + padded[:-2, 1:-1, 1:-1]
    neighbours = neighbours + padded[1:-1, 2:, 1:-1] + padded[1:-1, :-2, 1:-1]
    neighbours = neighbours + padded[1:-1, 1:-1, 2:] + padded[1:-1, 1:-1, :-2]
    return centre + coef * (neighbours - 6.0 * centre)


SHOT = ("xh", "z", "core")
DEPTH = ("xl", "y")
PEERS = ("xh", "z")
SWAP = [(0, 1), (1, 0)]


def both_cores(mine):
    other = lax.ppermute(mine, "core", SWAP)
    first = lax.axis_index("core") == 0
    return jnp.stack([jnp.where(first, mine, other), jnp.where(first, other, mine)], axis=1)


def gather_rows(block):
    peers = lax.axis_size(PEERS)
    spread = jnp.broadcast_to(block[None], (peers, *block.shape))
    mine = lax.all_to_all(spread, PEERS, 0, 0, tiled=True)
    return both_cores(mine)


def halo(block, dim, width):
    count = lax.axis_size(DEPTH)
    forward = [(i, i + 1) for i in range(count - 1)]
    backward = [(target, source) for source, target in forward]
    low = lax.ppermute(
        lax.slice_in_dim(block, block.shape[dim] - width, None, axis=dim), DEPTH, forward
    )
    high = lax.ppermute(lax.slice_in_dim(block, 0, width, axis=dim), DEPTH, backward)
    return low, high


def extended_z(block, dim, width):
    low, high = halo(block, dim, width)
    return jnp.concatenate([low, block, high], axis=dim)


def body(
    u_prev,
    u_cur,
    a_prev,
    a_cur,
    model,
    aniso_h,
    aniso_c,
    smooth_coef,
    bin_onehot,
    shot_group,
    src_cell,
    rec_cell,
    src_wave,
    rec_data,
):
    shot_count, cells_x, cells_z, cells_y = u_cur.shape
    depth_cells = cells_z * lax.axis_size(DEPTH)
    z_start = lax.axis_index(DEPTH) * cells_z
    rows = model.shape[0]
    own = jnp.stack([model, aniso_h, aniso_c, smooth_coef])
    slabs = gather_rows(own)
    slabs = jnp.moveaxis(slabs, 2, 0).reshape(4, cells_x, cells_z, cells_y)
    model_slab, aniso_hs, aniso_cs, coef_slab = slabs[0], slabs[1], slabs[2], slabs[3]
    x_pos = lax.broadcasted_iota(jnp.int32, (cells_x, cells_z, cells_y), 0)
    z_pos = lax.broadcasted_iota(jnp.int32, (cells_x, cells_z, cells_y), 1) + z_start
    y_pos = lax.broadcasted_iota(jnp.int32, (cells_x, cells_z, cells_y), 2)
    flat_pos = (x_pos * depth_cells + z_pos) * cells_y + y_pos
    receiver_x = rec_cell // (depth_cells * cells_y)
    receiver_z = rec_cell // cells_y % depth_cells
    receiver_y = rec_cell % cells_y
    receivers = rec_cell.shape[1]

    def source_term(step_index):
        hits = flat_pos[None] == src_cell[:, None, None, None]
        return jnp.where(hits, src_wave[:, step_index][:, None, None, None], 0.0)

    def receiver_term(step_index):
        records = rec_data[:, step_index]
        along_x = (receiver_x[..., None] == jnp.arange(cells_x, dtype=jnp.int32)).astype(
            jnp.float32
        ) * records[..., None]
        along_z = (receiver_z[..., None] == z_start + jnp.arange(cells_z, dtype=jnp.int32)).astype(
            jnp.float32
        )
        along_y = (receiver_y[..., None] == jnp.arange(cells_y, dtype=jnp.int32)).astype(
            jnp.float32
        )
        plane = (along_x[..., :, None] * along_z[..., None, :]).reshape(
            shot_count, receivers, cells_x * cells_z
        )
        placed = jnp.einsum("srk,sry->sky", plane, along_y, precision=lax.Precision.HIGHEST)
        return placed.reshape(shot_count, cells_x, cells_z, cells_y)

    wave, adjoint = u_cur, a_cur
    wave_old, adjoint_old = u_prev, a_prev
    gradient = jnp.zeros_like(u_cur)
    for step_index in range(rec_data.shape[1]):
        pair = extended_z(jnp.stack([wave, adjoint]), 3, 4) if step_index == 0 else None
        wave_ext = pair[0] if step_index == 0 else extended_z(wave, 2, 4)
        adjoint_ext = pair[1] if step_index == 0 else extended_z(adjoint, 2, 4)
        applied = apply_operator(wave_ext, aniso_hs, aniso_cs)
        adjoint_applied = apply_operator(adjoint_ext, aniso_hs, aniso_cs)
        gradient = gradient + adjoint * applied
        wave_new = 2.0 * wave - wave_old + model_slab * applied + source_term(step_index)
        adjoint_new = (
            2.0 * adjoint - adjoint_old + model_slab * adjoint_applied + receiver_term(step_index)
        )
        wave_old, wave = wave, wave_new
        adjoint_old, adjoint = adjoint, adjoint_new
    nbins = bin_onehot.shape[2]
    groups = bin_onehot.shape[0]
    powers = jnp.exp2(-jnp.arange(nbins, dtype=jnp.float32))
    block_weight = jnp.sum(bin_onehot.astype(jnp.float32) * powers, axis=2)
    chosen = (shot_group[:, None] == jnp.arange(groups, dtype=jnp.int32)).astype(jnp.float32)
    shot_weight = jnp.dot(chosen, block_weight, precision=lax.Precision.HIGHEST)
    depth_weight = jnp.repeat(shot_weight, cells_z // bin_onehot.shape[1], axis=1)
    local_sum = jnp.sum(depth_weight[:, None, :, None] * gradient, axis=0)
    total_cells = cells_x * depth_cells * cells_y

    peers = lax.axis_size(PEERS)
    core = lax.axis_index("core")
    parts = local_sum.reshape(peers, 2, rows, cells_z, cells_y)
    keep = jnp.where(core == 0, parts[:, 0], parts[:, 1])
    send = jnp.where(core == 0, parts[:, 1], parts[:, 0])
    chip_sum = keep + lax.ppermute(send, "core", SWAP)
    summed = jnp.sum(lax.all_to_all(chip_sum, PEERS, 0, 0, tiled=True), axis=0)
    summed = gather_rows(summed).reshape(cells_x, cells_z, cells_y)

    coef_ext = extended_z(coef_slab, 1, 1)
    low, high = halo(summed, 1, 2)
    wide = jnp.concatenate([low, summed, high], axis=1)
    index = lax.axis_index(DEPTH)
    inside = jnp.ones((cells_z + 2,), jnp.float32)
    inside = inside.at[0].set(jnp.where(index == 0, 0.0, 1.0))
    inside = inside.at[cells_z + 1].set(jnp.where(index == lax.axis_size(DEPTH) - 1, 0.0, 1.0))
    around = jnp.pad(wide, ((1, 1), (0, 0), (1, 1)))
    once = relax_once(around, wide[:, 1:-1], coef_ext) * inside[None, :, None]
    around = jnp.pad(once, ((1, 1), (0, 0), (1, 1)))
    smoothed = relax_once(around, once[:, 1:-1], coef_slab)
    slab_square = jnp.sum(smoothed * smoothed)
    squares = jnp.broadcast_to(slab_square, (lax.axis_size(DEPTH), 1, 128))
    square_sum = jnp.sum(lax.all_to_all(squares, DEPTH, 0, 0, tiled=True)[:, 0, 0])
    norm_scale = jnp.sqrt(square_sum / total_cells + 1e-06)
    direction = smoothed / norm_scale
    model_full = model_slab * (1.0 - 0.25 * jnp.tanh(direction))
    final_applied = apply_operator(extended_z(wave, 2, 4), aniso_hs, aniso_cs)
    wave_next = 2.0 * wave - wave_old + model_full * final_applied + source_term(rec_data.shape[1])
    start = lax.axis_index(SHOT) * rows
    model_next = lax.dynamic_slice_in_dim(model_full, start, rows, axis=0)
    grad_dir = lax.dynamic_slice_in_dim(direction, start, rows, axis=0)
    return (model_next, grad_dir, wave_next)


def solution(mesh):
    mesh = jax.sharding.Mesh(
        mesh.devices.reshape(2, 8, 2, 2, 4), ("xh", "z", "core", "xl", "y")
    )
    return jax.shard_map(
        body,
        mesh=mesh,
        in_specs=(
            P(SHOT, None, DEPTH, None),
            P(SHOT, None, DEPTH, None),
            P(SHOT, None, DEPTH, None),
            P(SHOT, None, DEPTH, None),
            P(SHOT, DEPTH, None),
            P(SHOT, DEPTH, None),
            P(SHOT, DEPTH, None),
            P(SHOT, DEPTH, None),
            P(None, DEPTH, None),
            P(SHOT),
            P(SHOT),
            P(SHOT, None),
            P(SHOT, None),
            P(SHOT, None, None),
        ),
        out_specs=(
            P(SHOT, DEPTH, None),
            P(SHOT, DEPTH, None),
            P(SHOT, None, DEPTH, None),
        ),
        check_vma=False,
    )
```

```python
import jax
import jax.numpy as jnp
from jax import lax
from jax.experimental import pallas as pl
from jax.experimental.pallas import tpu as pltpu
from jax.sharding import PartitionSpec as P


second_coef = (-205.0 / 72.0, 8.0 / 5.0, -1.0 / 5.0, 8.0 / 315.0, -1.0 / 560.0)
first_coef = (0.8, -0.2, 4.0 / 105.0, -1.0 / 280.0)

SHOT = ("xh", "z", "core")
DEPTH = ("xl", "y")
PEERS = ("xh", "z")
SWAP = [(0, 1), (1, 0)]
REACH = 4
VMEM_LIMIT = 16 * 2**20
MID = 8
CHUNK = 4
VMEM = pl.BlockSpec(memory_space=pltpu.VMEM)
SMEM = pl.BlockSpec(memory_space=pltpu.SMEM)


def f32(*shape):
    return jax.ShapeDtypeStruct(shape, jnp.float32)


def call(kernel, args, smem, outs, scratch=(), flops=0):
    bytes_accessed = 4 * sum(a.size for a in args)
    return pl.pallas_call(
        kernel,
        out_shape=outs,
        in_specs=[SMEM if i < smem else VMEM for i in range(len(args))],
        out_specs=jax.tree.map(lambda _: VMEM, outs),
        scratch_shapes=list(scratch),
        cost_estimate=pl.CostEstimate(
            flops=flops, bytes_accessed=bytes_accessed, transcendentals=0
        ),
        compiler_params=pltpu.CompilerParams(vmem_limit_bytes=VMEM_LIMIT),
    )(*args)


def fill_padded(pad, read, low, high):
    cells_x, cells_z = pad.shape[0] - 2 * REACH, pad.shape[1] - 2 * MID
    zeros = jnp.zeros((REACH, *pad.shape[1:]), jnp.float32)
    pad[pl.ds(0, REACH)] = zeros
    pad[pl.ds(REACH + cells_x, REACH)] = zeros

    @pl.loop(0, cells_x // CHUNK)
    def _(step):
        x = step * CHUNK
        to = pl.ds(REACH + x, CHUNK)
        pad[to, pl.ds(MID, cells_z), :] = read(x)
        pad[to, pl.ds(MID - REACH, REACH), :] = low(x)
        pad[to, pl.ds(MID + cells_z, REACH), :] = high(x)


def depth_pass(pad, first_z, second_z):
    cells_x, cells_z = second_z.shape[0], second_z.shape[1]
    zeros = jnp.zeros((REACH, *first_z.shape[1:]), jnp.float32)
    first_z[pl.ds(0, REACH)] = zeros
    first_z[pl.ds(REACH + cells_x, REACH)] = zeros

    @pl.loop(0, cells_x // CHUNK)
    def _(step):
        x = step * CHUNK
        at = lambda k: pad[pl.ds(REACH + x, CHUNK), pl.ds(MID + k, cells_z), :]
        two = second_coef[0] * at(0)
        one = None
        for k in range(1, 5):
            above, below = at(k), at(-k)
            two = two + second_coef[k] * (above + below)
            term = first_coef[k - 1] * (above - below)
            one = term if one is None else one + term
        second_z[pl.ds(x, CHUNK)] = two
        first_z[pl.ds(REACH + x, CHUNK)] = one


def lateral_masks(cells_y):
    lane = lax.broadcasted_iota(jnp.int32, (1, 8, cells_y), 2)
    up = [jnp.where(lane < cells_y - k, second_coef[k], 0.0) for k in range(1, 5)]
    down = [jnp.where(lane >= k, second_coef[k], 0.0) for k in range(1, 5)]
    return up, down


def lateral(pad, x, masks, cells_z):
    up, down = masks
    at = lambda k: pad[pl.ds(REACH + x + k, CHUNK), pl.ds(MID, cells_z), :]
    v = at(0)
    cells_y = v.shape[2]
    total = (2.0 * second_coef[0]) * v
    for k in range(1, 5):
        total = total + second_coef[k] * (at(k) + at(-k))
    flat = v.reshape(CHUNK * cells_z // 8, 8, cells_y)
    along_y = None
    for k in range(1, 5):
        term = up[k - 1] * pltpu.roll(flat, cells_y - k, 2) + down[k - 1] * pltpu.roll(flat, k, 2)
        along_y = term if along_y is None else along_y + term
    return total + along_y.reshape(v.shape)


def crossing(first_z, x):
    at = lambda k: first_z[pl.ds(REACH + x + k, CHUNK)]
    total = None
    for k in range(1, 5):
        term = first_coef[k - 1] * (at(k) - at(-k))
        total = term if total is None else total + term
    return total


def add_at(ref, cell, amount, z_start, depth_cells):
    cells_z, cells_y = ref.shape[1], ref.shape[2]
    row = cell // cells_y
    x, z = row // depth_cells, row % depth_cells - z_start

    @pl.when((z >= 0) & (z < cells_z))
    def _():
        lane = lax.broadcasted_iota(jnp.int32, (1, 1, cells_y), 2)
        at = (pl.ds(x, 1), pl.ds(z, 1), slice(None))
        ref[at] = ref[at] + jnp.where(lane == cell % cells_y, amount, 0.0)


def spread_kernel(model, aniso_h, aniso_c, smooth, out):
    for j, ref in enumerate((model, aniso_h, aniso_c, smooth)):
        block = ref[...]
        for peer in range(out.shape[0]):
            out[peer, j] = block


def land_kernel(low, high, low_out, high_out):
    low_out[...] = low[...]
    high_out[...] = high[...]


def open_kernel(
    place, src_cell, src_wave, rec_cell, rec_data, onehot, shot_group,
    u_prev, u_cur, a_prev, a_cur, low, high,
    base_u, lat_u, dep_u, cross_u, base_a, lat_a, dep_a, cross_a, weight,
    pad, first_z,
):
    cells_x, cells_z, cells_y = lat_u.shape
    masks = lateral_masks(cells_y)
    sides = ((u_prev, u_cur, base_u, lat_u, dep_u, cross_u),
             (a_prev, a_cur, base_a, lat_a, dep_a, cross_a))
    for j, (old, now, base, lat, dep, cross) in enumerate(sides):
        fill_padded(
            pad,
            lambda x, now=now: now[0, pl.ds(x, CHUNK)],
            lambda x, j=j: low[j, pl.ds(x, CHUNK)],
            lambda x, j=j: high[j, pl.ds(x, CHUNK)],
        )
        depth_pass(pad, first_z, dep)

        @pl.loop(0, cells_x // CHUNK)
        def _(step, old=old, now=now, base=base, lat=lat, cross=cross):
            x = step * CHUNK
            rows = pl.ds(x, CHUNK)
            lat[rows] = lateral(pad, x, masks, cells_z)
            cross[rows] = crossing(first_z, x)
            base[rows] = 2.0 * now[0, rows] - old[0, rows]

    z_start, depth_cells = place[0], place[1]
    add_at(base_u, src_cell[0], src_wave[0, 0], z_start, depth_cells)

    @pl.loop(0, rec_cell.shape[1])
    def _(r):
        add_at(base_a, rec_cell[0, r], rec_data[0, 0, r], z_start, depth_cells)

    blocks = onehot.shape[1]
    position = lax.broadcasted_iota(jnp.int32, weight.shape, 1)
    value = jnp.zeros(weight.shape, jnp.float32)
    for block in range(blocks):
        scale = sum(
            onehot[shot_group[0], block, b].astype(jnp.float32) * 2.0 ** (-b)
            for b in range(onehot.shape[2])
        )
        value = jnp.where(position // (cells_z // blocks) == block, scale, value)
    weight[...] = value


def first_kernel(
    place, mine, other, a_cur,
    base_u, lat_u, dep_u, cross_u, base_a, lat_a, dep_a, cross_a,
    u_one, a_one, grad, model, aniso_h, aniso_c, smooth, low, high,
):
    cells_x, cells_z, _ = u_one.shape
    own = place[2] == 0

    @pl.loop(0, mine.shape[0])
    def _(q):
        for p in range(2):
            rows = pl.ds(q * 4 + p * 2, 2)
            pick = lambda j: jnp.where(own == (p == 0), mine[q, j], other[q, j])
            m, h, c, s = pick(0), pick(1), pick(2), pick(3)
            model[rows], aniso_h[rows], aniso_c[rows], smooth[rows] = m, h, c, s
            k_u = h * lat_u[rows] + dep_u[rows] + c * cross_u[rows]
            k_a = h * lat_a[rows] + dep_a[rows] + c * cross_a[rows]
            grad[rows] = a_cur[0, rows] * k_u
            new = base_u[rows] + m * k_u
            u_one[rows] = new
            a_one[rows] = base_a[rows] + m * k_a
            low[rows] = new[:, :REACH]
            high[rows] = new[:, cells_z - REACH :]
            edge = (pl.ds(cells_x + q, 1), pl.ds(2 * p, 2), slice(None))
            low[edge] = s[:, 0][None]
            high[edge] = s[:, cells_z - 1][None]


def second_kernel(
    place, src_cell, src_wave,
    u_one, u_cur, a_one, grad, weight, model, aniso_h, aniso_c, low, high,
    u_two, keep, send, pad, first_z, dep,
):
    cells_x, cells_z, cells_y = u_two.shape
    masks = lateral_masks(cells_y)
    fill_padded(
        pad,
        lambda x: u_one[pl.ds(x, CHUNK)],
        lambda x: low[pl.ds(x, CHUNK)],
        lambda x: high[pl.ds(x, CHUNK)],
    )
    depth_pass(pad, first_z, dep)
    own = place[2] == 0

    @pl.loop(0, cells_x // CHUNK)
    def _(step):
        x = step * CHUNK
        rows = pl.ds(x, CHUNK)
        k_u = (
            aniso_h[rows] * lateral(pad, x, masks, cells_z)
            + dep[rows]
            + aniso_c[rows] * crossing(first_z, x)
        )
        u_two[rows] = 2.0 * u_one[rows] - u_cur[0, rows] + model[rows] * k_u
        total = weight[...] * (grad[rows] + a_one[rows] * k_u)
        keep[step] = jnp.where(own, total[:2], total[2:])
        send[step] = jnp.where(own, total[2:], total[:2])

    add_at(u_two, src_cell[0], src_wave[0, 1], place[0], place[1])


def sum_kernel(parts, out):
    total = parts[0]
    for peer in range(1, parts.shape[0]):
        total = total + parts[peer]
    for peer in range(parts.shape[0]):
        out[peer] = total


def join_kernel(place, mine, other, u_two, summed, low, high):
    cells_x, cells_z, _ = summed.shape
    own = place[2] == 0

    @pl.loop(0, mine.shape[0])
    def _(q):
        for p in range(2):
            rows = pl.ds(q * 4 + p * 2, 2)
            g = jnp.where(own == (p == 0), mine[q], other[q])
            summed[rows] = g
            low[rows] = u_two[rows, :REACH]
            high[rows] = u_two[rows, cells_z - REACH :]
            for r in range(2):
                edge = (pl.ds(cells_x + 2 * q + p, 1), pl.ds(2 * r, 2), slice(None))
                low[edge] = g[r, :2][None]
                high[edge] = g[r, cells_z - 2 :][None]


SM = 16


def relax_kernel(summed, smooth, low_g, high_g, low_s, high_s, out, square, wide, once, coef):
    cells_x, cells_z, cells_y = summed.shape
    tall = wide.shape[1]
    zero_row = jnp.zeros((1, tall, cells_y), jnp.float32)
    for ref in (wide, once):
        ref[pl.ds(0, 1)] = zero_row
        ref[pl.ds(cells_x + 1, 1)] = zero_row

    @pl.loop(0, cells_x // CHUNK)
    def _(q):
        for ref, shift in ((wide, 1), (coef, 0)):
            zero = jnp.zeros((CHUNK, 8, cells_y), jnp.float32)
            for tile in (0, 8, SM + cells_z, SM + cells_z + 8):
                ref[pl.ds(q * CHUNK + shift, CHUNK), pl.ds(tile, 8), :] = zero
        for j in range(CHUNK):
            x = q * CHUNK + j
            halo = (pl.ds(cells_x + 2 * q + j // 2, 1), pl.ds(2 * (j % 2), 2), slice(None))
            wide[pl.ds(x + 1, 1), pl.ds(SM, cells_z), :] = summed[pl.ds(x, 1)]
            wide[pl.ds(x + 1, 1), pl.ds(SM - 2, 2), :] = low_g[halo]
            wide[pl.ds(x + 1, 1), pl.ds(SM + cells_z, 2), :] = high_g[halo]
            edge = (pl.ds(cells_x + q, 1), pl.ds(j, 1), slice(None))
            coef[pl.ds(x, 1), pl.ds(SM, cells_z), :] = smooth[pl.ds(x, 1)]
            coef[pl.ds(x, 1), pl.ds(SM - 1, 1), :] = low_s[edge]
            coef[pl.ds(x, 1), pl.ds(SM + cells_z, 1), :] = high_s[edge]

    lane = lax.broadcasted_iota(jnp.int32, (1, 8, cells_y), 2)

    def relaxed(ref, x, start, count, factor):
        at = lambda dx, dz: ref[pl.ds(x + 1 + dx, CHUNK), pl.ds(start + dz, count), :]
        v = at(0, 0)
        near = at(1, 0) + at(-1, 0) + at(0, 1) + at(0, -1)
        flat = v.reshape(CHUNK * count // 8, 8, cells_y)
        right = jnp.where(lane < cells_y - 1, pltpu.roll(flat, cells_y - 1, 2), 0.0)
        left = jnp.where(lane >= 1, pltpu.roll(flat, 1, 2), 0.0)
        near = near + (right + left).reshape(v.shape)
        return v + factor * (near - 6.0 * v)

    @pl.loop(0, cells_x // CHUNK)
    def _(q):
        x = q * CHUNK
        once[pl.ds(x + 1, CHUNK), pl.ds(8, cells_z + 16), :] = relaxed(
            wide, x, 8, cells_z + 16, coef[pl.ds(x, CHUNK), pl.ds(8, cells_z + 16), :]
        )

    def sweep(q, total):
        x = q * CHUNK
        value = relaxed(once, x, SM, cells_z, smooth[pl.ds(x, CHUNK)])
        out[pl.ds(x, CHUNK)] = value
        squares = (value * value).reshape(CHUNK * cells_z // 8, 8, cells_y)
        return total + jnp.sum(squares, axis=0)

    total = lax.fori_loop(0, cells_x // CHUNK, sweep, jnp.zeros((8, cells_y), jnp.float32))
    row = jnp.sum(total, axis=0, keepdims=True)
    square[...] = jnp.broadcast_to(row[None], square.shape)


def third_kernel(
    place, src_cell, src_wave, u_two, u_one, model, aniso_h, aniso_c, low, high,
    base, change, pad, first_z, dep,
):
    cells_x, cells_z, cells_y = base.shape
    masks = lateral_masks(cells_y)
    fill_padded(
        pad,
        lambda x: u_two[pl.ds(x, CHUNK)],
        lambda x: low[pl.ds(x, CHUNK)],
        lambda x: high[pl.ds(x, CHUNK)],
    )
    depth_pass(pad, first_z, dep)

    @pl.loop(0, cells_x // CHUNK)
    def _(step):
        x = step * CHUNK
        rows = pl.ds(x, CHUNK)
        k_u = (
            aniso_h[rows] * lateral(pad, x, masks, cells_z)
            + dep[rows]
            + aniso_c[rows] * crossing(first_z, x)
        )
        base[rows] = 2.0 * u_two[rows] - u_one[rows]
        change[rows] = model[rows] * k_u

    add_at(base, src_cell[0], src_wave[0, 2], place[0], place[1])


def close_kernel(place, squares, smoothed, model, base, change, model_next, grad_dir, wave_next):
    cells_x, cells_z, cells_y = smoothed.shape
    rows = grad_dir.shape[0]
    total = jnp.sum(jnp.sum(squares[...], axis=0), axis=1, keepdims=True)
    cells = (cells_x * place[1] * cells_y).astype(jnp.float32)
    scale = lax.rsqrt(total / cells + 1e-06)
    scale = jnp.broadcast_to(scale, (8, cells_y))[None]

    def factor(value):
        flat = value.reshape(value.shape[0] * cells_z // 8, 8, cells_y) * scale
        return flat.reshape(value.shape)

    @pl.loop(0, cells_x // CHUNK)
    def _(step):
        at = pl.ds(step * CHUNK, CHUNK)
        shrink = 1.0 - 0.25 * jnp.tanh(factor(smoothed[at]))
        wave_next[0, at] = base[at] + change[at] * shrink

    at = pl.ds(place[3], rows)
    direction = factor(smoothed[at])
    grad_dir[...] = direction
    model_next[...] = model[at] * (1.0 - 0.25 * jnp.tanh(direction))


def shift(low_edge, high_edge):
    count = lax.axis_size(DEPTH)
    forward = [(i, i + 1) for i in range(count - 1)]
    backward = [(target, source) for source, target in forward]
    return lax.ppermute(high_edge, DEPTH, forward), lax.ppermute(low_edge, DEPTH, backward)


def body(
    u_prev,
    u_cur,
    a_prev,
    a_cur,
    model,
    aniso_h,
    aniso_c,
    smooth_coef,
    bin_onehot,
    shot_group,
    src_cell,
    rec_cell,
    src_wave,
    rec_data,
):
    _, cells_x, cells_z, cells_y = u_cur.shape
    rows = model.shape[0]
    peers = lax.axis_size(PEERS)
    slab = f32(cells_x, cells_z, cells_y)
    depth_cells = cells_z * lax.axis_size(DEPTH)
    place = jnp.stack(
        [
            lax.axis_index(DEPTH) * cells_z,
            jnp.int32(depth_cells),
            lax.axis_index("core"),
            lax.axis_index(SHOT) * rows,
        ]
    )
    pad = pltpu.VMEM((cells_x + 2 * REACH, cells_z + 2 * MID, cells_y), jnp.float32)
    first_z = pltpu.VMEM((cells_x + 2 * REACH, cells_z, cells_y), jnp.float32)
    dep = pltpu.VMEM((cells_x, cells_z, cells_y), jnp.float32)
    work = 80 * cells_x * cells_z * cells_y

    spread = call(
        spread_kernel,
        (model, aniso_h, aniso_c, smooth_coef),
        0,
        f32(peers, 4, rows, cells_z, cells_y),
    )
    mine = lax.all_to_all(spread, PEERS, 0, 0, tiled=True)

    edges = lambda start: jnp.concatenate(
        [lax.slice_in_dim(v, start, start + REACH, axis=2) for v in (u_cur, a_cur)]
    )
    low, high = shift(edges(0), edges(cells_z - REACH))
    low, high = call(land_kernel, (low, high), 0, (f32(*low.shape), f32(*high.shape)))
    *parts, weight = call(
        open_kernel,
        (place, src_cell, src_wave, rec_cell, rec_data, bin_onehot, shot_group)
        + (u_prev, u_cur, a_prev, a_cur, low, high),
        7,
        (slab,) * 8 + (f32(1, cells_z, cells_y),),
        (pad, first_z),
        2 * work,
    )
    other = lax.ppermute(mine, "core", SWAP)
    payload = f32(cells_x + peers, REACH, cells_y)
    u_one, a_one, grad, model_slab, h_slab, c_slab, smooth_slab, low_edge, high_edge = call(
        first_kernel,
        (place, mine, other, a_cur, *parts),
        1,
        (slab,) * 7 + (payload, payload),
        (),
        20 * slab.size,
    )
    low_one, high_one = shift(low_edge, high_edge)
    split = f32(peers, rows, cells_z, cells_y)
    u_two, keep, send = call(
        second_kernel,
        (place, src_cell, src_wave)
        + (u_one, u_cur, a_one, grad, weight, model_slab, h_slab, c_slab, low_one, high_one),
        3,
        (slab, split, split),
        (pad, first_z, dep),
        work,
    )
    chip_sum = keep + lax.ppermute(send, "core", SWAP)
    shares = lax.all_to_all(chip_sum, PEERS, 0, 0, tiled=True)
    total = call(sum_kernel, (shares,), 0, split)
    mine = lax.all_to_all(total, PEERS, 0, 0, tiled=True)
    other = lax.ppermute(mine, "core", SWAP)
    payload = f32(cells_x + 2 * peers, REACH, cells_y)
    summed, low_edge, high_edge = call(
        join_kernel, (place, mine, other, u_two), 1, (slab, payload, payload)
    )
    low_two, high_two = shift(low_edge, high_edge)
    tall = cells_z + 2 * SM
    smoothed, square = call(
        relax_kernel,
        (summed, smooth_slab, low_two, high_two, low_one, high_one),
        0,
        (slab, f32(lax.axis_size(DEPTH), 1, cells_y)),
        (
            pltpu.VMEM((cells_x + 2, tall, cells_y), jnp.float32),
            pltpu.VMEM((cells_x + 2, tall, cells_y), jnp.float32),
            pltpu.VMEM((cells_x, tall, cells_y), jnp.float32),
        ),
        40 * slab.size,
    )
    squares = lax.all_to_all(square, DEPTH, 0, 0, tiled=True)
    base, change = call(
        third_kernel,
        (place, src_cell, src_wave)
        + (u_two, u_one, model_slab, h_slab, c_slab, low_two, high_two),
        3,
        (slab, slab),
        (pad, first_z, dep),
        work,
    )
    share = f32(rows, cells_z, cells_y)
    return call(
        close_kernel,
        (place, squares, smoothed, model_slab, base, change),
        1,
        (share, share, f32(1, cells_x, cells_z, cells_y)),
        (),
        20 * slab.size,
    )


def solution(mesh):
    mesh = jax.sharding.Mesh(
        mesh.devices.reshape(2, 8, 2, 2, 4), ("xh", "z", "core", "xl", "y")
    )
    return jax.shard_map(
        body,
        mesh=mesh,
        in_specs=(
            P(SHOT, None, DEPTH, None),
            P(SHOT, None, DEPTH, None),
            P(SHOT, None, DEPTH, None),
            P(SHOT, None, DEPTH, None),
            P(SHOT, DEPTH, None),
            P(SHOT, DEPTH, None),
            P(SHOT, DEPTH, None),
            P(SHOT, DEPTH, None),
            P(None, DEPTH, None),
            P(SHOT),
            P(SHOT),
            P(SHOT, None),
            P(SHOT, None),
            P(SHOT, None, None),
        ),
        out_specs=(
            P(SHOT, DEPTH, None),
            P(SHOT, DEPTH, None),
            P(SHOT, None, DEPTH, None),
        ),
        check_vma=False,
    )
```

```python
import jax
import jax.numpy as jnp
from jax import lax
from jax.experimental import pallas as pl
from jax.experimental.pallas import tpu as pltpu
from jax.sharding import PartitionSpec as P


second_coef = (-205.0 / 72.0, 8.0 / 5.0, -1.0 / 5.0, 8.0 / 315.0, -1.0 / 560.0)
first_coef = (0.8, -0.2, 4.0 / 105.0, -1.0 / 280.0)

SHOT = ("xh", "z", "core")
DEPTH = ("xl", "y")
PEERS = ("xh", "z")
SWAP = [(0, 1), (1, 0)]
REACH = 4
MID = 8
CHUNK = 4
VMEM = pl.BlockSpec(memory_space=pltpu.VMEM)
SMEM = pl.BlockSpec(memory_space=pltpu.SMEM)
HBM = pl.BlockSpec(memory_space=pltpu.HBM)


def f32(*shape):
    return jax.ShapeDtypeStruct(shape, jnp.float32)


def call(kernel, args, smem, outs, scratch=(), flops=0, hbm_in=(), hbm_out=(), grant=16):
    bytes_accessed = 4 * sum(a.size for a in args)
    spec = lambda i: SMEM if i < smem else HBM if i in hbm_in else VMEM
    single = not isinstance(outs, tuple)
    out_specs = [HBM if i in hbm_out else VMEM for i in range(1 if single else len(outs))]
    return pl.pallas_call(
        kernel,
        out_shape=outs,
        in_specs=[spec(i) for i in range(len(args))],
        out_specs=out_specs[0] if single else tuple(out_specs),
        scratch_shapes=list(scratch),
        cost_estimate=pl.CostEstimate(
            flops=flops, bytes_accessed=bytes_accessed, transcendentals=0
        ),
        compiler_params=pltpu.CompilerParams(vmem_limit_bytes=grant * 2**20),
    )(*args)


def fill_rows(rows, read):
    cells_x = rows.shape[0] - 2 * REACH
    zeros = jnp.zeros((REACH, *rows.shape[1:]), jnp.float32)
    rows[pl.ds(0, REACH)] = zeros
    rows[pl.ds(REACH + cells_x, REACH)] = zeros

    @pl.loop(0, cells_x // CHUNK)
    def _(step):
        x = step * CHUNK
        rows[pl.ds(REACH + x, CHUNK)] = read(pl.ds(x, CHUNK))


def fill_depth(pad, place, read, low, high):
    cells_x, cells_z = pad.shape[0], pad.shape[1] - 2 * MID
    below = place[0] > 0
    above = place[0] + cells_z < place[1]

    @pl.loop(0, cells_x // CHUNK)
    def _(step):
        at = pl.ds(step * CHUNK, CHUNK)
        pad[at, pl.ds(MID, cells_z), :] = read(at)
        pad[at, pl.ds(MID - REACH, REACH), :] = jnp.where(below, low(at), 0.0)
        pad[at, pl.ds(MID + cells_z, REACH), :] = jnp.where(above, high(at), 0.0)


def depth_pass(pad, first_z, second_z):
    cells_x, cells_z = second_z.shape[0], second_z.shape[1]
    zeros = jnp.zeros((REACH, *first_z.shape[1:]), jnp.float32)
    first_z[pl.ds(0, REACH)] = zeros
    first_z[pl.ds(REACH + cells_x, REACH)] = zeros

    @pl.loop(0, cells_x // CHUNK)
    def _(step):
        x = step * CHUNK
        at = lambda k: pad[pl.ds(x, CHUNK), pl.ds(MID + k, cells_z), :]
        two = second_coef[0] * at(0)
        one = None
        for k in range(1, 5):
            above, below = at(k), at(-k)
            two = two + second_coef[k] * (above + below)
            term = first_coef[k - 1] * (above - below)
            one = term if one is None else one + term
        second_z[pl.ds(x, CHUNK)] = two
        first_z[pl.ds(REACH + x, CHUNK)] = one


def lateral_masks(cells_y):
    lane = lax.broadcasted_iota(jnp.int32, (1, 8, cells_y), 2)
    up = [jnp.where(lane < cells_y - k, second_coef[k], 0.0) for k in range(1, 5)]
    down = [jnp.where(lane >= k, second_coef[k], 0.0) for k in range(1, 5)]
    return up, down


def lateral(rows, x, masks):
    up, down = masks
    at = lambda k: rows[pl.ds(REACH + x + k, CHUNK)]
    v = at(0)
    cells_z, cells_y = v.shape[1:]
    total = (2.0 * second_coef[0]) * v
    for k in range(1, 5):
        total = total + second_coef[k] * (at(k) + at(-k))
    flat = v.reshape(CHUNK * cells_z // 8, 8, cells_y)
    along_y = None
    for k in range(1, 5):
        term = up[k - 1] * pltpu.roll(flat, cells_y - k, 2) + down[k - 1] * pltpu.roll(flat, k, 2)
        along_y = term if along_y is None else along_y + term
    return total + along_y.reshape(v.shape)


def crossing(first_z, x):
    at = lambda k: first_z[pl.ds(REACH + x + k, CHUNK)]
    total = None
    for k in range(1, 5):
        term = first_coef[k - 1] * (at(k) - at(-k))
        total = term if total is None else total + term
    return total


def add_at(ref, cell, amount, z_start, depth_cells):
    cells_z, cells_y = ref.shape[1], ref.shape[2]
    row = cell // cells_y
    x, z = row // depth_cells, row % depth_cells - z_start

    @pl.when((z >= 0) & (z < cells_z))
    def _():
        lane = lax.broadcasted_iota(jnp.int32, (1, 1, cells_y), 2)
        at = (pl.ds(x, 1), pl.ds(z, 1), slice(None))
        ref[at] = ref[at] + jnp.where(lane == cell % cells_y, amount, 0.0)


def spread_kernel(model, aniso_h, aniso_c, smooth, out, own, sem_in, sem_out):
    arrays = (model, aniso_h, aniso_c, smooth)
    loads = [pltpu.make_async_copy(ref, own.at[j], sem_in.at[j]) for j, ref in enumerate(arrays)]
    for load in loads:
        load.start()
    for load in loads:
        load.wait()
    sends = [pltpu.make_async_copy(own, out.at[p], sem_out.at[p]) for p in range(out.shape[0])]
    for send in sends:
        send.start()
    for send in sends:
        send.wait()


def place_receivers(out, rec_cell, rec_data, z_start, depth_cells):
    cells_x, cells_z, cells_y = out.shape
    cell = rec_cell[...]
    row = cell // cells_y
    z = row % depth_cells - z_start
    key = jnp.where((z >= 0) & (z < cells_z), row // depth_cells * cells_z + z, -1)
    y = cell % cells_y
    count = cell.shape[1]
    lanes = jnp.where(
        lax.broadcasted_iota(jnp.int32, (cells_y, count), 0) == y, 1.0, 0.0
    ).astype(jnp.bfloat16)
    rest, terms = rec_data[0, pl.ds(0, 1), :], []
    for _ in range(3):
        term = rest.astype(jnp.bfloat16).astype(jnp.float32)
        terms.append(term)
        rest = rest - term
    block = min(16, cells_x)

    @pl.loop(0, cells_x // block)
    def _(step):
        first = step * block * cells_z
        index = first + lax.broadcasted_iota(jnp.int32, (block * cells_z, count), 0)
        hit = index == key
        total = None
        for term in terms:
            left = jnp.where(hit, term, 0.0).astype(jnp.bfloat16)
            part = lax.dot_general(
                left, lanes, (((1,), (1,)), ((), ())), preferred_element_type=jnp.float32
            )
            total = part if total is None else total + part
        at = pl.ds(step * block, block)
        out[at] = out[at] + total.reshape(block, cells_z, cells_y)


def open_kernel(
    place, src_cell, src_wave, onehot, shot_group, rec_cell, rec_data,
    u_prev, u_cur, a_prev, a_cur, low, high,
    base_u, lat_u, dep_u, cross_u, base_a, lat_a, dep_a, cross_a, weight,
    old, now, base, lat, dep, cross, scale_row, rows, pad, first_z, sem_in, sem_out,
):
    cells_x, cells_z, cells_y = lat_u.shape
    masks = lateral_masks(cells_y)
    loads = []
    for j, (before, current) in enumerate(((u_prev, u_cur), (a_prev, a_cur))):
        loads.append(pltpu.make_async_copy(current.at[0], now.at[j], sem_in.at[j, 0]))
        loads.append(pltpu.make_async_copy(before.at[0], old.at[j], sem_in.at[j, 1]))
    for load in loads:
        load.start()
    sends = []

    def send(source, target):
        copy = pltpu.make_async_copy(source, target, sem_out.at[len(sends)])
        copy.start()
        sends.append(copy)

    blocks = onehot.shape[1]
    position = lax.broadcasted_iota(jnp.int32, weight.shape, 1)
    value = jnp.zeros(weight.shape, jnp.float32)
    for block in range(blocks):
        scale = sum(
            onehot[shot_group[0], block, b].astype(jnp.float32) * 2.0 ** (-b)
            for b in range(onehot.shape[2])
        )
        value = jnp.where(position // (cells_z // blocks) == block, scale, value)
    scale_row[...] = value
    send(scale_row, weight)

    targets = ((base_u, lat_u, dep_u, cross_u), (base_a, lat_a, dep_a, cross_a))
    for j in range(2):
        loads[2 * j].wait()
        loads[2 * j + 1].wait()
        fill_depth(
            pad,
            place,
            lambda at, j=j: now[j, at],
            lambda at, j=j: low[j, at],
            lambda at, j=j: high[j, at],
        )
        depth_pass(pad, first_z, dep.at[j])
        send(dep.at[j], targets[j][2])
        fill_rows(rows, lambda at, j=j: now[j, at])

        @pl.loop(0, cells_x // CHUNK)
        def _(step, j=j):
            x = step * CHUNK
            at = pl.ds(x, CHUNK)
            lat[j, at] = lateral(rows, x, masks)
            cross[j, at] = crossing(first_z, x)
            base[j, at] = 2.0 * now[j, at] - old[j, at]

        send(lat.at[j], targets[j][1])
        send(cross.at[j], targets[j][3])
        if j == 0:
            add_at(base.at[0], src_cell[0], src_wave[0, 0], place[0], place[1])
        else:
            place_receivers(base.at[1], rec_cell, rec_data, place[0], place[1])
        send(base.at[j], targets[j][0])
    for copy in sends:
        copy.wait()


def fetch_kernel(*refs):
    count = (len(refs) - 1) // 2
    sources, targets, sem = refs[:count], refs[count:-1], refs[-1]
    copies = [
        pltpu.make_async_copy(source, target, sem.at[i])
        for i, (source, target) in enumerate(zip(sources, targets))
    ]
    for copy in copies:
        copy.start()
    for copy in copies:
        copy.wait()


def first_kernel(
    place, mine, other, a_cur,
    base_u, lat_u, dep_u, cross_u, base_a, lat_a, dep_a, cross_a,
    u_one, a_one, grad, model, aniso_h, aniso_c, smooth, low, high,
):
    cells_x, cells_z, _ = u_one.shape
    own = place[2] == 0

    @pl.loop(0, mine.shape[0])
    def _(q):
        for p in range(2):
            rows = pl.ds(q * 4 + p * 2, 2)
            pick = lambda j: jnp.where(own == (p == 0), mine[q, j], other[q, j])
            m, h, c, s = pick(0), pick(1), pick(2), pick(3)
            model[rows], aniso_h[rows], aniso_c[rows], smooth[rows] = m, h, c, s
            k_u = h * lat_u[rows] + dep_u[rows] + c * cross_u[rows]
            k_a = h * lat_a[rows] + dep_a[rows] + c * cross_a[rows]
            grad[rows] = a_cur[0, rows] * k_u
            new = base_u[rows] + m * k_u
            u_one[rows] = new
            a_one[rows] = base_a[rows] + m * k_a
            low[rows] = new[:, :REACH]
            high[rows] = new[:, cells_z - REACH :]
            edge = (pl.ds(cells_x + q, 1), pl.ds(2 * p, 2), slice(None))
            low[edge] = s[:, 0][None]
            high[edge] = s[:, cells_z - 1][None]


def side_kernel(now, old, aniso_h, base, side, rows):
    cells_x, _, cells_y = base.shape
    masks = lateral_masks(cells_y)
    fill_rows(rows, lambda at: now[at])

    @pl.loop(0, cells_x // CHUNK)
    def _(step):
        x = step * CHUNK
        at = pl.ds(x, CHUNK)
        base[at] = 2.0 * now[at] - old[at]
        side[at] = aniso_h[at] * lateral(rows, x, masks)


def second_kernel(
    place, src_cell, src_wave,
    u_one, base, side, a_one, grad, weight, model, aniso_c, low, high,
    u_two, keep, send, pad, first_z, dep,
):
    cells_x, _, _ = u_two.shape
    fill_depth(pad, place, lambda at: u_one[at], lambda at: low[at], lambda at: high[at])
    depth_pass(pad, first_z, dep)
    own = place[2] == 0

    @pl.loop(0, cells_x // CHUNK)
    def _(step):
        x = step * CHUNK
        at = pl.ds(x, CHUNK)
        k_u = side[at] + dep[at] + aniso_c[at] * crossing(first_z, x)
        u_two[at] = base[at] + model[at] * k_u
        total = weight[...] * (grad[at] + a_one[at] * k_u)
        keep[step] = jnp.where(own, total[:2], total[2:])
        send[step] = jnp.where(own, total[2:], total[:2])

    add_at(u_two, src_cell[0], src_wave[0, 1], place[0], place[1])


def sum_kernel(parts, out):
    total = parts[0]
    for peer in range(1, parts.shape[0]):
        total = total + parts[peer]
    for peer in range(parts.shape[0]):
        out[peer] = total


def join_kernel(place, mine, other, u_two, summed, low, high):
    cells_x, cells_z, _ = summed.shape
    own = place[2] == 0

    @pl.loop(0, mine.shape[0])
    def _(q):
        for p in range(2):
            rows = pl.ds(q * 4 + p * 2, 2)
            g = jnp.where(own == (p == 0), mine[q], other[q])
            summed[rows] = g
            low[rows] = u_two[rows, :REACH]
            high[rows] = u_two[rows, cells_z - REACH :]
            for r in range(2):
                edge = (pl.ds(cells_x + 2 * q + p, 1), pl.ds(2 * r, 2), slice(None))
                low[edge] = g[r, :2][None]
                high[edge] = g[r, cells_z - 2 :][None]


SM = 16


def relax_kernel(place, summed, smooth, low_g, high_g, low_s, high_s, out, square, wide, once, coef):
    cells_x, cells_z, cells_y = summed.shape
    tall = wide.shape[1]
    below = place[0] > 0
    above = place[0] + cells_z < place[1]
    zero_row = jnp.zeros((1, tall, cells_y), jnp.float32)
    for ref in (wide, once):
        ref[pl.ds(0, 1)] = zero_row
        ref[pl.ds(cells_x + 1, 1)] = zero_row

    @pl.loop(0, cells_x // CHUNK)
    def _(q):
        for ref, shift in ((wide, 1), (coef, 0)):
            zero = jnp.zeros((CHUNK, 8, cells_y), jnp.float32)
            for tile in (0, 8, SM + cells_z, SM + cells_z + 8):
                ref[pl.ds(q * CHUNK + shift, CHUNK), pl.ds(tile, 8), :] = zero
        for j in range(CHUNK):
            x = q * CHUNK + j
            halo = (pl.ds(cells_x + 2 * q + j // 2, 1), pl.ds(2 * (j % 2), 2), slice(None))
            wide[pl.ds(x + 1, 1), pl.ds(SM, cells_z), :] = summed[pl.ds(x, 1)]
            wide[pl.ds(x + 1, 1), pl.ds(SM - 2, 2), :] = jnp.where(below, low_g[halo], 0.0)
            wide[pl.ds(x + 1, 1), pl.ds(SM + cells_z, 2), :] = jnp.where(above, high_g[halo], 0.0)
            edge = (pl.ds(cells_x + q, 1), pl.ds(j, 1), slice(None))
            coef[pl.ds(x, 1), pl.ds(SM, cells_z), :] = smooth[pl.ds(x, 1)]
            coef[pl.ds(x, 1), pl.ds(SM - 1, 1), :] = jnp.where(below, low_s[edge], 0.0)
            coef[pl.ds(x, 1), pl.ds(SM + cells_z, 1), :] = jnp.where(above, high_s[edge], 0.0)

    lane = lax.broadcasted_iota(jnp.int32, (1, 8, cells_y), 2)

    def relaxed(ref, x, start, count, factor):
        at = lambda dx, dz: ref[pl.ds(x + 1 + dx, CHUNK), pl.ds(start + dz, count), :]
        v = at(0, 0)
        near = at(1, 0) + at(-1, 0) + at(0, 1) + at(0, -1)
        flat = v.reshape(CHUNK * count // 8, 8, cells_y)
        right = jnp.where(lane < cells_y - 1, pltpu.roll(flat, cells_y - 1, 2), 0.0)
        left = jnp.where(lane >= 1, pltpu.roll(flat, 1, 2), 0.0)
        near = near + (right + left).reshape(v.shape)
        return v + factor * (near - 6.0 * v)

    @pl.loop(0, cells_x // CHUNK)
    def _(q):
        x = q * CHUNK
        once[pl.ds(x + 1, CHUNK), pl.ds(8, cells_z + 16), :] = relaxed(
            wide, x, 8, cells_z + 16, coef[pl.ds(x, CHUNK), pl.ds(8, cells_z + 16), :]
        )

    def sweep(q, total):
        x = q * CHUNK
        value = relaxed(once, x, SM, cells_z, smooth[pl.ds(x, CHUNK)])
        out[pl.ds(x, CHUNK)] = value
        squares = (value * value).reshape(CHUNK * cells_z // 8, 8, cells_y)
        return total + jnp.sum(squares, axis=0)

    total = lax.fori_loop(0, cells_x // CHUNK, sweep, jnp.zeros((8, cells_y), jnp.float32))
    row = jnp.sum(total, axis=0, keepdims=True)
    square[...] = jnp.broadcast_to(row[None], square.shape)


def third_kernel(
    place, src_cell, src_wave, u_two, base_in, side, model, aniso_c, low, high,
    base, change, pad, first_z, dep,
):
    cells_x = base.shape[0]
    fill_depth(pad, place, lambda at: u_two[at], lambda at: low[at], lambda at: high[at])
    depth_pass(pad, first_z, dep)

    @pl.loop(0, cells_x // CHUNK)
    def _(step):
        x = step * CHUNK
        at = pl.ds(x, CHUNK)
        base[at] = base_in[at]
        change[at] = model[at] * (side[at] + dep[at] + aniso_c[at] * crossing(first_z, x))

    add_at(base, src_cell[0], src_wave[0, 2], place[0], place[1])


def close_kernel(place, squares, smoothed, model, base, change, model_next, grad_dir, wave_next):
    cells_x, cells_z, cells_y = smoothed.shape
    rows = grad_dir.shape[0]
    total = jnp.sum(jnp.sum(squares[...], axis=0), axis=1, keepdims=True)
    cells = (cells_x * place[1] * cells_y).astype(jnp.float32)
    scale = lax.rsqrt(total / cells + 1e-06)
    scale = jnp.broadcast_to(scale, (8, cells_y))[None]

    def factor(value):
        flat = value.reshape(value.shape[0] * cells_z // 8, 8, cells_y) * scale
        return flat.reshape(value.shape)

    @pl.loop(0, cells_x // CHUNK)
    def _(step):
        at = pl.ds(step * CHUNK, CHUNK)
        shrink = 1.0 - 0.25 * jnp.tanh(factor(smoothed[at]))
        wave_next[0, at] = base[at] + change[at] * shrink

    at = pl.ds(place[3], rows)
    direction = factor(smoothed[at])
    grad_dir[...] = direction
    model_next[...] = model[at] * (1.0 - 0.25 * jnp.tanh(direction))


def shift(low_edge, high_edge):
    count = lax.axis_size(DEPTH)
    forward = [(i, (i + 1) % count) for i in range(count)]
    backward = [(target, source) for source, target in forward]
    return lax.ppermute(high_edge, DEPTH, forward), lax.ppermute(low_edge, DEPTH, backward)


def body(
    u_prev,
    u_cur,
    a_prev,
    a_cur,
    model,
    aniso_h,
    aniso_c,
    smooth_coef,
    bin_onehot,
    shot_group,
    src_cell,
    rec_cell,
    src_wave,
    rec_data,
):
    _, cells_x, cells_z, cells_y = u_cur.shape
    rows = model.shape[0]
    peers = lax.axis_size(PEERS)
    slab = f32(cells_x, cells_z, cells_y)
    depth_cells = cells_z * lax.axis_size(DEPTH)
    place = jnp.stack(
        [
            lax.axis_index(DEPTH) * cells_z,
            jnp.int32(depth_cells),
            lax.axis_index("core"),
            lax.axis_index(SHOT) * rows,
        ]
    )
    scratch = lambda *shape: pltpu.VMEM(shape, jnp.float32)
    pad = scratch(cells_x, cells_z + 2 * MID, cells_y)
    first_z = scratch(cells_x + 2 * REACH, cells_z, cells_y)
    padded_rows = first_z
    dep = scratch(cells_x, cells_z, cells_y)
    pair = scratch(2, cells_x, cells_z, cells_y)
    work = 80 * cells_x * cells_z * cells_y

    spread = call(
        spread_kernel,
        (model, aniso_h, aniso_c, smooth_coef),
        0,
        f32(peers, 4, rows, cells_z, cells_y),
        (
            scratch(4, rows, cells_z, cells_y),
            pltpu.SemaphoreType.DMA((4,)),
            pltpu.SemaphoreType.DMA((peers,)),
        ),
        hbm_in=range(4),
        hbm_out=(0,),
        grant=62,
    )
    mine = lax.all_to_all(spread, PEERS, 0, 0, tiled=True)

    edges = lambda start: jnp.concatenate(
        [lax.slice_in_dim(v, start, start + REACH, axis=2) for v in (u_cur, a_cur)]
    )
    low, high = shift(edges(0), edges(cells_z - REACH))
    *parts, weight = call(
        open_kernel,
        (place, src_cell, src_wave, bin_onehot, shot_group, rec_cell, rec_data)
        + (u_prev, u_cur, a_prev, a_cur, low, high),
        5,
        (slab,) * 8 + (f32(1, cells_z, cells_y),),
        (pair,) * 6
        + (scratch(1, cells_z, cells_y), padded_rows, pad, first_z)
        + (pltpu.SemaphoreType.DMA((2, 2)), pltpu.SemaphoreType.DMA((9,))),
        2 * work,
        hbm_in=range(7, 11),
        hbm_out=range(9),
        grant=61,
    )
    other = lax.ppermute(mine, "core", SWAP)
    *parts, weight, adjoint = call(
        fetch_kernel,
        (*parts, weight, a_cur),
        0,
        (slab,) * 8 + (f32(1, cells_z, cells_y), f32(*a_cur.shape)),
        (pltpu.SemaphoreType.DMA((10,)),),
        hbm_in=range(10),
        grant=49,
    )
    payload = f32(cells_x + peers, REACH, cells_y)
    u_one, a_one, grad, model_slab, h_slab, c_slab, smooth_slab, low_edge, high_edge = call(
        first_kernel,
        (place, mine, other, adjoint, *parts),
        1,
        (slab,) * 7 + (payload, payload),
        (),
        20 * slab.size,
    )
    low_one, high_one = shift(low_edge, high_edge)
    base, side = call(
        side_kernel, (u_one, u_cur[0], h_slab), 0, (slab, slab), (padded_rows,), work // 2
    )
    split = f32(peers, rows, cells_z, cells_y)
    u_two, keep, send = call(
        second_kernel,
        (place, src_cell, src_wave)
        + (u_one, base, side, a_one, grad, weight, model_slab, c_slab, low_one, high_one),
        3,
        (slab, split, split),
        (pad, first_z, dep),
        work,
    )
    chip_sum = keep + lax.ppermute(send, "core", SWAP)
    shares = lax.all_to_all(chip_sum, PEERS, 0, 0, tiled=True)
    total = call(sum_kernel, (shares,), 0, split)
    mine = lax.all_to_all(total, PEERS, 0, 0, tiled=True)
    other = lax.ppermute(mine, "core", SWAP)
    payload = f32(cells_x + 2 * peers, REACH, cells_y)
    summed, low_edge, high_edge = call(
        join_kernel, (place, mine, other, u_two), 1, (slab, payload, payload)
    )
    low_two, high_two = shift(low_edge, high_edge)
    base, side = call(
        side_kernel, (u_two, u_one, h_slab), 0, (slab, slab), (padded_rows,), work // 2
    )
    tall = cells_z + 2 * SM
    smoothed, square = call(
        relax_kernel,
        (place, summed, smooth_slab, low_two, high_two, low_one, high_one),
        1,
        (slab, f32(lax.axis_size(DEPTH), 1, cells_y)),
        (
            pltpu.VMEM((cells_x + 2, tall, cells_y), jnp.float32),
            pltpu.VMEM((cells_x + 2, tall, cells_y), jnp.float32),
            pltpu.VMEM((cells_x, tall, cells_y), jnp.float32),
        ),
        40 * slab.size,
    )
    squares = lax.all_to_all(square, DEPTH, 0, 0, tiled=True)
    base, change = call(
        third_kernel,
        (place, src_cell, src_wave)
        + (u_two, base, side, model_slab, c_slab, low_two, high_two),
        3,
        (slab, slab),
        (pad, first_z, dep),
        work,
    )
    share = f32(rows, cells_z, cells_y)
    return call(
        close_kernel,
        (place, squares, smoothed, model_slab, base, change),
        1,
        (share, share, f32(1, cells_x, cells_z, cells_y)),
        (),
        20 * slab.size,
    )


def solution(mesh):
    mesh = jax.sharding.Mesh(
        mesh.devices.reshape(2, 8, 2, 2, 4), ("xh", "z", "core", "xl", "y")
    )
    return jax.shard_map(
        body,
        mesh=mesh,
        in_specs=(
            P(SHOT, None, DEPTH, None),
            P(SHOT, None, DEPTH, None),
            P(SHOT, None, DEPTH, None),
            P(SHOT, None, DEPTH, None),
            P(SHOT, DEPTH, None),
            P(SHOT, DEPTH, None),
            P(SHOT, DEPTH, None),
            P(SHOT, DEPTH, None),
            P(None, DEPTH, None),
            P(SHOT),
            P(SHOT),
            P(SHOT, None),
            P(SHOT, None),
            P(SHOT, None, None),
        ),
        out_specs=(
            P(SHOT, DEPTH, None),
            P(SHOT, DEPTH, None),
            P(SHOT, None, DEPTH, None),
        ),
        check_vma=False,
    )
```

```python
import functools

import jax
import jax.numpy as jnp
from jax import lax
from jax.experimental import pallas as pl
from jax.experimental.pallas import tpu as pltpu
from jax.sharding import PartitionSpec as P


second_coef = (-205.0 / 72.0, 8.0 / 5.0, -1.0 / 5.0, 8.0 / 315.0, -1.0 / 560.0)
first_coef = (0.8, -0.2, 4.0 / 105.0, -1.0 / 280.0)

SHOT = ("xh", "z", "core")
DEPTH = ("xl", "y")
PEERS = ("xh", "z")
SWAP = [(0, 1), (1, 0)]
REACH = 4
MID = 8
CHUNK = 4
VMEM = pl.BlockSpec(memory_space=pltpu.VMEM)
SMEM = pl.BlockSpec(memory_space=pltpu.SMEM)
HBM = pl.BlockSpec(memory_space=pltpu.HBM)


def f32(*shape):
    return jax.ShapeDtypeStruct(shape, jnp.float32)


def call(kernel, args, smem, outs, scratch=(), flops=0, hbm_in=(), hbm_out=(), grant=16):
    bytes_accessed = 4 * sum(a.size for a in args)
    spec = lambda i: SMEM if i < smem else HBM if i in hbm_in else VMEM
    single = not isinstance(outs, tuple)
    out_specs = [HBM if i in hbm_out else VMEM for i in range(1 if single else len(outs))]
    return pl.pallas_call(
        kernel,
        out_shape=outs,
        in_specs=[spec(i) for i in range(len(args))],
        out_specs=out_specs[0] if single else tuple(out_specs),
        scratch_shapes=list(scratch),
        cost_estimate=pl.CostEstimate(
            flops=flops, bytes_accessed=bytes_accessed, transcendentals=0
        ),
        compiler_params=pltpu.CompilerParams(vmem_limit_bytes=grant * 2**20),
    )(*args)


def position():
    layer = lax.axis_index("xl") * lax.axis_size("y") + lax.axis_index("y")
    chip = lax.axis_index("xh") * lax.axis_size("z") + lax.axis_index("z")
    return layer, lax.axis_index("core"), chip


def fill_rows(rows, read):
    cells_x = rows.shape[0] - 2 * REACH
    zeros = jnp.zeros((REACH, *rows.shape[1:]), jnp.float32)
    rows[pl.ds(0, REACH)] = zeros
    rows[pl.ds(REACH + cells_x, REACH)] = zeros

    @pl.loop(0, cells_x // CHUNK)
    def _(step):
        x = step * CHUNK
        rows[pl.ds(REACH + x, CHUNK)] = read(pl.ds(x, CHUNK))


def has_sides():
    layer, _, _ = position()
    return layer > 0, layer < lax.axis_size("xl") * lax.axis_size("y") - 1


def depth_range(cells_z):
    layer, _, _ = position()
    return layer * cells_z, cells_z * lax.axis_size("xl") * lax.axis_size("y")


def fill_depth(pad, read, low, high):
    cells_x, cells_z = pad.shape[0], pad.shape[1] - 2 * MID
    below, above = has_sides()

    @pl.loop(0, cells_x // CHUNK)
    def _(step):
        at = pl.ds(step * CHUNK, CHUNK)
        pad[at, pl.ds(MID, cells_z), :] = read(at)
        pad[at, pl.ds(MID - REACH, REACH), :] = jnp.where(below, low(at), 0.0)
        pad[at, pl.ds(MID + cells_z, REACH), :] = jnp.where(above, high(at), 0.0)


def depth_pass(pad, first_z, second_z):
    cells_x, cells_z = second_z.shape[0], second_z.shape[1]
    zeros = jnp.zeros((REACH, *first_z.shape[1:]), jnp.float32)
    first_z[pl.ds(0, REACH)] = zeros
    first_z[pl.ds(REACH + cells_x, REACH)] = zeros

    @pl.loop(0, cells_x // CHUNK)
    def _(step):
        x = step * CHUNK
        at = lambda k: pad[pl.ds(x, CHUNK), pl.ds(MID + k, cells_z), :]
        two = second_coef[0] * at(0)
        one = None
        for k in range(1, 5):
            above, below = at(k), at(-k)
            two = two + second_coef[k] * (above + below)
            term = first_coef[k - 1] * (above - below)
            one = term if one is None else one + term
        second_z[pl.ds(x, CHUNK)] = two
        first_z[pl.ds(REACH + x, CHUNK)] = one


def lateral_masks(cells_y):
    lane = lax.broadcasted_iota(jnp.int32, (1, 8, cells_y), 2)
    up = [jnp.where(lane < cells_y - k, second_coef[k], 0.0) for k in range(1, 5)]
    down = [jnp.where(lane >= k, second_coef[k], 0.0) for k in range(1, 5)]
    return up, down


def lateral(rows, x, masks):
    up, down = masks
    at = lambda k: rows[pl.ds(REACH + x + k, CHUNK)]
    v = at(0)
    cells_z, cells_y = v.shape[1:]
    total = (2.0 * second_coef[0]) * v
    for k in range(1, 5):
        total = total + second_coef[k] * (at(k) + at(-k))
    flat = v.reshape(CHUNK * cells_z // 8, 8, cells_y)
    along_y = None
    for k in range(1, 5):
        term = up[k - 1] * pltpu.roll(flat, cells_y - k, 2) + down[k - 1] * pltpu.roll(flat, k, 2)
        along_y = term if along_y is None else along_y + term
    return total + along_y.reshape(v.shape)


def crossing(first_z, x):
    at = lambda k: first_z[pl.ds(REACH + x + k, CHUNK)]
    total = None
    for k in range(1, 5):
        term = first_coef[k - 1] * (at(k) - at(-k))
        total = term if total is None else total + term
    return total


def add_at(ref, cell, amount):
    cells_z, cells_y = ref.shape[1], ref.shape[2]
    z_start, depth_cells = depth_range(cells_z)
    row = cell // cells_y
    x, z = row // depth_cells, row % depth_cells - z_start

    @pl.when((z >= 0) & (z < cells_z))
    def _():
        lane = lax.broadcasted_iota(jnp.int32, (1, 1, cells_y), 2)
        at = (pl.ds(x, 1), pl.ds(z, 1), slice(None))
        ref[at] = ref[at] + jnp.where(lane == cell % cells_y, amount, 0.0)


def spread_kernel(model, aniso_h, aniso_c, smooth, out, own, sem_in, sem_out):
    arrays = (model, aniso_h, aniso_c, smooth)
    loads = [pltpu.make_async_copy(ref, own.at[j], sem_in.at[j]) for j, ref in enumerate(arrays)]
    for load in loads:
        load.start()
    for load in loads:
        load.wait()
    sends = [pltpu.make_async_copy(own, out.at[p], sem_out.at[p]) for p in range(out.shape[0])]
    for send in sends:
        send.start()
    for send in sends:
        send.wait()


def place_receivers(out, rec_cell, rec_data):
    cells_x, cells_z, cells_y = out.shape
    z_start, depth_cells = depth_range(cells_z)
    cell = rec_cell[...]
    row = cell // cells_y
    z = row % depth_cells - z_start
    key = jnp.where((z >= 0) & (z < cells_z), row // depth_cells * cells_z + z, -1)
    y = cell % cells_y
    count = cell.shape[1]
    lanes = jnp.where(
        lax.broadcasted_iota(jnp.int32, (cells_y, count), 0) == y, 1.0, 0.0
    ).astype(jnp.bfloat16)
    rest, terms = rec_data[0, pl.ds(0, 1), :], []
    for _ in range(3):
        term = rest.astype(jnp.bfloat16).astype(jnp.float32)
        terms.append(term)
        rest = rest - term
    block = min(16, cells_x)

    @pl.loop(0, cells_x // block)
    def _(step):
        first = step * block * cells_z
        index = first + lax.broadcasted_iota(jnp.int32, (block * cells_z, count), 0)
        hit = index == key
        total = None
        for term in terms:
            left = jnp.where(hit, term, 0.0).astype(jnp.bfloat16)
            part = lax.dot_general(
                left, lanes, (((1,), (1,)), ((), ())), preferred_element_type=jnp.float32
            )
            total = part if total is None else total + part
        at = pl.ds(step * block, block)
        out[at] = out[at] + total.reshape(block, cells_z, cells_y)


def open_kernel(
    src_cell, src_wave, onehot, shot_group, rec_cell, rec_data,
    u_prev, u_cur, a_prev, a_cur, low, high,
    base_u, lat_u, dep_u, cross_u, base_a, lat_a, dep_a, cross_a, weight,
    old, now, base, lat, dep, cross, scale_row, rows, pad, first_z, sem_in, sem_out,
):
    cells_x, cells_z, cells_y = lat_u.shape
    masks = lateral_masks(cells_y)
    loads = []
    for j, (before, current) in enumerate(((u_prev, u_cur), (a_prev, a_cur))):
        loads.append(pltpu.make_async_copy(current.at[0], now.at[j], sem_in.at[j, 0]))
        loads.append(pltpu.make_async_copy(before.at[0], old.at[j], sem_in.at[j, 1]))
    for load in loads:
        load.start()
    sends = []

    def send(source, target):
        copy = pltpu.make_async_copy(source, target, sem_out.at[len(sends)])
        copy.start()
        sends.append(copy)

    blocks = onehot.shape[1]
    depth = lax.broadcasted_iota(jnp.int32, weight.shape, 1)
    value = jnp.zeros(weight.shape, jnp.float32)
    for block in range(blocks):
        scale = sum(
            onehot[shot_group[0], block, b].astype(jnp.float32) * 2.0 ** (-b)
            for b in range(onehot.shape[2])
        )
        value = jnp.where(depth // (cells_z // blocks) == block, scale, value)
    scale_row[...] = value
    send(scale_row, weight)

    targets = ((base_u, lat_u, dep_u, cross_u), (base_a, lat_a, dep_a, cross_a))
    for j in range(2):
        loads[2 * j].wait()
        loads[2 * j + 1].wait()
        fill_depth(
            pad,
            lambda at, j=j: now[j, at],
            lambda at, j=j: low[j, at],
            lambda at, j=j: high[j, at],
        )
        depth_pass(pad, first_z, dep.at[j])
        send(dep.at[j], targets[j][2])
        fill_rows(rows, lambda at, j=j: now[j, at])

        @pl.loop(0, cells_x // CHUNK)
        def _(step, j=j):
            x = step * CHUNK
            at = pl.ds(x, CHUNK)
            lat[j, at] = lateral(rows, x, masks)
            cross[j, at] = crossing(first_z, x)
            base[j, at] = 2.0 * now[j, at] - old[j, at]

        send(lat.at[j], targets[j][1])
        send(cross.at[j], targets[j][3])
        if j == 0:
            add_at(base.at[0], src_cell[0], src_wave[0, 0])
        else:
            place_receivers(base.at[1], rec_cell, rec_data)
        send(base.at[j], targets[j][0])
    for copy in sends:
        copy.wait()


def fetch_kernel(*refs):
    count = (len(refs) - 1) // 2
    sources, targets, sem = refs[:count], refs[count:-1], refs[-1]
    copies = [
        pltpu.make_async_copy(source, target, sem.at[i])
        for i, (source, target) in enumerate(zip(sources, targets))
    ]
    for copy in copies:
        copy.start()
    for copy in copies:
        copy.wait()


def first_kernel(
    mine, other, a_cur,
    base_u, lat_u, dep_u, cross_u, base_a, lat_a, dep_a, cross_a,
    u_one, a_one, grad, model, aniso_h, aniso_c, smooth, low, high,
):
    cells_x, cells_z, _ = u_one.shape
    own = position()[1] == 0

    @pl.loop(0, mine.shape[0])
    def _(q):
        for p in range(2):
            rows = pl.ds(q * 4 + p * 2, 2)
            pick = lambda j: jnp.where(own == (p == 0), mine[q, j], other[q, j])
            m, h, c, s = pick(0), pick(1), pick(2), pick(3)
            model[rows], aniso_h[rows], aniso_c[rows], smooth[rows] = m, h, c, s
            k_u = h * lat_u[rows] + dep_u[rows] + c * cross_u[rows]
            k_a = h * lat_a[rows] + dep_a[rows] + c * cross_a[rows]
            grad[rows] = a_cur[0, rows] * k_u
            new = base_u[rows] + m * k_u
            u_one[rows] = new
            a_one[rows] = base_a[rows] + m * k_a
            low[rows] = new[:, :REACH]
            high[rows] = new[:, cells_z - REACH :]
            edge = (pl.ds(cells_x + q, 1), pl.ds(2 * p, 2), slice(None))
            low[edge] = s[:, 0][None]
            high[edge] = s[:, cells_z - 1][None]


def side_kernel(step_index, src_cell, src_wave, now, old, aniso_h, base, side, rows):
    cells_x, _, cells_y = base.shape
    masks = lateral_masks(cells_y)
    fill_rows(rows, lambda at: now[at])

    @pl.loop(0, cells_x // CHUNK)
    def _(step):
        x = step * CHUNK
        at = pl.ds(x, CHUNK)
        base[at] = 2.0 * now[at] - old[at]
        side[at] = aniso_h[at] * lateral(rows, x, masks)

    add_at(base, src_cell[0], src_wave[0, step_index])


def second_kernel(
    u_one, base, side, a_one, grad, weight, model, aniso_c, low, high,
    u_two, keep, send, pad, first_z, dep,
):
    cells_x = u_two.shape[0]
    fill_depth(pad, lambda at: u_one[at], lambda at: low[at], lambda at: high[at])
    depth_pass(pad, first_z, dep)
    own = position()[1] == 0

    @pl.loop(0, cells_x // CHUNK)
    def _(step):
        x = step * CHUNK
        at = pl.ds(x, CHUNK)
        k_u = side[at] + dep[at] + aniso_c[at] * crossing(first_z, x)
        u_two[at] = base[at] + model[at] * k_u
        total = weight[...] * (grad[at] + a_one[at] * k_u)
        keep[step] = jnp.where(own, total[:2], total[2:])
        send[step] = jnp.where(own, total[2:], total[:2])


def sum_kernel(parts, out):
    total = parts[0]
    for peer in range(1, parts.shape[0]):
        total = total + parts[peer]
    for peer in range(parts.shape[0]):
        out[peer] = total


def join_kernel(mine, other, u_two, summed, low, high):
    cells_x, cells_z, _ = summed.shape
    count = mine.shape[0]
    own = position()[1] == 0

    @pl.loop(0, count)
    def _(q):
        for p in range(2):
            rows = pl.ds(q * 4 + p * 2, 2)
            g = jnp.where(own == (p == 0), mine[q], other[q])
            summed[rows] = g
            low[rows] = u_two[rows, :REACH]
            high[rows] = u_two[rows, cells_z - REACH :]
            for k in range(2):
                edge = (pl.ds(cells_x + k * count + q, 1), pl.ds(2 * p, 2), slice(None))
                low[edge] = g[:, k][None]
                high[edge] = g[:, cells_z - 1 - k][None]


def shifted_y(flat):
    cells_y = flat.shape[-1]
    lane = lax.broadcasted_iota(jnp.int32, (1,) * (flat.ndim - 2) + (8, cells_y), flat.ndim - 1)
    axis = flat.ndim - 1
    if flat.ndim == 2:
        lane = lax.broadcasted_iota(jnp.int32, flat.shape, 1)
    right = jnp.where(lane < cells_y - 1, pltpu.roll(flat, cells_y - 1, axis), 0.0)
    left = jnp.where(lane >= 1, pltpu.roll(flat, 1, axis), 0.0)
    return right + left


def relax_kernel(summed, smooth, out, inner, own_g, own_s, own_out, wide, once):
    cells_x, cells_z, cells_y = summed.shape
    for ref in (wide, once):
        blank = jnp.zeros((1, *ref.shape[1:]), jnp.float32)
        ref[pl.ds(0, 1)] = blank
        ref[pl.ds(cells_x + 1, 1)] = blank

    @pl.loop(0, cells_x // CHUNK)
    def _(q):
        at = pl.ds(q * CHUNK + 1, CHUNK)
        blank = jnp.zeros((CHUNK, 1, cells_y), jnp.float32)
        for ref in (wide, once):
            ref[at, pl.ds(MID - 1, 1), :] = blank
            ref[at, pl.ds(MID + cells_z, 1), :] = blank
        wide[at, pl.ds(MID, cells_z), :] = summed[pl.ds(q * CHUNK, CHUNK)]

    def relaxed(ref, x, factor):
        at = lambda dx, dz: ref[pl.ds(x + 1 + dx, CHUNK), pl.ds(MID + dz, cells_z), :]
        v = at(0, 0)
        near = at(1, 0) + at(-1, 0) + at(0, 1) + at(0, -1)
        flat = v.reshape(CHUNK * cells_z // 8, 8, cells_y)
        near = near + shifted_y(flat).reshape(v.shape)
        return v + factor * (near - 6.0 * v)

    @pl.loop(0, cells_x // CHUNK)
    def _(q):
        x = q * CHUNK
        factor = smooth[pl.ds(x, CHUNK)]
        once[pl.ds(x + 1, CHUNK), pl.ds(MID, cells_z), :] = relaxed(wide, x, factor)
        g = summed[pl.ds(x, CHUNK)]
        for i, k in enumerate((0, cells_z - 1)):
            own_g[i, pl.ds(x, CHUNK)] = g[:, k]
        for i, k in enumerate((0, 1, cells_z - 2, cells_z - 1)):
            own_s[i, pl.ds(x, CHUNK)] = factor[:, k]

    depth = lax.broadcasted_iota(jnp.int32, (1, cells_z, cells_y), 1)
    between = (depth >= 2) & (depth < cells_z - 2)

    def sweep(q, total):
        x = q * CHUNK
        value = relaxed(once, x, smooth[pl.ds(x, CHUNK)])
        out[pl.ds(x, CHUNK)] = value
        for i, k in enumerate((0, 1, cells_z - 2, cells_z - 1)):
            own_out[i, pl.ds(x, CHUNK)] = value[:, k]
        squares = jnp.where(between, value * value, 0.0)
        return total + jnp.sum(squares.reshape(CHUNK * cells_z // 8, 8, cells_y), axis=0)

    inner[...] = lax.fori_loop(
        0, cells_x // CHUNK, sweep, jnp.zeros((8, cells_y), jnp.float32)
    )


def edge_kernel(
    smoothed_in, inner, own_g, own_s, own_out, low_two, high_two, low_one, high_one,
    smoothed, square, planes,
):
    cells_x, cells_z, cells_y = smoothed.shape
    smoothed[...] = smoothed_in[...]
    count = cells_x // 4
    blank = jnp.zeros((8, cells_y), jnp.float32)
    total = inner[...]
    for side, (sums, smooth, present) in enumerate(
        ((low_two, low_one, has_sides()[0]), (high_two, high_one, has_sides()[1]))
    ):
        for k in range(4):
            planes[k, pl.ds(0, 8)] = blank
            planes[k, pl.ds(8 + cells_x, 8)] = blank

        @pl.loop(0, count)
        def _(q, sums=sums, smooth=smooth, present=present):
            at = pl.ds(8 + 4 * q, 4)
            for k in range(2):
                planes[k, at] = jnp.where(present, sums[cells_x + k * count + q], 0.0)
            planes[2, at] = jnp.where(present, smooth[cells_x + q], 0.0)

        def near(k):
            at = lambda dx: planes[k, pl.ds(8 + dx, cells_x)]
            return at(1) + at(-1) + shifted_y(at(0))

        whole = pl.ds(8, cells_x)
        first, second, factor = planes[0, whole], planes[1, whole], planes[2, whole]
        outside = first + factor * (near(0) + second + own_g[side] - 6.0 * first)
        edge, inside = (0, 1) if side == 0 else (3, 2)
        change = own_s[edge] * first
        planes[3, whole] = change
        value = own_out[edge] + change + own_s[edge] * (near(3) - 6.0 * change + outside)
        beside = own_out[inside] + own_s[inside] * change
        squares = value * value + beside * beside
        total = total + jnp.sum(squares.reshape(cells_x // 8, 8, cells_y), axis=0)
        planes[0, whole] = value
        planes[1, whole] = beside
        rows = (0, 1) if side == 0 else (cells_z - 1, cells_z - 2)

        @pl.loop(0, count)
        def _(q, rows=rows):
            for k, z in enumerate(rows):
                smoothed[pl.ds(4 * q, 4), pl.ds(z, 1), :] = planes[k, pl.ds(8 + 4 * q, 4)][:, None]

    row = jnp.sum(total, axis=0, keepdims=True)
    square[...] = jnp.broadcast_to(row[None], square.shape)


def third_kernel(u_two, side, model, aniso_c, low, high, change, pad, first_z, dep):
    cells_x = change.shape[0]
    fill_depth(pad, lambda at: u_two[at], lambda at: low[at], lambda at: high[at])
    depth_pass(pad, first_z, dep)

    @pl.loop(0, cells_x // CHUNK)
    def _(step):
        x = step * CHUNK
        at = pl.ds(x, CHUNK)
        change[at] = model[at] * (side[at] + dep[at] + aniso_c[at] * crossing(first_z, x))


def close_kernel(squares, smoothed, model, base, change, model_next, grad_dir, wave_next):
    cells_x, cells_z, cells_y = smoothed.shape
    rows = grad_dir.shape[0]
    total = jnp.sum(jnp.sum(squares[...], axis=0), axis=1, keepdims=True)
    cells = cells_x * depth_range(cells_z)[1] * cells_y
    scale = lax.rsqrt(total / cells + 1e-06)
    scale = jnp.broadcast_to(scale, (8, cells_y))[None]

    def factor(value):
        flat = value.reshape(value.shape[0] * cells_z // 8, 8, cells_y) * scale
        return flat.reshape(value.shape)

    @pl.loop(0, cells_x // CHUNK)
    def _(step):
        at = pl.ds(step * CHUNK, CHUNK)
        shrink = 1.0 - 0.25 * jnp.tanh(factor(smoothed[at]))
        wave_next[0, at] = base[at] + change[at] * shrink

    _, core, chip = position()
    at = pl.ds((2 * chip + core) * rows, rows)
    direction = factor(smoothed[at])
    grad_dir[...] = direction
    model_next[...] = model[at] * (1.0 - 0.25 * jnp.tanh(direction))


def shift(low_edge, high_edge):
    count = lax.axis_size(DEPTH)
    forward = [(i, (i + 1) % count) for i in range(count)]
    backward = [(target, source) for source, target in forward]
    return lax.ppermute(high_edge, DEPTH, forward), lax.ppermute(low_edge, DEPTH, backward)


def body(
    u_prev,
    u_cur,
    a_prev,
    a_cur,
    model,
    aniso_h,
    aniso_c,
    smooth_coef,
    bin_onehot,
    shot_group,
    src_cell,
    rec_cell,
    src_wave,
    rec_data,
):
    _, cells_x, cells_z, cells_y = u_cur.shape
    rows = model.shape[0]
    peers = lax.axis_size(PEERS)
    slab = f32(cells_x, cells_z, cells_y)
    scratch = lambda *shape: pltpu.VMEM(shape, jnp.float32)
    pad = scratch(cells_x, cells_z + 2 * MID, cells_y)
    first_z = scratch(cells_x + 2 * REACH, cells_z, cells_y)
    padded_rows = first_z
    dep = scratch(cells_x, cells_z, cells_y)
    pair = scratch(2, cells_x, cells_z, cells_y)
    work = 80 * cells_x * cells_z * cells_y

    spread = call(
        spread_kernel,
        (model, aniso_h, aniso_c, smooth_coef),
        0,
        f32(peers, 4, rows, cells_z, cells_y),
        (
            scratch(4, rows, cells_z, cells_y),
            pltpu.SemaphoreType.DMA((4,)),
            pltpu.SemaphoreType.DMA((peers,)),
        ),
        hbm_in=range(4),
        hbm_out=(0,),
        grant=62,
    )
    mine = lax.all_to_all(spread, PEERS, 0, 0, tiled=True)

    edges = lambda start: jnp.concatenate(
        [lax.slice_in_dim(v, start, start + REACH, axis=2) for v in (u_cur, a_cur)]
    )
    low, high = shift(edges(0), edges(cells_z - REACH))
    *parts, weight = call(
        open_kernel,
        (src_cell, src_wave, bin_onehot, shot_group, rec_cell, rec_data)
        + (u_prev, u_cur, a_prev, a_cur, low, high),
        4,
        (slab,) * 8 + (f32(1, cells_z, cells_y),),
        (pair,) * 6
        + (scratch(1, cells_z, cells_y), padded_rows, pad, first_z)
        + (pltpu.SemaphoreType.DMA((2, 2)), pltpu.SemaphoreType.DMA((9,))),
        2 * work,
        hbm_in=range(6, 10),
        hbm_out=range(9),
        grant=61,
    )
    other = lax.ppermute(mine, "core", SWAP)
    *parts, weight, adjoint = call(
        fetch_kernel,
        (*parts, weight, a_cur),
        0,
        (slab,) * 8 + (f32(1, cells_z, cells_y), f32(*a_cur.shape)),
        (pltpu.SemaphoreType.DMA((10,)),),
        hbm_in=range(10),
        grant=49,
    )
    payload = f32(cells_x + peers, REACH, cells_y)
    u_one, a_one, grad, model_slab, h_slab, c_slab, smooth_slab, low_edge, high_edge = call(
        first_kernel,
        (mine, other, adjoint, *parts),
        0,
        (slab,) * 7 + (payload, payload),
        (),
        20 * slab.size,
    )
    low_one, high_one = shift(low_edge, high_edge)
    base, side = call(
        functools.partial(side_kernel, 1),
        (src_cell, src_wave, u_one, u_cur[0], h_slab),
        2,
        (slab, slab),
        (padded_rows,),
        work // 2,
    )
    split = f32(peers, rows, cells_z, cells_y)
    u_two, keep, send = call(
        second_kernel,
        (u_one, base, side, a_one, grad, weight, model_slab, c_slab, low_one, high_one),
        0,
        (slab, split, split),
        (pad, first_z, dep),
        work,
    )
    chip_sum = keep + lax.ppermute(send, "core", SWAP)
    shares = lax.all_to_all(chip_sum, PEERS, 0, 0, tiled=True)
    total = call(sum_kernel, (shares,), 0, split)
    mine = lax.all_to_all(total, PEERS, 0, 0, tiled=True)
    other = lax.ppermute(mine, "core", SWAP)
    payload = f32(cells_x + 2 * peers, REACH, cells_y)
    summed, low_edge, high_edge = call(
        join_kernel, (mine, other, u_two), 0, (slab, payload, payload)
    )
    low_two, high_two = shift(low_edge, high_edge)
    base, side = call(
        functools.partial(side_kernel, 2),
        (src_cell, src_wave, u_two, u_one, h_slab),
        2,
        (slab, slab),
        (padded_rows,),
        work // 2,
    )
    edges = f32(4, cells_x, cells_y)
    smoothed, inner, own_g, own_s, own_out = call(
        relax_kernel,
        (summed, smooth_slab),
        0,
        (slab, f32(8, cells_y), f32(2, cells_x, cells_y), edges, edges),
        (scratch(cells_x + 2, cells_z + 2 * MID, cells_y),) * 2,
        40 * slab.size,
    )
    change = call(
        third_kernel,
        (u_two, side, model_slab, c_slab, low_two, high_two),
        0,
        slab,
        (pad, first_z, dep),
        work,
    )
    smoothed, square = call(
        edge_kernel,
        (smoothed, inner, own_g, own_s, own_out, low_two, high_two, low_one, high_one),
        0,
        (slab, f32(lax.axis_size(DEPTH), 1, cells_y)),
        (scratch(4, cells_x + 16, cells_y),),
        4 * slab.size,
    )
    squares = lax.all_to_all(square, DEPTH, 0, 0, tiled=True)
    share = f32(rows, cells_z, cells_y)
    return call(
        close_kernel,
        (squares, smoothed, model_slab, base, change),
        0,
        (share, share, f32(1, cells_x, cells_z, cells_y)),
        (),
        20 * slab.size,
    )


def solution(mesh):
    mesh = jax.sharding.Mesh(
        mesh.devices.reshape(2, 8, 2, 2, 4), ("xh", "z", "core", "xl", "y")
    )
    return jax.shard_map(
        body,
        mesh=mesh,
        in_specs=(
            P(SHOT, None, DEPTH, None),
            P(SHOT, None, DEPTH, None),
            P(SHOT, None, DEPTH, None),
            P(SHOT, None, DEPTH, None),
            P(SHOT, DEPTH, None),
            P(SHOT, DEPTH, None),
            P(SHOT, DEPTH, None),
            P(SHOT, DEPTH, None),
            P(None, DEPTH, None),
            P(SHOT),
            P(SHOT),
            P(SHOT, None),
            P(SHOT, None),
            P(SHOT, None, None),
        ),
        out_specs=(
            P(SHOT, DEPTH, None),
            P(SHOT, DEPTH, None),
            P(SHOT, None, DEPTH, None),
        ),
        check_vma=False,
    )
```

```python
import functools

import jax
import jax.numpy as jnp
from jax import lax
from jax.experimental import pallas as pl
from jax.experimental.pallas import tpu as pltpu
from jax.sharding import PartitionSpec as P


second_coef = (-205.0 / 72.0, 8.0 / 5.0, -1.0 / 5.0, 8.0 / 315.0, -1.0 / 560.0)
first_coef = (0.8, -0.2, 4.0 / 105.0, -1.0 / 280.0)

SHOT = ("xh", "z", "core")
DEPTH = ("xl", "y")
PEERS = ("xh", "z")
SWAP = [(0, 1), (1, 0)]
REACH = 4
MID = 8
CHUNK = 4
UNROLL = 4
VMEM = pl.BlockSpec(memory_space=pltpu.VMEM)
SMEM = pl.BlockSpec(memory_space=pltpu.SMEM)
HBM = pl.BlockSpec(memory_space=pltpu.HBM)


def f32(*shape):
    return jax.ShapeDtypeStruct(shape, jnp.float32)


def call(kernel, args, smem, outs, scratch=(), flops=0, hbm_in=(), hbm_out=(), grant=16):
    bytes_accessed = 4 * sum(a.size for a in args)
    spec = lambda i: SMEM if i < smem else HBM if i in hbm_in else VMEM
    single = not isinstance(outs, tuple)
    out_specs = [HBM if i in hbm_out else VMEM for i in range(1 if single else len(outs))]
    return pl.pallas_call(
        kernel,
        out_shape=outs,
        in_specs=[spec(i) for i in range(len(args))],
        out_specs=out_specs[0] if single else tuple(out_specs),
        scratch_shapes=list(scratch),
        cost_estimate=pl.CostEstimate(
            flops=flops, bytes_accessed=bytes_accessed, transcendentals=0
        ),
        compiler_params=pltpu.CompilerParams(vmem_limit_bytes=grant * 2**20),
    )(*args)


def position():
    layer = lax.axis_index("xl") * lax.axis_size("y") + lax.axis_index("y")
    chip = lax.axis_index("xh") * lax.axis_size("z") + lax.axis_index("z")
    return layer, lax.axis_index("core"), chip


def fill_rows(rows, read):
    cells_x = rows.shape[0] - 2 * REACH
    zeros = jnp.zeros((REACH, *rows.shape[1:]), jnp.float32)
    rows[pl.ds(0, REACH)] = zeros
    rows[pl.ds(REACH + cells_x, REACH)] = zeros

    @pl.loop(0, cells_x // CHUNK)
    def _(step):
        x = step * CHUNK
        rows[pl.ds(REACH + x, CHUNK)] = read(pl.ds(x, CHUNK))


def has_sides():
    layer, _, _ = position()
    return layer > 0, layer < lax.axis_size("xl") * lax.axis_size("y") - 1


def depth_range(cells_z):
    layer, _, _ = position()
    return layer * cells_z, cells_z * lax.axis_size("xl") * lax.axis_size("y")


def fill_depth(pad, read, low, high):
    cells_x, cells_z = pad.shape[0], pad.shape[1] - 2 * MID
    below, above = has_sides()

    @pl.loop(0, cells_x // CHUNK)
    def _(step):
        at = pl.ds(step * CHUNK, CHUNK)
        pad[at, pl.ds(MID, cells_z), :] = read(at)
        pad[at, pl.ds(MID - REACH, REACH), :] = jnp.where(below, low(at), 0.0)
        pad[at, pl.ds(MID + cells_z, REACH), :] = jnp.where(above, high(at), 0.0)


def depth_pass(pad, first_z, second_z):
    cells_x, cells_z = second_z.shape[0], second_z.shape[1]
    zeros = jnp.zeros((REACH, *first_z.shape[1:]), jnp.float32)
    first_z[pl.ds(0, REACH)] = zeros
    first_z[pl.ds(REACH + cells_x, REACH)] = zeros

    @pl.loop(0, cells_x // CHUNK)
    def _(step):
        x = step * CHUNK
        at = lambda k: pad[pl.ds(x, CHUNK), pl.ds(MID + k, cells_z), :]
        two = second_coef[0] * at(0)
        one = None
        for k in range(1, 5):
            above, below = at(k), at(-k)
            two = two + second_coef[k] * (above + below)
            term = first_coef[k - 1] * (above - below)
            one = term if one is None else one + term
        second_z[pl.ds(x, CHUNK)] = two
        first_z[pl.ds(REACH + x, CHUNK)] = one


def lateral_masks(cells_y):
    lane = lax.broadcasted_iota(jnp.int32, (1, 8, cells_y), 2)
    up = [jnp.where(lane < cells_y - k, second_coef[k], 0.0) for k in range(1, 5)]
    down = [jnp.where(lane >= k, second_coef[k], 0.0) for k in range(1, 5)]
    return up, down


def lateral(rows, x, masks):
    up, down = masks
    at = lambda k: rows[pl.ds(REACH + x + k, CHUNK)]
    v = at(0)
    cells_z, cells_y = v.shape[1:]
    total = (2.0 * second_coef[0]) * v
    for k in range(1, 5):
        total = total + second_coef[k] * (at(k) + at(-k))
    flat = v.reshape(CHUNK * cells_z // 8, 8, cells_y)
    along_y = None
    for k in range(1, 5):
        term = up[k - 1] * pltpu.roll(flat, cells_y - k, 2) + down[k - 1] * pltpu.roll(flat, k, 2)
        along_y = term if along_y is None else along_y + term
    return total + along_y.reshape(v.shape)


def crossing(first_z, x):
    at = lambda k: first_z[pl.ds(REACH + x + k, CHUNK)]
    total = None
    for k in range(1, 5):
        term = first_coef[k - 1] * (at(k) - at(-k))
        total = term if total is None else total + term
    return total


def add_at(ref, cell, amount):
    cells_z, cells_y = ref.shape[1], ref.shape[2]
    z_start, depth_cells = depth_range(cells_z)
    row = cell // cells_y
    x, z = row // depth_cells, row % depth_cells - z_start

    @pl.when((z >= 0) & (z < cells_z))
    def _():
        lane = lax.broadcasted_iota(jnp.int32, (1, 1, cells_y), 2)
        at = (pl.ds(x, 1), pl.ds(z, 1), slice(None))
        ref[at] = ref[at] + jnp.where(lane == cell % cells_y, amount, 0.0)


def spread_kernel(model, aniso_h, aniso_c, smooth, out, own, sem_in, sem_out):
    arrays = (model, aniso_h, aniso_c, smooth)
    loads = [pltpu.make_async_copy(ref, own.at[j], sem_in.at[j]) for j, ref in enumerate(arrays)]
    for load in loads:
        load.start()
    for load in loads:
        load.wait()
    sends = [pltpu.make_async_copy(own, out.at[p], sem_out.at[p]) for p in range(out.shape[0])]
    for send in sends:
        send.start()
    for send in sends:
        send.wait()


def place_receivers(out, rec_cell, rec_data):
    cells_x, cells_z, cells_y = out.shape
    z_start, depth_cells = depth_range(cells_z)
    cell = rec_cell[...]
    row = cell // cells_y
    z = row % depth_cells - z_start
    key = jnp.where((z >= 0) & (z < cells_z), row // depth_cells * cells_z + z, -1)
    y = cell % cells_y
    count = cell.shape[1]
    lanes = jnp.where(
        lax.broadcasted_iota(jnp.int32, (cells_y, count), 0) == y, 1.0, 0.0
    ).astype(jnp.bfloat16)
    rest, terms = rec_data[0, pl.ds(0, 1), :], []
    for _ in range(3):
        term = rest.astype(jnp.bfloat16).astype(jnp.float32)
        terms.append(term)
        rest = rest - term
    block = min(16, cells_x)

    @pl.loop(0, cells_x // block)
    def _(step):
        first = step * block * cells_z
        index = first + lax.broadcasted_iota(jnp.int32, (block * cells_z, count), 0)
        hit = index == key
        total = None
        for term in terms:
            left = jnp.where(hit, term, 0.0).astype(jnp.bfloat16)
            part = lax.dot_general(
                left, lanes, (((1,), (1,)), ((), ())), preferred_element_type=jnp.float32
            )
            total = part if total is None else total + part
        at = pl.ds(step * block, block)
        out[at] = out[at] + total.reshape(block, cells_z, cells_y)


def open_kernel(
    src_cell, src_wave, onehot, shot_group, rec_cell, rec_data,
    u_prev, u_cur, a_prev, a_cur, low, high,
    base_u, lat_u, dep_u, cross_u, base_a, lat_a, dep_a, cross_a, weight,
    old, now, base, lat, dep, cross, scale_row, rows, pad, first_z, sem_in, sem_out,
):
    cells_x, cells_z, cells_y = lat_u.shape
    masks = lateral_masks(cells_y)
    loads = []
    for j, (before, current) in enumerate(((u_prev, u_cur), (a_prev, a_cur))):
        loads.append(pltpu.make_async_copy(current.at[0], now.at[j], sem_in.at[j, 0]))
        loads.append(pltpu.make_async_copy(before.at[0], old.at[j], sem_in.at[j, 1]))
    for load in loads:
        load.start()
    sends = []

    def send(source, target):
        copy = pltpu.make_async_copy(source, target, sem_out.at[len(sends)])
        copy.start()
        sends.append(copy)

    blocks = onehot.shape[1]
    depth = lax.broadcasted_iota(jnp.int32, weight.shape, 1)
    value = jnp.zeros(weight.shape, jnp.float32)
    for block in range(blocks):
        scale = sum(
            onehot[shot_group[0], block, b].astype(jnp.float32) * 2.0 ** (-b)
            for b in range(onehot.shape[2])
        )
        value = jnp.where(depth // (cells_z // blocks) == block, scale, value)
    scale_row[...] = value
    send(scale_row, weight)

    targets = ((base_u, lat_u, dep_u, cross_u), (base_a, lat_a, dep_a, cross_a))
    for j in range(2):
        loads[2 * j].wait()
        loads[2 * j + 1].wait()
        fill_depth(
            pad,
            lambda at, j=j: now[j, at],
            lambda at, j=j: low[j, at],
            lambda at, j=j: high[j, at],
        )
        depth_pass(pad, first_z, dep.at[j])
        send(dep.at[j], targets[j][2])
        fill_rows(rows, lambda at, j=j: now[j, at])

        @pl.loop(0, cells_x // CHUNK)
        def _(step, j=j):
            x = step * CHUNK
            at = pl.ds(x, CHUNK)
            lat[j, at] = lateral(rows, x, masks)
            cross[j, at] = crossing(first_z, x)
            base[j, at] = 2.0 * now[j, at] - old[j, at]

        send(lat.at[j], targets[j][1])
        send(cross.at[j], targets[j][3])
        if j == 0:
            add_at(base.at[0], src_cell[0], src_wave[0, 0])
        else:
            place_receivers(base.at[1], rec_cell, rec_data)
        send(base.at[j], targets[j][0])
    for copy in sends:
        copy.wait()


def fetch_kernel(*refs):
    count = (len(refs) - 1) // 2
    sources, targets, sem = refs[:count], refs[count:-1], refs[-1]
    copies = [
        pltpu.make_async_copy(source, target, sem.at[i])
        for i, (source, target) in enumerate(zip(sources, targets))
    ]
    for copy in copies:
        copy.start()
    for copy in copies:
        copy.wait()


def first_kernel(
    mine, other, a_cur,
    base_u, lat_u, dep_u, cross_u, base_a, lat_a, dep_a, cross_a,
    u_one, a_one, grad, model, aniso_h, aniso_c, smooth, low, high,
):
    cells_x, cells_z, _ = u_one.shape
    own = position()[1] == 0

    @pl.loop(0, mine.shape[0])
    def _(q):
        for p in range(2):
            rows = pl.ds(q * 4 + p * 2, 2)
            pick = lambda j: jnp.where(own == (p == 0), mine[q, j], other[q, j])
            m, h, c, s = pick(0), pick(1), pick(2), pick(3)
            model[rows], aniso_h[rows], aniso_c[rows], smooth[rows] = m, h, c, s
            k_u = h * lat_u[rows] + dep_u[rows] + c * cross_u[rows]
            k_a = h * lat_a[rows] + dep_a[rows] + c * cross_a[rows]
            grad[rows] = a_cur[0, rows] * k_u
            new = base_u[rows] + m * k_u
            u_one[rows] = new
            a_one[rows] = base_a[rows] + m * k_a
            low[rows] = new[:, :REACH]
            high[rows] = new[:, cells_z - REACH :]
            edge = (pl.ds(cells_x + q, 1), pl.ds(2 * p, 2), slice(None))
            low[edge] = s[:, 0][None]
            high[edge] = s[:, cells_z - 1][None]


def side_kernel(step_index, src_cell, src_wave, now, old, aniso_h, base, side, rows):
    cells_x, _, cells_y = base.shape
    masks = lateral_masks(cells_y)
    fill_rows(rows, lambda at: now[at])

    @pl.loop(0, cells_x // CHUNK, unroll=UNROLL)
    def _(step):
        x = step * CHUNK
        at = pl.ds(x, CHUNK)
        base[at] = 2.0 * now[at] - old[at]
        side[at] = aniso_h[at] * lateral(rows, x, masks)

    add_at(base, src_cell[0], src_wave[0, step_index])


def second_kernel(
    u_one, base, side, a_one, grad, weight, model, aniso_c, low, high,
    u_two, keep, send, pad, first_z, dep,
):
    cells_x = u_two.shape[0]
    fill_depth(pad, lambda at: u_one[at], lambda at: low[at], lambda at: high[at])
    depth_pass(pad, first_z, dep)
    own = position()[1] == 0

    @pl.loop(0, cells_x // CHUNK)
    def _(step):
        x = step * CHUNK
        at = pl.ds(x, CHUNK)
        k_u = side[at] + dep[at] + aniso_c[at] * crossing(first_z, x)
        u_two[at] = base[at] + model[at] * k_u
        total = weight[...] * (grad[at] + a_one[at] * k_u)
        keep[step] = jnp.where(own, total[:2], total[2:])
        send[step] = jnp.where(own, total[2:], total[:2])


def sum_kernel(parts, out):
    total = parts[0]
    for peer in range(1, parts.shape[0]):
        total = total + parts[peer]
    for peer in range(parts.shape[0]):
        out[peer] = total


def join_kernel(mine, other, u_two, summed, low, high):
    cells_x, cells_z, _ = summed.shape
    count = mine.shape[0]
    own = position()[1] == 0

    @pl.loop(0, count)
    def _(q):
        for p in range(2):
            rows = pl.ds(q * 4 + p * 2, 2)
            g = jnp.where(own == (p == 0), mine[q], other[q])
            summed[rows] = g
            low[rows] = u_two[rows, :REACH]
            high[rows] = u_two[rows, cells_z - REACH :]
            for k in range(2):
                edge = (pl.ds(cells_x + k * count + q, 1), pl.ds(2 * p, 2), slice(None))
                low[edge] = g[:, k][None]
                high[edge] = g[:, cells_z - 1 - k][None]


def shifted_y(flat):
    cells_y = flat.shape[-1]
    lane = lax.broadcasted_iota(jnp.int32, (1,) * (flat.ndim - 2) + (8, cells_y), flat.ndim - 1)
    axis = flat.ndim - 1
    if flat.ndim == 2:
        lane = lax.broadcasted_iota(jnp.int32, flat.shape, 1)
    right = jnp.where(lane < cells_y - 1, pltpu.roll(flat, cells_y - 1, axis), 0.0)
    left = jnp.where(lane >= 1, pltpu.roll(flat, 1, axis), 0.0)
    return right + left


def relax_kernel(summed, smooth, out, inner, own_g, own_s, own_out, wide, once):
    cells_x, cells_z, cells_y = summed.shape
    for ref in (wide, once):
        blank = jnp.zeros((1, *ref.shape[1:]), jnp.float32)
        ref[pl.ds(0, 1)] = blank
        ref[pl.ds(cells_x + 1, 1)] = blank

    @pl.loop(0, cells_x // CHUNK, unroll=2)
    def _(q):
        at = pl.ds(q * CHUNK + 1, CHUNK)
        blank = jnp.zeros((CHUNK, 1, cells_y), jnp.float32)
        for ref in (wide, once):
            ref[at, pl.ds(MID - 1, 1), :] = blank
            ref[at, pl.ds(MID + cells_z, 1), :] = blank
        wide[at, pl.ds(MID, cells_z), :] = summed[pl.ds(q * CHUNK, CHUNK)]

    def relaxed(ref, x, factor):
        at = lambda dx, dz: ref[pl.ds(x + 1 + dx, CHUNK), pl.ds(MID + dz, cells_z), :]
        v = at(0, 0)
        near = at(1, 0) + at(-1, 0) + at(0, 1) + at(0, -1)
        flat = v.reshape(CHUNK * cells_z // 8, 8, cells_y)
        near = near + shifted_y(flat).reshape(v.shape)
        return v + factor * (near - 6.0 * v)

    @pl.loop(0, cells_x // CHUNK, unroll=2)
    def _(q):
        x = q * CHUNK
        factor = smooth[pl.ds(x, CHUNK)]
        once[pl.ds(x + 1, CHUNK), pl.ds(MID, cells_z), :] = relaxed(wide, x, factor)
        g = summed[pl.ds(x, CHUNK)]
        for i, k in enumerate((0, cells_z - 1)):
            own_g[i, pl.ds(x, CHUNK)] = g[:, k]
        for i, k in enumerate((0, 1, cells_z - 2, cells_z - 1)):
            own_s[i, pl.ds(x, CHUNK)] = factor[:, k]

    depth = lax.broadcasted_iota(jnp.int32, (1, cells_z, cells_y), 1)
    between = (depth >= 2) & (depth < cells_z - 2)

    def sweep(q, total):
        x = q * CHUNK
        value = relaxed(once, x, smooth[pl.ds(x, CHUNK)])
        out[pl.ds(x, CHUNK)] = value
        for i, k in enumerate((0, 1, cells_z - 2, cells_z - 1)):
            own_out[i, pl.ds(x, CHUNK)] = value[:, k]
        squares = jnp.where(between, value * value, 0.0)
        return total + jnp.sum(squares.reshape(CHUNK * cells_z // 8, 8, cells_y), axis=0)

    inner[...] = lax.fori_loop(
        0, cells_x // CHUNK, sweep, jnp.zeros((8, cells_y), jnp.float32), unroll=2
    )


def edge_kernel(
    smoothed_in, inner, own_g, own_s, own_out, low_two, high_two, low_one, high_one,
    smoothed, square, planes,
):
    cells_x, cells_z, cells_y = smoothed.shape
    smoothed[...] = smoothed_in[...]
    count = cells_x // 4
    blank = jnp.zeros((8, cells_y), jnp.float32)
    total = inner[...]
    for side, (sums, smooth, present) in enumerate(
        ((low_two, low_one, has_sides()[0]), (high_two, high_one, has_sides()[1]))
    ):
        for k in range(4):
            planes[k, pl.ds(0, 8)] = blank
            planes[k, pl.ds(8 + cells_x, 8)] = blank

        @pl.loop(0, count)
        def _(q, sums=sums, smooth=smooth, present=present):
            at = pl.ds(8 + 4 * q, 4)
            for k in range(2):
                planes[k, at] = jnp.where(present, sums[cells_x + k * count + q], 0.0)
            planes[2, at] = jnp.where(present, smooth[cells_x + q], 0.0)

        def near(k):
            at = lambda dx: planes[k, pl.ds(8 + dx, cells_x)]
            return at(1) + at(-1) + shifted_y(at(0))

        whole = pl.ds(8, cells_x)
        first, second, factor = planes[0, whole], planes[1, whole], planes[2, whole]
        outside = first + factor * (near(0) + second + own_g[side] - 6.0 * first)
        edge, inside = (0, 1) if side == 0 else (3, 2)
        change = own_s[edge] * first
        planes[3, whole] = change
        value = own_out[edge] + change + own_s[edge] * (near(3) - 6.0 * change + outside)
        beside = own_out[inside] + own_s[inside] * change
        squares = value * value + beside * beside
        total = total + jnp.sum(squares.reshape(cells_x // 8, 8, cells_y), axis=0)
        planes[0, whole] = value
        planes[1, whole] = beside
        rows = (0, 1) if side == 0 else (cells_z - 1, cells_z - 2)

        @pl.loop(0, count)
        def _(q, rows=rows):
            for k, z in enumerate(rows):
                smoothed[pl.ds(4 * q, 4), pl.ds(z, 1), :] = planes[k, pl.ds(8 + 4 * q, 4)][:, None]

    row = jnp.sum(total, axis=0, keepdims=True)
    square[...] = jnp.broadcast_to(row[None], square.shape)


def third_kernel(u_two, side, model, aniso_c, low, high, change, pad, first_z, dep):
    cells_x = change.shape[0]
    fill_depth(pad, lambda at: u_two[at], lambda at: low[at], lambda at: high[at])
    depth_pass(pad, first_z, dep)

    @pl.loop(0, cells_x // CHUNK)
    def _(step):
        x = step * CHUNK
        at = pl.ds(x, CHUNK)
        change[at] = model[at] * (side[at] + dep[at] + aniso_c[at] * crossing(first_z, x))


def close_kernel(squares, smoothed, model, base, change, model_next, grad_dir, wave_next):
    cells_x, cells_z, cells_y = smoothed.shape
    rows = grad_dir.shape[0]
    total = jnp.sum(jnp.sum(squares[...], axis=0), axis=1, keepdims=True)
    cells = cells_x * depth_range(cells_z)[1] * cells_y
    scale = lax.rsqrt(total / cells + 1e-06)
    scale = jnp.broadcast_to(scale, (8, cells_y))[None]

    def factor(value):
        flat = value.reshape(value.shape[0] * cells_z // 8, 8, cells_y) * scale
        return flat.reshape(value.shape)

    @pl.loop(0, cells_x // CHUNK)
    def _(step):
        at = pl.ds(step * CHUNK, CHUNK)
        shrink = 1.0 - 0.25 * jnp.tanh(factor(smoothed[at]))
        wave_next[0, at] = base[at] + change[at] * shrink

    _, core, chip = position()
    at = pl.ds((2 * chip + core) * rows, rows)
    direction = factor(smoothed[at])
    grad_dir[...] = direction
    model_next[...] = model[at] * (1.0 - 0.25 * jnp.tanh(direction))


def shift(low_edge, high_edge):
    count = lax.axis_size(DEPTH)
    forward = [(i, (i + 1) % count) for i in range(count)]
    backward = [(target, source) for source, target in forward]
    return lax.ppermute(high_edge, DEPTH, forward), lax.ppermute(low_edge, DEPTH, backward)


def body(
    u_prev,
    u_cur,
    a_prev,
    a_cur,
    model,
    aniso_h,
    aniso_c,
    smooth_coef,
    bin_onehot,
    shot_group,
    src_cell,
    rec_cell,
    src_wave,
    rec_data,
):
    _, cells_x, cells_z, cells_y = u_cur.shape
    rows = model.shape[0]
    peers = lax.axis_size(PEERS)
    slab = f32(cells_x, cells_z, cells_y)
    scratch = lambda *shape: pltpu.VMEM(shape, jnp.float32)
    pad = scratch(cells_x, cells_z + 2 * MID, cells_y)
    first_z = scratch(cells_x + 2 * REACH, cells_z, cells_y)
    padded_rows = first_z
    dep = scratch(cells_x, cells_z, cells_y)
    pair = scratch(2, cells_x, cells_z, cells_y)
    work = 80 * cells_x * cells_z * cells_y

    spread = call(
        spread_kernel,
        (model, aniso_h, aniso_c, smooth_coef),
        0,
        f32(peers, 4, rows, cells_z, cells_y),
        (
            scratch(4, rows, cells_z, cells_y),
            pltpu.SemaphoreType.DMA((4,)),
            pltpu.SemaphoreType.DMA((peers,)),
        ),
        hbm_in=range(4),
        hbm_out=(0,),
        grant=62,
    )
    mine = lax.all_to_all(spread, PEERS, 0, 0, tiled=True)

    edges = lambda start: jnp.concatenate(
        [lax.slice_in_dim(v, start, start + REACH, axis=2) for v in (u_cur, a_cur)]
    )
    low, high = shift(edges(0), edges(cells_z - REACH))
    *parts, weight = call(
        open_kernel,
        (src_cell, src_wave, bin_onehot, shot_group, rec_cell, rec_data)
        + (u_prev, u_cur, a_prev, a_cur, low, high),
        4,
        (slab,) * 8 + (f32(1, cells_z, cells_y),),
        (pair,) * 6
        + (scratch(1, cells_z, cells_y), padded_rows, pad, first_z)
        + (pltpu.SemaphoreType.DMA((2, 2)), pltpu.SemaphoreType.DMA((9,))),
        2 * work,
        hbm_in=range(6, 10),
        hbm_out=range(9),
        grant=61,
    )
    other = lax.ppermute(mine, "core", SWAP)
    *parts, weight, adjoint = call(
        fetch_kernel,
        (*parts, weight, a_cur),
        0,
        (slab,) * 8 + (f32(1, cells_z, cells_y), f32(*a_cur.shape)),
        (pltpu.SemaphoreType.DMA((10,)),),
        hbm_in=range(10),
        grant=49,
    )
    payload = f32(cells_x + peers, REACH, cells_y)
    u_one, a_one, grad, model_slab, h_slab, c_slab, smooth_slab, low_edge, high_edge = call(
        first_kernel,
        (mine, other, adjoint, *parts),
        0,
        (slab,) * 7 + (payload, payload),
        (),
        20 * slab.size,
    )
    low_one, high_one = shift(low_edge, high_edge)
    base, side = call(
        functools.partial(side_kernel, 1),
        (src_cell, src_wave, u_one, u_cur[0], h_slab),
        2,
        (slab, slab),
        (padded_rows,),
        work // 2,
    )
    split = f32(peers, rows, cells_z, cells_y)
    u_two, keep, send = call(
        second_kernel,
        (u_one, base, side, a_one, grad, weight, model_slab, c_slab, low_one, high_one),
        0,
        (slab, split, split),
        (pad, first_z, dep),
        work,
    )
    chip_sum = keep + lax.ppermute(send, "core", SWAP)
    shares = lax.all_to_all(chip_sum, PEERS, 0, 0, tiled=True)
    total = call(sum_kernel, (shares,), 0, split)
    mine = lax.all_to_all(total, PEERS, 0, 0, tiled=True)
    other = lax.ppermute(mine, "core", SWAP)
    payload = f32(cells_x + 2 * peers, REACH, cells_y)
    summed, low_edge, high_edge = call(
        join_kernel, (mine, other, u_two), 0, (slab, payload, payload)
    )
    low_two, high_two = shift(low_edge, high_edge)
    base, side = call(
        functools.partial(side_kernel, 2),
        (src_cell, src_wave, u_two, u_one, h_slab),
        2,
        (slab, slab),
        (padded_rows,),
        work // 2,
    )
    edges = f32(4, cells_x, cells_y)
    smoothed, inner, own_g, own_s, own_out = call(
        relax_kernel,
        (summed, smooth_slab),
        0,
        (slab, f32(8, cells_y), f32(2, cells_x, cells_y), edges, edges),
        (scratch(cells_x + 2, cells_z + 2 * MID, cells_y),) * 2,
        40 * slab.size,
    )
    change = call(
        third_kernel,
        (u_two, side, model_slab, c_slab, low_two, high_two),
        0,
        slab,
        (pad, first_z, dep),
        work,
    )
    smoothed, square = call(
        edge_kernel,
        (smoothed, inner, own_g, own_s, own_out, low_two, high_two, low_one, high_one),
        0,
        (slab, f32(lax.axis_size(DEPTH), 1, cells_y)),
        (scratch(4, cells_x + 16, cells_y),),
        4 * slab.size,
    )
    squares = lax.all_to_all(square, DEPTH, 0, 0, tiled=True)
    share = f32(rows, cells_z, cells_y)
    return call(
        close_kernel,
        (squares, smoothed, model_slab, base, change),
        0,
        (share, share, f32(1, cells_x, cells_z, cells_y)),
        (),
        20 * slab.size,
    )


def solution(mesh):
    mesh = jax.sharding.Mesh(
        mesh.devices.reshape(2, 8, 2, 2, 4), ("xh", "z", "core", "xl", "y")
    )
    return jax.shard_map(
        body,
        mesh=mesh,
        in_specs=(
            P(SHOT, None, DEPTH, None),
            P(SHOT, None, DEPTH, None),
            P(SHOT, None, DEPTH, None),
            P(SHOT, None, DEPTH, None),
            P(SHOT, DEPTH, None),
            P(SHOT, DEPTH, None),
            P(SHOT, DEPTH, None),
            P(SHOT, DEPTH, None),
            P(None, DEPTH, None),
            P(SHOT),
            P(SHOT),
            P(SHOT, None),
            P(SHOT, None),
            P(SHOT, None, None),
        ),
        out_specs=(
            P(SHOT, DEPTH, None),
            P(SHOT, DEPTH, None),
            P(SHOT, None, DEPTH, None),
        ),
        check_vma=False,
    )
```

```python
import functools

import jax
import jax.numpy as jnp
from jax import lax
from jax.experimental import pallas as pl
from jax.experimental.pallas import tpu as pltpu
from jax.sharding import PartitionSpec as P


second_coef = (-205.0 / 72.0, 8.0 / 5.0, -1.0 / 5.0, 8.0 / 315.0, -1.0 / 560.0)
first_coef = (0.8, -0.2, 4.0 / 105.0, -1.0 / 280.0)

SHOT = ("xh", "z", "core")
DEPTH = ("xl", "y")
PEERS = ("xh", "z")
SWAP = [(0, 1), (1, 0)]
REACH = 4
MID = 8
CHUNK = 4
UNROLL = 4
VMEM = pl.BlockSpec(memory_space=pltpu.VMEM)
SMEM = pl.BlockSpec(memory_space=pltpu.SMEM)
HBM = pl.BlockSpec(memory_space=pltpu.HBM)


def f32(*shape):
    return jax.ShapeDtypeStruct(shape, jnp.float32)


def call(kernel, args, smem, outs, scratch=(), flops=0, hbm_in=(), hbm_out=(), grant=16):
    bytes_accessed = 4 * sum(a.size for a in args)
    spec = lambda i: SMEM if i < smem else HBM if i in hbm_in else VMEM
    single = not isinstance(outs, tuple)
    out_specs = [HBM if i in hbm_out else VMEM for i in range(1 if single else len(outs))]
    return pl.pallas_call(
        kernel,
        out_shape=outs,
        in_specs=[spec(i) for i in range(len(args))],
        out_specs=out_specs[0] if single else tuple(out_specs),
        scratch_shapes=list(scratch),
        cost_estimate=pl.CostEstimate(
            flops=flops, bytes_accessed=bytes_accessed, transcendentals=0
        ),
        compiler_params=pltpu.CompilerParams(vmem_limit_bytes=grant * 2**20),
    )(*args)


def position():
    layer = lax.axis_index("xl") * lax.axis_size("y") + lax.axis_index("y")
    chip = lax.axis_index("xh") * lax.axis_size("z") + lax.axis_index("z")
    return layer, lax.axis_index("core"), chip


def fill_rows(rows, read):
    cells_x = rows.shape[0] - 2 * REACH
    zeros = jnp.zeros((REACH, *rows.shape[1:]), jnp.float32)
    rows[pl.ds(0, REACH)] = zeros
    rows[pl.ds(REACH + cells_x, REACH)] = zeros

    @pl.loop(0, cells_x // CHUNK)
    def _(step):
        x = step * CHUNK
        rows[pl.ds(REACH + x, CHUNK)] = read(pl.ds(x, CHUNK))


def has_sides():
    layer, _, _ = position()
    return layer > 0, layer < lax.axis_size("xl") * lax.axis_size("y") - 1


def depth_range(cells_z):
    layer, _, _ = position()
    return layer * cells_z, cells_z * lax.axis_size("xl") * lax.axis_size("y")


def fill_depth(pad, read, low, high):
    cells_x, cells_z = pad.shape[0], pad.shape[1] - 2 * MID
    below, above = has_sides()

    @pl.loop(0, cells_x // CHUNK, unroll=2)
    def _(step):
        at = pl.ds(step * CHUNK, CHUNK)
        pad[at, pl.ds(MID, cells_z), :] = read(at)
        pad[at, pl.ds(MID - REACH, REACH), :] = jnp.where(below, low(at), 0.0)
        pad[at, pl.ds(MID + cells_z, REACH), :] = jnp.where(above, high(at), 0.0)


def depth_pass(pad, first_z, second_z):
    cells_x, cells_z = second_z.shape[0], second_z.shape[1]
    zeros = jnp.zeros((REACH, *first_z.shape[1:]), jnp.float32)
    first_z[pl.ds(0, REACH)] = zeros
    first_z[pl.ds(REACH + cells_x, REACH)] = zeros

    @pl.loop(0, cells_x // CHUNK, unroll=2)
    def _(step):
        x = step * CHUNK
        at = lambda k: pad[pl.ds(x, CHUNK), pl.ds(MID + k, cells_z), :]
        two = second_coef[0] * at(0)
        one = None
        for k in range(1, 5):
            above, below = at(k), at(-k)
            two = two + second_coef[k] * (above + below)
            term = first_coef[k - 1] * (above - below)
            one = term if one is None else one + term
        second_z[pl.ds(x, CHUNK)] = two
        first_z[pl.ds(REACH + x, CHUNK)] = one


def lateral_masks(cells_y):
    lane = lax.broadcasted_iota(jnp.int32, (1, 8, cells_y), 2)
    up = [jnp.where(lane < cells_y - k, second_coef[k], 0.0) for k in range(1, 5)]
    down = [jnp.where(lane >= k, second_coef[k], 0.0) for k in range(1, 5)]
    return up, down


def lateral(rows, x, masks):
    up, down = masks
    at = lambda k: rows[pl.ds(REACH + x + k, CHUNK)]
    v = at(0)
    cells_z, cells_y = v.shape[1:]
    total = (2.0 * second_coef[0]) * v
    for k in range(1, 5):
        total = total + second_coef[k] * (at(k) + at(-k))
    flat = v.reshape(CHUNK * cells_z // 8, 8, cells_y)
    along_y = None
    for k in range(1, 5):
        term = up[k - 1] * pltpu.roll(flat, cells_y - k, 2) + down[k - 1] * pltpu.roll(flat, k, 2)
        along_y = term if along_y is None else along_y + term
    return total + along_y.reshape(v.shape)


def crossing(first_z, x):
    at = lambda k: first_z[pl.ds(REACH + x + k, CHUNK)]
    total = None
    for k in range(1, 5):
        term = first_coef[k - 1] * (at(k) - at(-k))
        total = term if total is None else total + term
    return total


def add_at(ref, cell, amount):
    cells_z, cells_y = ref.shape[1], ref.shape[2]
    z_start, depth_cells = depth_range(cells_z)
    row = cell // cells_y
    x, z = row // depth_cells, row % depth_cells - z_start

    @pl.when((z >= 0) & (z < cells_z))
    def _():
        lane = lax.broadcasted_iota(jnp.int32, (1, 1, cells_y), 2)
        at = (pl.ds(x, 1), pl.ds(z, 1), slice(None))
        ref[at] = ref[at] + jnp.where(lane == cell % cells_y, amount, 0.0)


def spread_kernel(model, aniso_h, aniso_c, smooth, out, own, sem_in, sem_out):
    arrays = (model, aniso_h, aniso_c, smooth)
    loads = [pltpu.make_async_copy(ref, own.at[j], sem_in.at[j]) for j, ref in enumerate(arrays)]
    for load in loads:
        load.start()
    for load in loads:
        load.wait()
    sends = [pltpu.make_async_copy(own, out.at[p], sem_out.at[p]) for p in range(out.shape[0])]
    for send in sends:
        send.start()
    for send in sends:
        send.wait()


def place_receivers(out, rec_cell, rec_data):
    cells_x, cells_z, cells_y = out.shape
    z_start, depth_cells = depth_range(cells_z)
    cell = rec_cell[...]
    row = cell // cells_y
    z = row % depth_cells - z_start
    key = jnp.where((z >= 0) & (z < cells_z), row // depth_cells * cells_z + z, -1)
    y = cell % cells_y
    count = cell.shape[1]
    lanes = jnp.where(
        lax.broadcasted_iota(jnp.int32, (cells_y, count), 0) == y, 1.0, 0.0
    ).astype(jnp.bfloat16)
    rest, terms = rec_data[0, pl.ds(0, 1), :], []
    for _ in range(3):
        term = rest.astype(jnp.bfloat16).astype(jnp.float32)
        terms.append(term)
        rest = rest - term
    block = min(16, cells_x)

    @pl.loop(0, cells_x // block)
    def _(step):
        first = step * block * cells_z
        index = first + lax.broadcasted_iota(jnp.int32, (block * cells_z, count), 0)
        hit = index == key
        total = None
        for term in terms:
            left = jnp.where(hit, term, 0.0).astype(jnp.bfloat16)
            part = lax.dot_general(
                left, lanes, (((1,), (1,)), ((), ())), preferred_element_type=jnp.float32
            )
            total = part if total is None else total + part
        at = pl.ds(step * block, block)
        out[at] = out[at] + total.reshape(block, cells_z, cells_y)


def open_kernel(
    src_cell, src_wave, onehot, shot_group, rec_cell, rec_data,
    u_prev, u_cur, a_prev, a_cur, low, high,
    base_u, lat_u, dep_u, cross_u, base_a, lat_a, dep_a, cross_a, weight,
    old, now, base, lat, dep, cross, scale_row, rows, pad, first_z, sem_in, sem_out,
):
    cells_x, cells_z, cells_y = lat_u.shape
    masks = lateral_masks(cells_y)
    loads = []
    for j, (before, current) in enumerate(((u_prev, u_cur), (a_prev, a_cur))):
        loads.append(pltpu.make_async_copy(current.at[0], now.at[j], sem_in.at[j, 0]))
        loads.append(pltpu.make_async_copy(before.at[0], old.at[j], sem_in.at[j, 1]))
    for load in loads:
        load.start()
    sends = []

    def send(source, target):
        copy = pltpu.make_async_copy(source, target, sem_out.at[len(sends)])
        copy.start()
        sends.append(copy)

    blocks = onehot.shape[1]
    depth = lax.broadcasted_iota(jnp.int32, weight.shape, 1)
    value = jnp.zeros(weight.shape, jnp.float32)
    for block in range(blocks):
        scale = sum(
            onehot[shot_group[0], block, b].astype(jnp.float32) * 2.0 ** (-b)
            for b in range(onehot.shape[2])
        )
        value = jnp.where(depth // (cells_z // blocks) == block, scale, value)
    scale_row[...] = value
    send(scale_row, weight)

    targets = ((base_u, lat_u, dep_u, cross_u), (base_a, lat_a, dep_a, cross_a))
    for j in range(2):
        loads[2 * j].wait()
        loads[2 * j + 1].wait()
        fill_depth(
            pad,
            lambda at, j=j: now[j, at],
            lambda at, j=j: low[j, at],
            lambda at, j=j: high[j, at],
        )
        depth_pass(pad, first_z, dep.at[j])
        send(dep.at[j], targets[j][2])
        fill_rows(rows, lambda at, j=j: now[j, at])

        @pl.loop(0, cells_x // CHUNK)
        def _(step, j=j):
            x = step * CHUNK
            at = pl.ds(x, CHUNK)
            lat[j, at] = lateral(rows, x, masks)
            cross[j, at] = crossing(first_z, x)
            base[j, at] = 2.0 * now[j, at] - old[j, at]

        send(lat.at[j], targets[j][1])
        send(cross.at[j], targets[j][3])
        if j == 0:
            add_at(base.at[0], src_cell[0], src_wave[0, 0])
        else:
            place_receivers(base.at[1], rec_cell, rec_data)
        send(base.at[j], targets[j][0])
    for copy in sends:
        copy.wait()


def fetch_kernel(*refs):
    count = (len(refs) - 1) // 2
    sources, targets, sem = refs[:count], refs[count:-1], refs[-1]
    copies = [
        pltpu.make_async_copy(source, target, sem.at[i])
        for i, (source, target) in enumerate(zip(sources, targets))
    ]
    for copy in copies:
        copy.start()
    for copy in copies:
        copy.wait()


def first_kernel(
    mine, other, a_cur,
    base_u, lat_u, dep_u, cross_u, base_a, lat_a, dep_a, cross_a,
    u_one, a_one, grad, model, aniso_h, aniso_c, smooth, low, high,
):
    cells_x, cells_z, _ = u_one.shape
    own = position()[1] == 0

    @pl.loop(0, mine.shape[0])
    def _(q):
        for p in range(2):
            rows = pl.ds(q * 4 + p * 2, 2)
            pick = lambda j: jnp.where(own == (p == 0), mine[q, j], other[q, j])
            m, h, c, s = pick(0), pick(1), pick(2), pick(3)
            model[rows], aniso_h[rows], aniso_c[rows], smooth[rows] = m, h, c, s
            k_u = h * lat_u[rows] + dep_u[rows] + c * cross_u[rows]
            k_a = h * lat_a[rows] + dep_a[rows] + c * cross_a[rows]
            grad[rows] = a_cur[0, rows] * k_u
            new = base_u[rows] + m * k_u
            u_one[rows] = new
            a_one[rows] = base_a[rows] + m * k_a
            low[rows] = new[:, :REACH]
            high[rows] = new[:, cells_z - REACH :]
            edge = (pl.ds(cells_x + q, 1), pl.ds(2 * p, 2), slice(None))
            low[edge] = s[:, 0][None]
            high[edge] = s[:, cells_z - 1][None]


def side_kernel(step_index, src_cell, src_wave, now, old, aniso_h, base, side, rows):
    cells_x, _, cells_y = base.shape
    masks = lateral_masks(cells_y)
    fill_rows(rows, lambda at: now[at])

    @pl.loop(0, cells_x // CHUNK, unroll=UNROLL)
    def _(step):
        x = step * CHUNK
        at = pl.ds(x, CHUNK)
        base[at] = 2.0 * now[at] - old[at]
        side[at] = aniso_h[at] * lateral(rows, x, masks)

    add_at(base, src_cell[0], src_wave[0, step_index])


def second_kernel(
    u_one, base, side, a_one, grad, weight, model, aniso_c, low, high,
    u_two, keep, send, low_two, high_two, pad, first_z, dep,
):
    cells_x, cells_z, _ = u_two.shape
    fill_depth(pad, lambda at: u_one[at], lambda at: low[at], lambda at: high[at])
    depth_pass(pad, first_z, dep)
    own = position()[1] == 0

    @pl.loop(0, cells_x // CHUNK, unroll=2)
    def _(step):
        x = step * CHUNK
        at = pl.ds(x, CHUNK)
        k_u = side[at] + dep[at] + aniso_c[at] * crossing(first_z, x)
        new = base[at] + model[at] * k_u
        u_two[at] = new
        low_two[at] = new[:, :REACH]
        high_two[at] = new[:, cells_z - REACH :]
        total = weight[...] * (grad[at] + a_one[at] * k_u)
        keep[step] = jnp.where(own, total[:2], total[2:])
        send[step] = jnp.where(own, total[2:], total[:2])


def sum_kernel(parts, out):
    total = parts[0]
    for peer in range(1, parts.shape[0]):
        total = total + parts[peer]
    for peer in range(parts.shape[0]):
        out[peer] = total


def join_kernel(mine, other, summed, low, high):
    cells_z = summed.shape[1]
    count = mine.shape[0]
    own = position()[1] == 0

    @pl.loop(0, count)
    def _(q):
        for p in range(2):
            rows = pl.ds(q * 4 + p * 2, 2)
            g = jnp.where(own == (p == 0), mine[q], other[q])
            summed[rows] = g
            for k in range(2):
                edge = (pl.ds(k * count + q, 1), pl.ds(2 * p, 2), slice(None))
                low[edge] = g[:, k][None]
                high[edge] = g[:, cells_z - 1 - k][None]


def shifted_y(flat):
    cells_y = flat.shape[-1]
    lane = lax.broadcasted_iota(jnp.int32, (1,) * (flat.ndim - 2) + (8, cells_y), flat.ndim - 1)
    axis = flat.ndim - 1
    if flat.ndim == 2:
        lane = lax.broadcasted_iota(jnp.int32, flat.shape, 1)
    right = jnp.where(lane < cells_y - 1, pltpu.roll(flat, cells_y - 1, axis), 0.0)
    left = jnp.where(lane >= 1, pltpu.roll(flat, 1, axis), 0.0)
    return right + left


def relax_kernel(summed, smooth, out, inner, own_g, own_s, own_out, wide, once):
    cells_x, cells_z, cells_y = summed.shape
    for ref in (wide, once):
        blank = jnp.zeros((1, *ref.shape[1:]), jnp.float32)
        ref[pl.ds(0, 1)] = blank
        ref[pl.ds(cells_x + 1, 1)] = blank

    @pl.loop(0, cells_x // CHUNK, unroll=2)
    def _(q):
        at = pl.ds(q * CHUNK + 1, CHUNK)
        blank = jnp.zeros((CHUNK, 1, cells_y), jnp.float32)
        for ref in (wide, once):
            ref[at, pl.ds(MID - 1, 1), :] = blank
            ref[at, pl.ds(MID + cells_z, 1), :] = blank
        wide[at, pl.ds(MID, cells_z), :] = summed[pl.ds(q * CHUNK, CHUNK)]

    def relaxed(ref, x, factor):
        at = lambda dx, dz: ref[pl.ds(x + 1 + dx, CHUNK), pl.ds(MID + dz, cells_z), :]
        v = at(0, 0)
        near = at(1, 0) + at(-1, 0) + at(0, 1) + at(0, -1)
        flat = v.reshape(CHUNK * cells_z // 8, 8, cells_y)
        near = near + shifted_y(flat).reshape(v.shape)
        return v + factor * (near - 6.0 * v)

    @pl.loop(0, cells_x // CHUNK, unroll=2)
    def _(q):
        x = q * CHUNK
        factor = smooth[pl.ds(x, CHUNK)]
        once[pl.ds(x + 1, CHUNK), pl.ds(MID, cells_z), :] = relaxed(wide, x, factor)
        g = summed[pl.ds(x, CHUNK)]
        for i, k in enumerate((0, cells_z - 1)):
            own_g[i, pl.ds(x, CHUNK)] = g[:, k]
        for i, k in enumerate((0, 1, cells_z - 2, cells_z - 1)):
            own_s[i, pl.ds(x, CHUNK)] = factor[:, k]

    depth = lax.broadcasted_iota(jnp.int32, (1, cells_z, cells_y), 1)
    between = (depth >= 2) & (depth < cells_z - 2)

    def sweep(q, total):
        x = q * CHUNK
        value = relaxed(once, x, smooth[pl.ds(x, CHUNK)])
        out[pl.ds(x, CHUNK)] = value
        for i, k in enumerate((0, 1, cells_z - 2, cells_z - 1)):
            own_out[i, pl.ds(x, CHUNK)] = value[:, k]
        squares = jnp.where(between, value * value, 0.0)
        return total + jnp.sum(squares.reshape(CHUNK * cells_z // 8, 8, cells_y), axis=0)

    inner[...] = lax.fori_loop(
        0, cells_x // CHUNK, sweep, jnp.zeros((8, cells_y), jnp.float32), unroll=2
    )


def edge_kernel(
    smoothed_in, inner, own_g, own_s, own_out, low_sum, high_sum, low_one, high_one,
    smoothed, square, planes,
):
    cells_x, cells_z, cells_y = smoothed.shape
    smoothed[...] = smoothed_in[...]
    count = cells_x // 4
    blank = jnp.zeros((8, cells_y), jnp.float32)
    total = inner[...]
    for side, (sums, smooth, present) in enumerate(
        ((low_sum, low_one, has_sides()[0]), (high_sum, high_one, has_sides()[1]))
    ):
        for k in range(4):
            planes[k, pl.ds(0, 8)] = blank
            planes[k, pl.ds(8 + cells_x, 8)] = blank

        @pl.loop(0, count)
        def _(q, sums=sums, smooth=smooth, present=present):
            at = pl.ds(8 + 4 * q, 4)
            for k in range(2):
                planes[k, at] = jnp.where(present, sums[k * count + q], 0.0)
            planes[2, at] = jnp.where(present, smooth[cells_x + q], 0.0)

        def near(k):
            at = lambda dx: planes[k, pl.ds(8 + dx, cells_x)]
            return at(1) + at(-1) + shifted_y(at(0))

        whole = pl.ds(8, cells_x)
        first, second, factor = planes[0, whole], planes[1, whole], planes[2, whole]
        outside = first + factor * (near(0) + second + own_g[side] - 6.0 * first)
        edge, inside = (0, 1) if side == 0 else (3, 2)
        change = own_s[edge] * first
        planes[3, whole] = change
        value = own_out[edge] + change + own_s[edge] * (near(3) - 6.0 * change + outside)
        beside = own_out[inside] + own_s[inside] * change
        squares = value * value + beside * beside
        total = total + jnp.sum(squares.reshape(cells_x // 8, 8, cells_y), axis=0)
        planes[0, whole] = value
        planes[1, whole] = beside
        rows = (0, 1) if side == 0 else (cells_z - 1, cells_z - 2)

        @pl.loop(0, count)
        def _(q, rows=rows):
            for k, z in enumerate(rows):
                smoothed[pl.ds(4 * q, 4), pl.ds(z, 1), :] = planes[k, pl.ds(8 + 4 * q, 4)][:, None]

    row = jnp.sum(total, axis=0, keepdims=True)
    square[...] = jnp.broadcast_to(row[None], square.shape)


def third_kernel(u_two, side, model, aniso_c, low, high, change, pad, first_z, dep):
    cells_x = change.shape[0]
    fill_depth(pad, lambda at: u_two[at], lambda at: low[at], lambda at: high[at])
    depth_pass(pad, first_z, dep)

    @pl.loop(0, cells_x // CHUNK, unroll=2)
    def _(step):
        x = step * CHUNK
        at = pl.ds(x, CHUNK)
        change[at] = model[at] * (side[at] + dep[at] + aniso_c[at] * crossing(first_z, x))


def shifted_y(flat):
    cells_y = flat.shape[-1]
    lane = lax.broadcasted_iota(jnp.int32, (1,) * (flat.ndim - 2) + (8, cells_y), flat.ndim - 1)
    axis = flat.ndim - 1
    if flat.ndim == 2:
        lane = lax.broadcasted_iota(jnp.int32, flat.shape, 1)
    right = jnp.where(lane < cells_y - 1, pltpu.roll(flat, cells_y - 1, axis), 0.0)
    left = jnp.where(lane >= 1, pltpu.roll(flat, 1, axis), 0.0)
    return right + left


def relax_kernel(summed, smooth, out, inner, own_g, own_s, own_out, wide, once):
    cells_x, cells_z, cells_y = summed.shape
    for ref in (wide, once):
        blank = jnp.zeros((1, *ref.shape[1:]), jnp.float32)
        ref[pl.ds(0, 1)] = blank
        ref[pl.ds(cells_x + 1, 1)] = blank

    @pl.loop(0, cells_x // CHUNK, unroll=2)
    def _(q):
        at = pl.ds(q * CHUNK + 1, CHUNK)
        blank = jnp.zeros((CHUNK, 1, cells_y), jnp.float32)
        for ref in (wide, once):
            ref[at, pl.ds(MID - 1, 1), :] = blank
            ref[at, pl.ds(MID + cells_z, 1), :] = blank
        wide[at, pl.ds(MID, cells_z), :] = summed[pl.ds(q * CHUNK, CHUNK)]

    def relaxed(ref, x, factor):
        at = lambda dx, dz: ref[pl.ds(x + 1 + dx, CHUNK), pl.ds(MID + dz, cells_z), :]
        v = at(0, 0)
        near = at(1, 0) + at(-1, 0) + at(0, 1) + at(0, -1)
        flat = v.reshape(CHUNK * cells_z // 8, 8, cells_y)
        near = near + shifted_y(flat).reshape(v.shape)
        return v + factor * (near - 6.0 * v)

    @pl.loop(0, cells_x // CHUNK, unroll=2)
    def _(q):
        x = q * CHUNK
        factor = smooth[pl.ds(x, CHUNK)]
        once[pl.ds(x + 1, CHUNK), pl.ds(MID, cells_z), :] = relaxed(wide, x, factor)
        g = summed[pl.ds(x, CHUNK)]
        for i, k in enumerate((0, cells_z - 1)):
            own_g[i, pl.ds(x, CHUNK)] = g[:, k]
        for i, k in enumerate((0, 1, cells_z - 2, cells_z - 1)):
            own_s[i, pl.ds(x, CHUNK)] = factor[:, k]

    depth = lax.broadcasted_iota(jnp.int32, (1, cells_z, cells_y), 1)
    between = (depth >= 2) & (depth < cells_z - 2)

    def sweep(q, total):
        x = q * CHUNK
        value = relaxed(once, x, smooth[pl.ds(x, CHUNK)])
        out[pl.ds(x, CHUNK)] = value
        for i, k in enumerate((0, 1, cells_z - 2, cells_z - 1)):
            own_out[i, pl.ds(x, CHUNK)] = value[:, k]
        squares = jnp.where(between, value * value, 0.0)
        return total + jnp.sum(squares.reshape(CHUNK * cells_z // 8, 8, cells_y), axis=0)

    inner[...] = lax.fori_loop(
        0, cells_x // CHUNK, sweep, jnp.zeros((8, cells_y), jnp.float32), unroll=2
    )


def edge_kernel(
    smoothed_in, inner, own_g, own_s, own_out, low_sum, high_sum, low_one, high_one,
    smoothed, square, planes,
):
    cells_x, cells_z, cells_y = smoothed.shape
    smoothed[...] = smoothed_in[...]
    count = cells_x // 4
    blank = jnp.zeros((8, cells_y), jnp.float32)
    total = inner[...]
    for side, (sums, smooth, present) in enumerate(
        ((low_sum, low_one, has_sides()[0]), (high_sum, high_one, has_sides()[1]))
    ):
        for k in range(4):
            planes[k, pl.ds(0, 8)] = blank
            planes[k, pl.ds(8 + cells_x, 8)] = blank

        @pl.loop(0, count)
        def _(q, sums=sums, smooth=smooth, present=present):
            at = pl.ds(8 + 4 * q, 4)
            for k in range(2):
                planes[k, at] = jnp.where(present, sums[k * count + q], 0.0)
            planes[2, at] = jnp.where(present, smooth[cells_x + q], 0.0)

        def near(k):
            at = lambda dx: planes[k, pl.ds(8 + dx, cells_x)]
            return at(1) + at(-1) + shifted_y(at(0))

        whole = pl.ds(8, cells_x)
        first, second, factor = planes[0, whole], planes[1, whole], planes[2, whole]
        outside = first + factor * (near(0) + second + own_g[side] - 6.0 * first)
        edge, inside = (0, 1) if side == 0 else (3, 2)
        change = own_s[edge] * first
        planes[3, whole] = change
        value = own_out[edge] + change + own_s[edge] * (near(3) - 6.0 * change + outside)
        beside = own_out[inside] + own_s[inside] * change
        squares = value * value + beside * beside
        total = total + jnp.sum(squares.reshape(cells_x // 8, 8, cells_y), axis=0)
        planes[0, whole] = value
        planes[1, whole] = beside
        rows = (0, 1) if side == 0 else (cells_z - 1, cells_z - 2)

        @pl.loop(0, count)
        def _(q, rows=rows):
            for k, z in enumerate(rows):
                smoothed[pl.ds(4 * q, 4), pl.ds(z, 1), :] = planes[k, pl.ds(8 + 4 * q, 4)][:, None]

    row = jnp.sum(total, axis=0, keepdims=True)
    square[...] = jnp.broadcast_to(row[None], square.shape)


def third_kernel(u_two, side, model, aniso_c, low, high, change, pad, first_z, dep):
    cells_x = change.shape[0]
    fill_depth(pad, lambda at: u_two[at], lambda at: low[at], lambda at: high[at])
    depth_pass(pad, first_z, dep)

    @pl.loop(0, cells_x // CHUNK, unroll=2)
    def _(step):
        x = step * CHUNK
        at = pl.ds(x, CHUNK)
        change[at] = model[at] * (side[at] + dep[at] + aniso_c[at] * crossing(first_z, x))


def close_kernel(squares, smoothed, model, base, change, model_next, grad_dir, wave_next):
    cells_x, cells_z, cells_y = smoothed.shape
    rows = grad_dir.shape[0]
    total = jnp.sum(jnp.sum(squares[...], axis=0), axis=1, keepdims=True)
    cells = cells_x * depth_range(cells_z)[1] * cells_y
    scale = lax.rsqrt(total / cells + 1e-06)
    scale = jnp.broadcast_to(scale, (8, cells_y))[None]

    def factor(value):
        flat = value.reshape(value.shape[0] * cells_z // 8, 8, cells_y) * scale
        return flat.reshape(value.shape)

    @pl.loop(0, cells_x // CHUNK)
    def _(step):
        at = pl.ds(step * CHUNK, CHUNK)
        shrink = 1.0 - 0.25 * jnp.tanh(factor(smoothed[at]))
        wave_next[0, at] = base[at] + change[at] * shrink

    _, core, chip = position()
    at = pl.ds((2 * chip + core) * rows, rows)
    direction = factor(smoothed[at])
    grad_dir[...] = direction
    model_next[...] = model[at] * (1.0 - 0.25 * jnp.tanh(direction))


def shift(low_edge, high_edge):
    count = lax.axis_size(DEPTH)
    forward = [(i, (i + 1) % count) for i in range(count)]
    backward = [(target, source) for source, target in forward]
    return lax.ppermute(high_edge, DEPTH, forward), lax.ppermute(low_edge, DEPTH, backward)


def body(
    u_prev,
    u_cur,
    a_prev,
    a_cur,
    model,
    aniso_h,
    aniso_c,
    smooth_coef,
    bin_onehot,
    shot_group,
    src_cell,
    rec_cell,
    src_wave,
    rec_data,
):
    _, cells_x, cells_z, cells_y = u_cur.shape
    rows = model.shape[0]
    peers = lax.axis_size(PEERS)
    slab = f32(cells_x, cells_z, cells_y)
    scratch = lambda *shape: pltpu.VMEM(shape, jnp.float32)
    pad = scratch(cells_x, cells_z + 2 * MID, cells_y)
    first_z = scratch(cells_x + 2 * REACH, cells_z, cells_y)
    padded_rows = first_z
    dep = scratch(cells_x, cells_z, cells_y)
    pair = scratch(2, cells_x, cells_z, cells_y)
    work = 80 * cells_x * cells_z * cells_y

    spread = call(
        spread_kernel,
        (model, aniso_h, aniso_c, smooth_coef),
        0,
        f32(peers, 4, rows, cells_z, cells_y),
        (
            scratch(4, rows, cells_z, cells_y),
            pltpu.SemaphoreType.DMA((4,)),
            pltpu.SemaphoreType.DMA((peers,)),
        ),
        hbm_in=range(4),
        hbm_out=(0,),
        grant=62,
    )
    mine = lax.all_to_all(spread, PEERS, 0, 0, tiled=True)

    edges = lambda start: jnp.concatenate(
        [lax.slice_in_dim(v, start, start + REACH, axis=2) for v in (u_cur, a_cur)]
    )
    low, high = shift(edges(0), edges(cells_z - REACH))
    *parts, weight = call(
        open_kernel,
        (src_cell, src_wave, bin_onehot, shot_group, rec_cell, rec_data)
        + (u_prev, u_cur, a_prev, a_cur, low, high),
        4,
        (slab,) * 8 + (f32(1, cells_z, cells_y),),
        (pair,) * 6
        + (scratch(1, cells_z, cells_y), padded_rows, pad, first_z)
        + (pltpu.SemaphoreType.DMA((2, 2)), pltpu.SemaphoreType.DMA((9,))),
        2 * work,
        hbm_in=range(6, 10),
        hbm_out=range(9),
        grant=61,
    )
    other = lax.ppermute(mine, "core", SWAP)
    *parts, weight, adjoint = call(
        fetch_kernel,
        (*parts, weight, a_cur),
        0,
        (slab,) * 8 + (f32(1, cells_z, cells_y), f32(*a_cur.shape)),
        (pltpu.SemaphoreType.DMA((10,)),),
        hbm_in=range(10),
        grant=49,
    )
    payload = f32(cells_x + peers, REACH, cells_y)
    u_one, a_one, grad, model_slab, h_slab, c_slab, smooth_slab, low_edge, high_edge = call(
        first_kernel,
        (mine, other, adjoint, *parts),
        0,
        (slab,) * 7 + (payload, payload),
        (),
        20 * slab.size,
    )
    low_one, high_one = shift(low_edge, high_edge)
    base, side = call(
        functools.partial(side_kernel, 1),
        (src_cell, src_wave, u_one, u_cur[0], h_slab),
        2,
        (slab, slab),
        (padded_rows,),
        work // 2,
    )
    split = f32(peers, rows, cells_z, cells_y)
    edge = f32(cells_x, REACH, cells_y)
    u_two, keep, send, low_edge, high_edge = call(
        second_kernel,
        (u_one, base, side, a_one, grad, weight, model_slab, c_slab, low_one, high_one),
        0,
        (slab, split, split, edge, edge),
        (pad, first_z, dep),
        work,
    )
    chip_sum = keep + lax.ppermute(send, "core", SWAP)
    shares = lax.all_to_all(chip_sum, PEERS, 0, 0, tiled=True)
    total = call(sum_kernel, (shares,), 0, split)
    mine = lax.all_to_all(total, PEERS, 0, 0, tiled=True)
    other = lax.ppermute(mine, "core", SWAP)
    low_two, high_two = shift(low_edge, high_edge)
    payload = f32(2 * peers, 4, cells_y)
    summed, low_edge, high_edge = call(
        join_kernel, (mine, other), 0, (slab, payload, payload)
    )
    low_sum, high_sum = shift(low_edge, high_edge)
    base, side = call(
        functools.partial(side_kernel, 2),
        (src_cell, src_wave, u_two, u_one, h_slab),
        2,
        (slab, slab),
        (padded_rows,),
        work // 2,
    )
    edges = f32(4, cells_x, cells_y)
    smoothed, inner, own_g, own_s, own_out = call(
        relax_kernel,
        (summed, smooth_slab),
        0,
        (slab, f32(8, cells_y), f32(2, cells_x, cells_y), edges, edges),
        (scratch(cells_x + 2, cells_z + 2 * MID, cells_y),) * 2,
        40 * slab.size,
    )
    change = call(
        third_kernel,
        (u_two, side, model_slab, c_slab, low_two, high_two),
        0,
        slab,
        (pad, first_z, dep),
        work,
    )
    smoothed, square = call(
        edge_kernel,
        (smoothed, inner, own_g, own_s, own_out, low_sum, high_sum, low_one, high_one),
        0,
        (slab, f32(lax.axis_size(DEPTH), 1, cells_y)),
        (scratch(4, cells_x + 16, cells_y),),
        4 * slab.size,
    )
    squares = lax.all_to_all(square, DEPTH, 0, 0, tiled=True)
    share = f32(rows, cells_z, cells_y)
    return call(
        close_kernel,
        (squares, smoothed, model_slab, base, change),
        0,
        (share, share, f32(1, cells_x, cells_z, cells_y)),
        (),
        20 * slab.size,
    )


def solution(mesh):
    mesh = jax.sharding.Mesh(
        mesh.devices.reshape(2, 8, 2, 2, 4), ("xh", "z", "core", "xl", "y")
    )
    return jax.shard_map(
        body,
        mesh=mesh,
        in_specs=(
            P(SHOT, None, DEPTH, None),
            P(SHOT, None, DEPTH, None),
            P(SHOT, None, DEPTH, None),
            P(SHOT, None, DEPTH, None),
            P(SHOT, DEPTH, None),
            P(SHOT, DEPTH, None),
            P(SHOT, DEPTH, None),
            P(SHOT, DEPTH, None),
            P(None, DEPTH, None),
            P(SHOT),
            P(SHOT),
            P(SHOT, None),
            P(SHOT, None),
            P(SHOT, None, None),
        ),
        out_specs=(
            P(SHOT, DEPTH, None),
            P(SHOT, DEPTH, None),
            P(SHOT, None, DEPTH, None),
        ),
        check_vma=False,
    )
```

```python
import functools

import jax
import jax.numpy as jnp
from jax import lax
from jax.experimental import pallas as pl
from jax.experimental.pallas import tpu as pltpu
from jax.sharding import PartitionSpec as P


second_coef = (-205.0 / 72.0, 8.0 / 5.0, -1.0 / 5.0, 8.0 / 315.0, -1.0 / 560.0)
first_coef = (0.8, -0.2, 4.0 / 105.0, -1.0 / 280.0)

SHOT = ("xh", "z", "core")
DEPTH = ("xl", "y")
PEERS = ("xh", "z")
SWAP = [(0, 1), (1, 0)]
REACH = 4
MID = 8
CHUNK = 4
UNROLL = 4
VMEM = pl.BlockSpec(memory_space=pltpu.VMEM)
SMEM = pl.BlockSpec(memory_space=pltpu.SMEM)
HBM = pl.BlockSpec(memory_space=pltpu.HBM)


def f32(*shape):
    return jax.ShapeDtypeStruct(shape, jnp.float32)


def call(kernel, args, smem, outs, scratch=(), flops=0, hbm_in=(), hbm_out=(), grant=16):
    bytes_accessed = 4 * sum(a.size for a in args)
    spec = lambda i: SMEM if i < smem else HBM if i in hbm_in else VMEM
    single = not isinstance(outs, tuple)
    out_specs = [HBM if i in hbm_out else VMEM for i in range(1 if single else len(outs))]
    return pl.pallas_call(
        kernel,
        out_shape=outs,
        in_specs=[spec(i) for i in range(len(args))],
        out_specs=out_specs[0] if single else tuple(out_specs),
        scratch_shapes=list(scratch),
        cost_estimate=pl.CostEstimate(
            flops=flops, bytes_accessed=bytes_accessed, transcendentals=0
        ),
        compiler_params=pltpu.CompilerParams(vmem_limit_bytes=grant * 2**20),
    )(*args)


def position():
    layer = lax.axis_index("xl") * lax.axis_size("y") + lax.axis_index("y")
    chip = lax.axis_index("xh") * lax.axis_size("z") + lax.axis_index("z")
    return layer, lax.axis_index("core"), chip


def fill_rows(rows, read):
    cells_x = rows.shape[0] - 2 * REACH
    zeros = jnp.zeros((REACH, *rows.shape[1:]), jnp.float32)
    rows[pl.ds(0, REACH)] = zeros
    rows[pl.ds(REACH + cells_x, REACH)] = zeros

    @pl.loop(0, cells_x // CHUNK)
    def _(step):
        x = step * CHUNK
        rows[pl.ds(REACH + x, CHUNK)] = read(pl.ds(x, CHUNK))


def has_sides():
    layer, _, _ = position()
    return layer > 0, layer < lax.axis_size("xl") * lax.axis_size("y") - 1


def depth_range(cells_z):
    layer, _, _ = position()
    return layer * cells_z, cells_z * lax.axis_size("xl") * lax.axis_size("y")


def fill_depth(pad, read, low, high):
    cells_x, cells_z = pad.shape[0], pad.shape[1] - 2 * MID
    below, above = has_sides()

    @pl.loop(0, cells_x // CHUNK, unroll=2)
    def _(step):
        at = pl.ds(step * CHUNK, CHUNK)
        pad[at, pl.ds(MID, cells_z), :] = read(at)
        pad[at, pl.ds(MID - REACH, REACH), :] = jnp.where(below, low(at), 0.0)
        pad[at, pl.ds(MID + cells_z, REACH), :] = jnp.where(above, high(at), 0.0)


def depth_pass(pad, first_z, second_z):
    cells_x, cells_z = second_z.shape[0], second_z.shape[1]
    zeros = jnp.zeros((REACH, *first_z.shape[1:]), jnp.float32)
    first_z[pl.ds(0, REACH)] = zeros
    first_z[pl.ds(REACH + cells_x, REACH)] = zeros

    @pl.loop(0, cells_x // CHUNK, unroll=2)
    def _(step):
        x = step * CHUNK
        at = lambda k: pad[pl.ds(x, CHUNK), pl.ds(MID + k, cells_z), :]
        two = second_coef[0] * at(0)
        one = None
        for k in range(1, 5):
            above, below = at(k), at(-k)
            two = two + second_coef[k] * (above + below)
            term = first_coef[k - 1] * (above - below)
            one = term if one is None else one + term
        second_z[pl.ds(x, CHUNK)] = two
        first_z[pl.ds(REACH + x, CHUNK)] = one


def lateral_masks(cells_y):
    lane = lax.broadcasted_iota(jnp.int32, (1, 8, cells_y), 2)
    up = [jnp.where(lane < cells_y - k, second_coef[k], 0.0) for k in range(1, 5)]
    down = [jnp.where(lane >= k, second_coef[k], 0.0) for k in range(1, 5)]
    return up, down


def lateral(rows, x, masks):
    up, down = masks
    at = lambda k: rows[pl.ds(REACH + x + k, CHUNK)]
    v = at(0)
    cells_z, cells_y = v.shape[1:]
    total = (2.0 * second_coef[0]) * v
    for k in range(1, 5):
        total = total + second_coef[k] * (at(k) + at(-k))
    flat = v.reshape(CHUNK * cells_z // 8, 8, cells_y)
    along_y = None
    for k in range(1, 5):
        term = up[k - 1] * pltpu.roll(flat, cells_y - k, 2) + down[k - 1] * pltpu.roll(flat, k, 2)
        along_y = term if along_y is None else along_y + term
    return total + along_y.reshape(v.shape)


def crossing(first_z, x):
    at = lambda k: first_z[pl.ds(REACH + x + k, CHUNK)]
    total = None
    for k in range(1, 5):
        term = first_coef[k - 1] * (at(k) - at(-k))
        total = term if total is None else total + term
    return total


def add_at(ref, cell, amount):
    cells_z, cells_y = ref.shape[1], ref.shape[2]
    z_start, depth_cells = depth_range(cells_z)
    row = cell // cells_y
    x, z = row // depth_cells, row % depth_cells - z_start

    @pl.when((z >= 0) & (z < cells_z))
    def _():
        lane = lax.broadcasted_iota(jnp.int32, (1, 1, cells_y), 2)
        at = (pl.ds(x, 1), pl.ds(z, 1), slice(None))
        ref[at] = ref[at] + jnp.where(lane == cell % cells_y, amount, 0.0)


def spread_kernel(model, aniso_h, aniso_c, smooth, out, own, sem_in, sem_out):
    arrays = (model, aniso_h, aniso_c, smooth)
    loads = [pltpu.make_async_copy(ref, own.at[j], sem_in.at[j]) for j, ref in enumerate(arrays)]
    for load in loads:
        load.start()
    for load in loads:
        load.wait()
    sends = [pltpu.make_async_copy(own, out.at[p], sem_out.at[p]) for p in range(out.shape[0])]
    for send in sends:
        send.start()
    for send in sends:
        send.wait()


def place_receivers(out, rec_cell, rec_data):
    cells_x, cells_z, cells_y = out.shape
    z_start, depth_cells = depth_range(cells_z)
    cell = rec_cell[...]
    row = cell // cells_y
    z = row % depth_cells - z_start
    key = jnp.where((z >= 0) & (z < cells_z), row // depth_cells * cells_z + z, -1)
    y = cell % cells_y
    count = cell.shape[1]
    lanes = jnp.where(
        lax.broadcasted_iota(jnp.int32, (cells_y, count), 0) == y, 1.0, 0.0
    ).astype(jnp.bfloat16)
    rest, terms = rec_data[0, pl.ds(0, 1), :], []
    for _ in range(3):
        term = rest.astype(jnp.bfloat16).astype(jnp.float32)
        terms.append(term)
        rest = rest - term
    block = min(16, cells_x)

    @pl.loop(0, cells_x // block)
    def _(step):
        first = step * block * cells_z
        index = first + lax.broadcasted_iota(jnp.int32, (block * cells_z, count), 0)
        hit = index == key
        total = None
        for term in terms:
            left = jnp.where(hit, term, 0.0).astype(jnp.bfloat16)
            part = lax.dot_general(
                left, lanes, (((1,), (1,)), ((), ())), preferred_element_type=jnp.float32
            )
            total = part if total is None else total + part
        at = pl.ds(step * block, block)
        out[at] = out[at] + total.reshape(block, cells_z, cells_y)


def open_kernel(
    src_cell, src_wave, onehot, shot_group, rec_cell, rec_data,
    u_prev, u_cur, a_prev, a_cur, low, high,
    base_u, lat_u, dep_u, cross_u, base_a, lat_a, dep_a, cross_a, weight,
    old, now, base, lat, dep, cross, scale_row, rows, pad, first_z, sem_in, sem_out,
):
    cells_x, cells_z, cells_y = lat_u.shape
    masks = lateral_masks(cells_y)
    loads = []
    for j, (before, current) in enumerate(((u_prev, u_cur), (a_prev, a_cur))):
        loads.append(pltpu.make_async_copy(current.at[0], now.at[j], sem_in.at[j, 0]))
        loads.append(pltpu.make_async_copy(before.at[0], old.at[j], sem_in.at[j, 1]))
    for load in loads:
        load.start()
    sends = []

    def send(source, target):
        copy = pltpu.make_async_copy(source, target, sem_out.at[len(sends)])
        copy.start()
        sends.append(copy)

    blocks = onehot.shape[1]
    depth = lax.broadcasted_iota(jnp.int32, weight.shape, 1)
    value = jnp.zeros(weight.shape, jnp.float32)
    for block in range(blocks):
        scale = sum(
            onehot[shot_group[0], block, b].astype(jnp.float32) * 2.0 ** (-b)
            for b in range(onehot.shape[2])
        )
        value = jnp.where(depth // (cells_z // blocks) == block, scale, value)
    scale_row[...] = value
    send(scale_row, weight)

    targets = ((base_u, lat_u, dep_u, cross_u), (base_a, lat_a, dep_a, cross_a))
    for j in range(2):
        loads[2 * j].wait()
        loads[2 * j + 1].wait()
        fill_depth(
            pad,
            lambda at, j=j: now[j, at],
            lambda at, j=j: low[j, at],
            lambda at, j=j: high[j, at],
        )
        depth_pass(pad, first_z, dep.at[j])
        send(dep.at[j], targets[j][2])
        fill_rows(rows, lambda at, j=j: now[j, at])

        @pl.loop(0, cells_x // CHUNK)
        def _(step, j=j):
            x = step * CHUNK
            at = pl.ds(x, CHUNK)
            lat[j, at] = lateral(rows, x, masks)
            cross[j, at] = crossing(first_z, x)
            base[j, at] = 2.0 * now[j, at] - old[j, at]

        send(lat.at[j], targets[j][1])
        send(cross.at[j], targets[j][3])
        if j == 0:
            add_at(base.at[0], src_cell[0], src_wave[0, 0])
        else:
            place_receivers(base.at[1], rec_cell, rec_data)
        send(base.at[j], targets[j][0])
    for copy in sends:
        copy.wait()


def fetch_kernel(*refs):
    count = (len(refs) - 1) // 2
    sources, targets, sem = refs[:count], refs[count:-1], refs[-1]
    copies = [
        pltpu.make_async_copy(source, target, sem.at[i])
        for i, (source, target) in enumerate(zip(sources, targets))
    ]
    for copy in copies:
        copy.start()
    for copy in copies:
        copy.wait()


def first_kernel(
    mine, other, a_cur,
    base_u, lat_u, dep_u, cross_u, base_a, lat_a, dep_a, cross_a,
    u_one, a_one, grad, model, aniso_h, aniso_c, smooth, low, high,
):
    cells_x, cells_z, _ = u_one.shape
    own = position()[1] == 0

    @pl.loop(0, mine.shape[0])
    def _(q):
        for p in range(2):
            rows = pl.ds(q * 4 + p * 2, 2)
            pick = lambda j: jnp.where(own == (p == 0), mine[q, j], other[q, j])
            m, h, c, s = pick(0), pick(1), pick(2), pick(3)
            model[rows], aniso_h[rows], aniso_c[rows], smooth[rows] = m, h, c, s
            k_u = h * lat_u[rows] + dep_u[rows] + c * cross_u[rows]
            k_a = h * lat_a[rows] + dep_a[rows] + c * cross_a[rows]
            grad[rows] = a_cur[0, rows] * k_u
            new = base_u[rows] + m * k_u
            u_one[rows] = new
            a_one[rows] = base_a[rows] + m * k_a
            low[rows] = new[:, :REACH]
            high[rows] = new[:, cells_z - REACH :]
            edge = (pl.ds(cells_x + q, 1), pl.ds(2 * p, 2), slice(None))
            low[edge] = s[:, 0][None]
            high[edge] = s[:, cells_z - 1][None]


def side_kernel(step_index, src_cell, src_wave, now, old, aniso_h, base, side, rows):
    cells_x, _, cells_y = base.shape
    masks = lateral_masks(cells_y)
    fill_rows(rows, lambda at: now[at])

    @pl.loop(0, cells_x // CHUNK, unroll=UNROLL)
    def _(step):
        x = step * CHUNK
        at = pl.ds(x, CHUNK)
        base[at] = 2.0 * now[at] - old[at]
        side[at] = aniso_h[at] * lateral(rows, x, masks)

    add_at(base, src_cell[0], src_wave[0, step_index])


def side_halo_kernel(
    step_index, src_cell, src_wave, now, old, aniso_h, low, high,
    base, side, low_in, high_in, rows, sem,
):
    copies = [
        pltpu.make_async_copy(low, low_in, sem.at[0]),
        pltpu.make_async_copy(high, high_in, sem.at[1]),
    ]
    for copy in copies:
        copy.start()
    side_kernel(step_index, src_cell, src_wave, now, old, aniso_h, base, side, rows)
    for copy in copies:
        copy.wait()


def second_kernel(
    u_one, base, side, a_one, grad, weight, model, aniso_c, low, high,
    u_two, keep, send, pad, first_z, dep,
):
    cells_x = u_two.shape[0]
    fill_depth(pad, lambda at: u_one[at], lambda at: low[at], lambda at: high[at])
    depth_pass(pad, first_z, dep)
    own = position()[1] == 0

    @pl.loop(0, cells_x // CHUNK, unroll=2)
    def _(step):
        x = step * CHUNK
        at = pl.ds(x, CHUNK)
        k_u = side[at] + dep[at] + aniso_c[at] * crossing(first_z, x)
        u_two[at] = base[at] + model[at] * k_u
        total = weight[...] * (grad[at] + a_one[at] * k_u)
        keep[step] = jnp.where(own, total[:2], total[2:])
        send[step] = jnp.where(own, total[2:], total[:2])


def rim_kernel(field, low, high):
    cells_x, cells_z, _ = field.shape

    @pl.loop(0, cells_x // CHUNK, unroll=2)
    def _(step):
        at = pl.ds(step * CHUNK, CHUNK)
        low[at] = field[at, :REACH]
        high[at] = field[at, cells_z - REACH :]


def sum_kernel(parts, out):
    total = parts[0]
    for peer in range(1, parts.shape[0]):
        total = total + parts[peer]
    for peer in range(parts.shape[0]):
        out[peer] = total


def join_kernel(mine, other, summed, low, high):
    cells_z = summed.shape[1]
    count = mine.shape[0]
    own = position()[1] == 0

    @pl.loop(0, count)
    def _(q):
        for p in range(2):
            rows = pl.ds(q * 4 + p * 2, 2)
            g = jnp.where(own == (p == 0), mine[q], other[q])
            summed[rows] = g
            for k in range(2):
                edge = (pl.ds(k * count + q, 1), pl.ds(2 * p, 2), slice(None))
                low[edge] = g[:, k][None]
                high[edge] = g[:, cells_z - 1 - k][None]


def shifted_y(flat):
    cells_y = flat.shape[-1]
    lane = lax.broadcasted_iota(jnp.int32, (1,) * (flat.ndim - 2) + (8, cells_y), flat.ndim - 1)
    axis = flat.ndim - 1
    if flat.ndim == 2:
        lane = lax.broadcasted_iota(jnp.int32, flat.shape, 1)
    right = jnp.where(lane < cells_y - 1, pltpu.roll(flat, cells_y - 1, axis), 0.0)
    left = jnp.where(lane >= 1, pltpu.roll(flat, 1, axis), 0.0)
    return right + left


def relax_kernel(summed, smooth, out, inner, own_g, own_s, own_out, wide, once):
    cells_x, cells_z, cells_y = summed.shape
    for ref in (wide, once):
        blank = jnp.zeros((1, *ref.shape[1:]), jnp.float32)
        ref[pl.ds(0, 1)] = blank
        ref[pl.ds(cells_x + 1, 1)] = blank

    @pl.loop(0, cells_x // CHUNK, unroll=2)
    def _(q):
        at = pl.ds(q * CHUNK + 1, CHUNK)
        blank = jnp.zeros((CHUNK, 1, cells_y), jnp.float32)
        for ref in (wide, once):
            ref[at, pl.ds(MID - 1, 1), :] = blank
            ref[at, pl.ds(MID + cells_z, 1), :] = blank
        wide[at, pl.ds(MID, cells_z), :] = summed[pl.ds(q * CHUNK, CHUNK)]

    def relaxed(ref, x, factor):
        at = lambda dx, dz: ref[pl.ds(x + 1 + dx, CHUNK), pl.ds(MID + dz, cells_z), :]
        v = at(0, 0)
        near = at(1, 0) + at(-1, 0) + at(0, 1) + at(0, -1)
        flat = v.reshape(CHUNK * cells_z // 8, 8, cells_y)
        near = near + shifted_y(flat).reshape(v.shape)
        return v + factor * (near - 6.0 * v)

    @pl.loop(0, cells_x // CHUNK, unroll=2)
    def _(q):
        x = q * CHUNK
        factor = smooth[pl.ds(x, CHUNK)]
        once[pl.ds(x + 1, CHUNK), pl.ds(MID, cells_z), :] = relaxed(wide, x, factor)
        g = summed[pl.ds(x, CHUNK)]
        for i, k in enumerate((0, cells_z - 1)):
            own_g[i, pl.ds(x, CHUNK)] = g[:, k]
        for i, k in enumerate((0, 1, cells_z - 2, cells_z - 1)):
            own_s[i, pl.ds(x, CHUNK)] = factor[:, k]

    depth = lax.broadcasted_iota(jnp.int32, (1, cells_z, cells_y), 1)
    between = (depth >= 2) & (depth < cells_z - 2)

    def sweep(q, total):
        x = q * CHUNK
        value = relaxed(once, x, smooth[pl.ds(x, CHUNK)])
        out[pl.ds(x, CHUNK)] = value
        for i, k in enumerate((0, 1, cells_z - 2, cells_z - 1)):
            own_out[i, pl.ds(x, CHUNK)] = value[:, k]
        squares = jnp.where(between, value * value, 0.0)
        return total + jnp.sum(squares.reshape(CHUNK * cells_z // 8, 8, cells_y), axis=0)

    inner[...] = lax.fori_loop(
        0, cells_x // CHUNK, sweep, jnp.zeros((8, cells_y), jnp.float32), unroll=2
    )


def edge_kernel(
    smoothed_in, inner, own_g, own_s, own_out, low_sum, high_sum, low_one, high_one,
    smoothed, square, planes,
):
    cells_x, cells_z, cells_y = smoothed.shape
    smoothed[...] = smoothed_in[...]
    count = cells_x // 4
    blank = jnp.zeros((8, cells_y), jnp.float32)
    total = inner[...]
    for side, (sums, smooth, present) in enumerate(
        ((low_sum, low_one, has_sides()[0]), (high_sum, high_one, has_sides()[1]))
    ):
        for k in range(4):
            planes[k, pl.ds(0, 8)] = blank
            planes[k, pl.ds(8 + cells_x, 8)] = blank

        @pl.loop(0, count)
        def _(q, sums=sums, smooth=smooth, present=present):
            at = pl.ds(8 + 4 * q, 4)
            for k in range(2):
                planes[k, at] = jnp.where(present, sums[k * count + q], 0.0)
            planes[2, at] = jnp.where(present, smooth[cells_x + q], 0.0)

        def near(k):
            at = lambda dx: planes[k, pl.ds(8 + dx, cells_x)]
            return at(1) + at(-1) + shifted_y(at(0))

        whole = pl.ds(8, cells_x)
        first, second, factor = planes[0, whole], planes[1, whole], planes[2, whole]
        outside = first + factor * (near(0) + second + own_g[side] - 6.0 * first)
        edge, inside = (0, 1) if side == 0 else (3, 2)
        change = own_s[edge] * first
        planes[3, whole] = change
        value = own_out[edge] + change + own_s[edge] * (near(3) - 6.0 * change + outside)
        beside = own_out[inside] + own_s[inside] * change
        squares = value * value + beside * beside
        total = total + jnp.sum(squares.reshape(cells_x // 8, 8, cells_y), axis=0)
        planes[0, whole] = value
        planes[1, whole] = beside
        rows = (0, 1) if side == 0 else (cells_z - 1, cells_z - 2)

        @pl.loop(0, count)
        def _(q, rows=rows):
            for k, z in enumerate(rows):
                smoothed[pl.ds(4 * q, 4), pl.ds(z, 1), :] = planes[k, pl.ds(8 + 4 * q, 4)][:, None]

    row = jnp.sum(total, axis=0, keepdims=True)
    square[...] = jnp.broadcast_to(row[None], square.shape)


def third_kernel(u_two, side, model, aniso_c, low, high, change, pad, first_z, dep):
    cells_x = change.shape[0]
    fill_depth(pad, lambda at: u_two[at], lambda at: low[at], lambda at: high[at])
    depth_pass(pad, first_z, dep)

    @pl.loop(0, cells_x // CHUNK, unroll=2)
    def _(step):
        x = step * CHUNK
        at = pl.ds(x, CHUNK)
        change[at] = model[at] * (side[at] + dep[at] + aniso_c[at] * crossing(first_z, x))


def shifted_y(flat):
    cells_y = flat.shape[-1]
    lane = lax.broadcasted_iota(jnp.int32, (1,) * (flat.ndim - 2) + (8, cells_y), flat.ndim - 1)
    axis = flat.ndim - 1
    if flat.ndim == 2:
        lane = lax.broadcasted_iota(jnp.int32, flat.shape, 1)
    right = jnp.where(lane < cells_y - 1, pltpu.roll(flat, cells_y - 1, axis), 0.0)
    left = jnp.where(lane >= 1, pltpu.roll(flat, 1, axis), 0.0)
    return right + left


def relax_kernel(summed, smooth, out, inner, own_g, own_s, own_out, wide, once):
    cells_x, cells_z, cells_y = summed.shape
    for ref in (wide, once):
        blank = jnp.zeros((1, *ref.shape[1:]), jnp.float32)
        ref[pl.ds(0, 1)] = blank
        ref[pl.ds(cells_x + 1, 1)] = blank

    @pl.loop(0, cells_x // CHUNK, unroll=2)
    def _(q):
        at = pl.ds(q * CHUNK + 1, CHUNK)
        blank = jnp.zeros((CHUNK, 1, cells_y), jnp.float32)
        for ref in (wide, once):
            ref[at, pl.ds(MID - 1, 1), :] = blank
            ref[at, pl.ds(MID + cells_z, 1), :] = blank
        wide[at, pl.ds(MID, cells_z), :] = summed[pl.ds(q * CHUNK, CHUNK)]

    def relaxed(ref, x, factor):
        at = lambda dx, dz: ref[pl.ds(x + 1 + dx, CHUNK), pl.ds(MID + dz, cells_z), :]
        v = at(0, 0)
        near = at(1, 0) + at(-1, 0) + at(0, 1) + at(0, -1)
        flat = v.reshape(CHUNK * cells_z // 8, 8, cells_y)
        near = near + shifted_y(flat).reshape(v.shape)
        return v + factor * (near - 6.0 * v)

    @pl.loop(0, cells_x // CHUNK, unroll=2)
    def _(q):
        x = q * CHUNK
        factor = smooth[pl.ds(x, CHUNK)]
        once[pl.ds(x + 1, CHUNK), pl.ds(MID, cells_z), :] = relaxed(wide, x, factor)
        g = summed[pl.ds(x, CHUNK)]
        for i, k in enumerate((0, cells_z - 1)):
            own_g[i, pl.ds(x, CHUNK)] = g[:, k]
        for i, k in enumerate((0, 1, cells_z - 2, cells_z - 1)):
            own_s[i, pl.ds(x, CHUNK)] = factor[:, k]

    depth = lax.broadcasted_iota(jnp.int32, (1, cells_z, cells_y), 1)
    between = (depth >= 2) & (depth < cells_z - 2)

    def sweep(q, total):
        x = q * CHUNK
        value = relaxed(once, x, smooth[pl.ds(x, CHUNK)])
        out[pl.ds(x, CHUNK)] = value
        for i, k in enumerate((0, 1, cells_z - 2, cells_z - 1)):
            own_out[i, pl.ds(x, CHUNK)] = value[:, k]
        squares = jnp.where(between, value * value, 0.0)
        return total + jnp.sum(squares.reshape(CHUNK * cells_z // 8, 8, cells_y), axis=0)

    inner[...] = lax.fori_loop(
        0, cells_x // CHUNK, sweep, jnp.zeros((8, cells_y), jnp.float32), unroll=2
    )


def edge_kernel(
    smoothed_in, inner, own_g, own_s, own_out, low_sum, high_sum, low_one, high_one,
    smoothed, square, planes,
):
    cells_x, cells_z, cells_y = smoothed.shape
    smoothed[...] = smoothed_in[...]
    count = cells_x // 4
    blank = jnp.zeros((8, cells_y), jnp.float32)
    total = inner[...]
    for side, (sums, smooth, present) in enumerate(
        ((low_sum, low_one, has_sides()[0]), (high_sum, high_one, has_sides()[1]))
    ):
        for k in range(4):
            planes[k, pl.ds(0, 8)] = blank
            planes[k, pl.ds(8 + cells_x, 8)] = blank

        @pl.loop(0, count)
        def _(q, sums=sums, smooth=smooth, present=present):
            at = pl.ds(8 + 4 * q, 4)
            for k in range(2):
                planes[k, at] = jnp.where(present, sums[k * count + q], 0.0)
            planes[2, at] = jnp.where(present, smooth[cells_x + q], 0.0)

        def near(k):
            at = lambda dx: planes[k, pl.ds(8 + dx, cells_x)]
            return at(1) + at(-1) + shifted_y(at(0))

        whole = pl.ds(8, cells_x)
        first, second, factor = planes[0, whole], planes[1, whole], planes[2, whole]
        outside = first + factor * (near(0) + second + own_g[side] - 6.0 * first)
        edge, inside = (0, 1) if side == 0 else (3, 2)
        change = own_s[edge] * first
        planes[3, whole] = change
        value = own_out[edge] + change + own_s[edge] * (near(3) - 6.0 * change + outside)
        beside = own_out[inside] + own_s[inside] * change
        squares = value * value + beside * beside
        total = total + jnp.sum(squares.reshape(cells_x // 8, 8, cells_y), axis=0)
        planes[0, whole] = value
        planes[1, whole] = beside
        rows = (0, 1) if side == 0 else (cells_z - 1, cells_z - 2)

        @pl.loop(0, count)
        def _(q, rows=rows):
            for k, z in enumerate(rows):
                smoothed[pl.ds(4 * q, 4), pl.ds(z, 1), :] = planes[k, pl.ds(8 + 4 * q, 4)][:, None]

    row = jnp.sum(total, axis=0, keepdims=True)
    square[...] = jnp.broadcast_to(row[None], square.shape)


def third_kernel(u_two, side, model, aniso_c, low, high, change, pad, first_z, dep):
    cells_x = change.shape[0]
    fill_depth(pad, lambda at: u_two[at], lambda at: low[at], lambda at: high[at])
    depth_pass(pad, first_z, dep)

    @pl.loop(0, cells_x // CHUNK, unroll=2)
    def _(step):
        x = step * CHUNK
        at = pl.ds(x, CHUNK)
        change[at] = model[at] * (side[at] + dep[at] + aniso_c[at] * crossing(first_z, x))


def close_kernel(squares, smoothed, model, base, change, model_next, grad_dir, wave_next):
    cells_x, cells_z, cells_y = smoothed.shape
    rows = grad_dir.shape[0]
    total = jnp.sum(jnp.sum(squares[...], axis=0), axis=1, keepdims=True)
    cells = cells_x * depth_range(cells_z)[1] * cells_y
    scale = lax.rsqrt(total / cells + 1e-06)
    scale = jnp.broadcast_to(scale, (8, cells_y))[None]

    def factor(value):
        flat = value.reshape(value.shape[0] * cells_z // 8, 8, cells_y) * scale
        return flat.reshape(value.shape)

    @pl.loop(0, cells_x // CHUNK)
    def _(step):
        at = pl.ds(step * CHUNK, CHUNK)
        shrink = 1.0 - 0.25 * jnp.tanh(factor(smoothed[at]))
        wave_next[0, at] = base[at] + change[at] * shrink

    _, core, chip = position()
    at = pl.ds((2 * chip + core) * rows, rows)
    direction = factor(smoothed[at])
    grad_dir[...] = direction
    model_next[...] = model[at] * (1.0 - 0.25 * jnp.tanh(direction))


def shift(low_edge, high_edge):
    count = lax.axis_size(DEPTH)
    forward = [(i, (i + 1) % count) for i in range(count)]
    backward = [(target, source) for source, target in forward]
    return lax.ppermute(high_edge, DEPTH, forward), lax.ppermute(low_edge, DEPTH, backward)


def body(
    u_prev,
    u_cur,
    a_prev,
    a_cur,
    model,
    aniso_h,
    aniso_c,
    smooth_coef,
    bin_onehot,
    shot_group,
    src_cell,
    rec_cell,
    src_wave,
    rec_data,
):
    _, cells_x, cells_z, cells_y = u_cur.shape
    rows = model.shape[0]
    peers = lax.axis_size(PEERS)
    slab = f32(cells_x, cells_z, cells_y)
    scratch = lambda *shape: pltpu.VMEM(shape, jnp.float32)
    pad = scratch(cells_x, cells_z + 2 * MID, cells_y)
    first_z = scratch(cells_x + 2 * REACH, cells_z, cells_y)
    padded_rows = first_z
    dep = scratch(cells_x, cells_z, cells_y)
    pair = scratch(2, cells_x, cells_z, cells_y)
    work = 80 * cells_x * cells_z * cells_y

    spread = call(
        spread_kernel,
        (model, aniso_h, aniso_c, smooth_coef),
        0,
        f32(peers, 4, rows, cells_z, cells_y),
        (
            scratch(4, rows, cells_z, cells_y),
            pltpu.SemaphoreType.DMA((4,)),
            pltpu.SemaphoreType.DMA((peers,)),
        ),
        hbm_in=range(4),
        hbm_out=(0,),
        grant=62,
    )
    mine = lax.all_to_all(spread, PEERS, 0, 0, tiled=True)

    edges = lambda start: jnp.concatenate(
        [lax.slice_in_dim(v, start, start + REACH, axis=2) for v in (u_cur, a_cur)]
    )
    low, high = shift(edges(0), edges(cells_z - REACH))
    *parts, weight = call(
        open_kernel,
        (src_cell, src_wave, bin_onehot, shot_group, rec_cell, rec_data)
        + (u_prev, u_cur, a_prev, a_cur, low, high),
        4,
        (slab,) * 8 + (f32(1, cells_z, cells_y),),
        (pair,) * 6
        + (scratch(1, cells_z, cells_y), padded_rows, pad, first_z)
        + (pltpu.SemaphoreType.DMA((2, 2)), pltpu.SemaphoreType.DMA((9,))),
        2 * work,
        hbm_in=range(6, 10),
        hbm_out=range(9),
        grant=61,
    )
    other = lax.ppermute(mine, "core", SWAP)
    *parts, weight, adjoint = call(
        fetch_kernel,
        (*parts, weight, a_cur),
        0,
        (slab,) * 8 + (f32(1, cells_z, cells_y), f32(*a_cur.shape)),
        (pltpu.SemaphoreType.DMA((10,)),),
        hbm_in=range(10),
        grant=49,
    )
    payload = f32(cells_x + peers, REACH, cells_y)
    u_one, a_one, grad, model_slab, h_slab, c_slab, smooth_slab, low_edge, high_edge = call(
        first_kernel,
        (mine, other, adjoint, *parts),
        0,
        (slab,) * 7 + (payload, payload),
        (),
        20 * slab.size,
    )
    low_one, high_one = shift(low_edge, high_edge)
    base, side = call(
        functools.partial(side_kernel, 1),
        (src_cell, src_wave, u_one, u_cur[0], h_slab),
        2,
        (slab, slab),
        (padded_rows,),
        work // 2,
    )
    split = f32(peers, rows, cells_z, cells_y)
    edge = f32(cells_x, REACH, cells_y)
    u_two, keep, send = call(
        second_kernel,
        (u_one, base, side, a_one, grad, weight, model_slab, c_slab, low_one, high_one),
        0,
        (slab, split, split),
        (pad, first_z, dep),
        work,
    )
    chip_sum = keep + lax.ppermute(send, "core", SWAP)
    shares = lax.all_to_all(chip_sum, PEERS, 0, 0, tiled=True)
    total = call(sum_kernel, (shares,), 0, split)
    mine = lax.all_to_all(total, PEERS, 0, 0, tiled=True)
    other = lax.ppermute(mine, "core", SWAP)
    low_edge, high_edge = call(rim_kernel, (u_two,), 0, (edge, edge))
    low_two, high_two = shift(low_edge, high_edge)
    payload = f32(2 * peers, 4, cells_y)
    summed, low_edge, high_edge = call(
        join_kernel, (mine, other), 0, (slab, payload, payload)
    )
    low_sum, high_sum = shift(low_edge, high_edge)
    base, side, low_two, high_two = call(
        functools.partial(side_halo_kernel, 2),
        (src_cell, src_wave, u_two, u_one, h_slab, low_two, high_two),
        2,
        (slab, slab, edge, edge),
        (padded_rows, pltpu.SemaphoreType.DMA((2,))),
        work // 2,
        hbm_in=(5, 6),
    )
    edges = f32(4, cells_x, cells_y)
    smoothed, inner, own_g, own_s, own_out = call(
        relax_kernel,
        (summed, smooth_slab),
        0,
        (slab, f32(8, cells_y), f32(2, cells_x, cells_y), edges, edges),
        (scratch(cells_x + 2, cells_z + 2 * MID, cells_y),) * 2,
        40 * slab.size,
    )
    change = call(
        third_kernel,
        (u_two, side, model_slab, c_slab, low_two, high_two),
        0,
        slab,
        (pad, first_z, dep),
        work,
    )
    smoothed, square = call(
        edge_kernel,
        (smoothed, inner, own_g, own_s, own_out, low_sum, high_sum, low_one, high_one),
        0,
        (slab, f32(lax.axis_size(DEPTH), 1, cells_y)),
        (scratch(4, cells_x + 16, cells_y),),
        4 * slab.size,
    )
    squares = lax.all_to_all(square, DEPTH, 0, 0, tiled=True)
    share = f32(rows, cells_z, cells_y)
    return call(
        close_kernel,
        (squares, smoothed, model_slab, base, change),
        0,
        (share, share, f32(1, cells_x, cells_z, cells_y)),
        (),
        20 * slab.size,
    )


def solution(mesh):
    mesh = jax.sharding.Mesh(
        mesh.devices.reshape(2, 8, 2, 2, 4), ("xh", "z", "core", "xl", "y")
    )
    return jax.shard_map(
        body,
        mesh=mesh,
        in_specs=(
            P(SHOT, None, DEPTH, None),
            P(SHOT, None, DEPTH, None),
            P(SHOT, None, DEPTH, None),
            P(SHOT, None, DEPTH, None),
            P(SHOT, DEPTH, None),
            P(SHOT, DEPTH, None),
            P(SHOT, DEPTH, None),
            P(SHOT, DEPTH, None),
            P(None, DEPTH, None),
            P(SHOT),
            P(SHOT),
            P(SHOT, None),
            P(SHOT, None),
            P(SHOT, None, None),
        ),
        out_specs=(
            P(SHOT, DEPTH, None),
            P(SHOT, DEPTH, None),
            P(SHOT, None, DEPTH, None),
        ),
        check_vma=False,
    )
```

```python
import jax
import jax.numpy as jnp
from jax import lax
from jax.experimental import pallas as pl
from jax.experimental.pallas import tpu as pltpu
from jax.sharding import PartitionSpec as P


second_coef = (-205.0 / 72.0, 8.0 / 5.0, -1.0 / 5.0, 8.0 / 315.0, -1.0 / 560.0)
first_coef = (0.8, -0.2, 4.0 / 105.0, -1.0 / 280.0)

SHOT = ("xh", "z", "core")
DEPTH = ("xl", "y")
PEERS = ("xh", "z")
SWAP = [(0, 1), (1, 0)]
REACH = 4
MID = 8
CHUNK = 4
BLOCK = 16
VMEM = pl.BlockSpec(memory_space=pltpu.VMEM)
SMEM = pl.BlockSpec(memory_space=pltpu.SMEM)
HBM = pl.BlockSpec(memory_space=pltpu.HBM)


def f32(*shape):
    return jax.ShapeDtypeStruct(shape, jnp.float32)


def call(kernel, args, smem, outs, scratch=(), flops=0, hbm_in=(), hbm_out=(), grant=16):
    bytes_accessed = 4 * sum(a.size for a in args)
    spec = lambda i: SMEM if i < smem else HBM if i in hbm_in else VMEM
    single = not isinstance(outs, tuple)
    out_specs = [HBM if i in hbm_out else VMEM for i in range(1 if single else len(outs))]
    return pl.pallas_call(
        kernel,
        out_shape=outs,
        in_specs=[spec(i) for i in range(len(args))],
        out_specs=out_specs[0] if single else tuple(out_specs),
        scratch_shapes=list(scratch),
        cost_estimate=pl.CostEstimate(
            flops=flops, bytes_accessed=bytes_accessed, transcendentals=0
        ),
        compiler_params=pltpu.CompilerParams(vmem_limit_bytes=grant * 2**20),
    )(*args)


def position():
    layer = lax.axis_index("xl") * lax.axis_size("y") + lax.axis_index("y")
    chip = lax.axis_index("xh") * lax.axis_size("z") + lax.axis_index("z")
    return layer, lax.axis_index("core"), chip


def fill_rows(rows, read):
    cells_x = rows.shape[0] - 2 * REACH
    zeros = jnp.zeros((REACH, *rows.shape[1:]), jnp.float32)
    rows[pl.ds(0, REACH)] = zeros
    rows[pl.ds(REACH + cells_x, REACH)] = zeros

    @pl.loop(0, cells_x // CHUNK)
    def _(step):
        x = step * CHUNK
        rows[pl.ds(REACH + x, CHUNK)] = read(pl.ds(x, CHUNK))


def has_sides():
    layer, _, _ = position()
    return layer > 0, layer < lax.axis_size("xl") * lax.axis_size("y") - 1


def depth_range(cells_z):
    layer, _, _ = position()
    return layer * cells_z, cells_z * lax.axis_size("xl") * lax.axis_size("y")


def fill_depth(pad, read, low, high):
    cells_x, cells_z = pad.shape[0], pad.shape[1] - 2 * MID
    below, above = has_sides()

    @pl.loop(0, cells_x // CHUNK, unroll=2)
    def _(step):
        at = pl.ds(step * CHUNK, CHUNK)
        pad[at, pl.ds(MID, cells_z), :] = read(at)
        pad[at, pl.ds(MID - REACH, REACH), :] = jnp.where(below, low(at), 0.0)
        pad[at, pl.ds(MID + cells_z, REACH), :] = jnp.where(above, high(at), 0.0)


def depth_pass(pad, first_z, second_z):
    cells_x, cells_z = second_z.shape[0], second_z.shape[1]
    zeros = jnp.zeros((REACH, *first_z.shape[1:]), jnp.float32)
    first_z[pl.ds(0, REACH)] = zeros
    first_z[pl.ds(REACH + cells_x, REACH)] = zeros

    @pl.loop(0, cells_x // CHUNK, unroll=2)
    def _(step):
        x = step * CHUNK
        at = lambda k: pad[pl.ds(x, CHUNK), pl.ds(MID + k, cells_z), :]
        two = second_coef[0] * at(0)
        one = None
        for k in range(1, 5):
            above, below = at(k), at(-k)
            two = two + second_coef[k] * (above + below)
            term = first_coef[k - 1] * (above - below)
            one = term if one is None else one + term
        second_z[pl.ds(x, CHUNK)] = two
        first_z[pl.ds(REACH + x, CHUNK)] = one


def lateral_masks(cells_y):
    lane = lax.broadcasted_iota(jnp.int32, (1, 8, cells_y), 2)
    up = [jnp.where(lane < cells_y - k, second_coef[k], 0.0) for k in range(1, 5)]
    down = [jnp.where(lane >= k, second_coef[k], 0.0) for k in range(1, 5)]
    return up, down


def lateral(rows, x, masks):
    up, down = masks
    at = lambda k: rows[pl.ds(REACH + x + k, CHUNK)]
    v = at(0)
    cells_z, cells_y = v.shape[1:]
    total = (2.0 * second_coef[0]) * v
    for k in range(1, 5):
        total = total + second_coef[k] * (at(k) + at(-k))
    flat = v.reshape(CHUNK * cells_z // 8, 8, cells_y)
    along_y = None
    for k in range(1, 5):
        term = up[k - 1] * pltpu.roll(flat, cells_y - k, 2) + down[k - 1] * pltpu.roll(flat, k, 2)
        along_y = term if along_y is None else along_y + term
    return total + along_y.reshape(v.shape)


def crossing(first_z, x):
    at = lambda k: first_z[pl.ds(REACH + x + k, CHUNK)]
    total = None
    for k in range(1, 5):
        term = first_coef[k - 1] * (at(k) - at(-k))
        total = term if total is None else total + term
    return total


def add_at(ref, cell, amount):
    cells_z, cells_y = ref.shape[1], ref.shape[2]
    z_start, depth_cells = depth_range(cells_z)
    row = cell // cells_y
    x, z = row // depth_cells, row % depth_cells - z_start

    @pl.when((z >= 0) & (z < cells_z))
    def _():
        lane = lax.broadcasted_iota(jnp.int32, (1, 1, cells_y), 2)
        at = (pl.ds(x, 1), pl.ds(z, 1), slice(None))
        ref[at] = ref[at] + jnp.where(lane == cell % cells_y, amount, 0.0)


def spread_kernel(model, aniso_h, aniso_c, smooth, out, own, sem_in, sem_out):
    arrays = (model, aniso_h, aniso_c, smooth)
    loads = [pltpu.make_async_copy(ref, own.at[j], sem_in.at[j]) for j, ref in enumerate(arrays)]
    for load in loads:
        load.start()
    for load in loads:
        load.wait()
    sends = [pltpu.make_async_copy(own, out.at[p], sem_out.at[p]) for p in range(out.shape[0])]
    for send in sends:
        send.start()
    for send in sends:
        send.wait()


def place_receivers(out, rec_cell, rec_data):
    cells_x, cells_z, cells_y = out.shape
    z_start, depth_cells = depth_range(cells_z)
    cell = rec_cell[...]
    row = cell // cells_y
    z = row % depth_cells - z_start
    key = jnp.where((z >= 0) & (z < cells_z), row // depth_cells * cells_z + z, -1)
    y = cell % cells_y
    count = cell.shape[1]
    lanes = jnp.where(
        lax.broadcasted_iota(jnp.int32, (cells_y, count), 0) == y, 1.0, 0.0
    ).astype(jnp.bfloat16)
    rest, terms = rec_data[0, pl.ds(0, 1), :], []
    for _ in range(3):
        term = rest.astype(jnp.bfloat16).astype(jnp.float32)
        terms.append(term)
        rest = rest - term
    block = min(16, cells_x)

    @pl.loop(0, cells_x // block)
    def _(step):
        first = step * block * cells_z
        index = first + lax.broadcasted_iota(jnp.int32, (block * cells_z, count), 0)
        hit = index == key
        total = None
        for term in terms:
            left = jnp.where(hit, term, 0.0).astype(jnp.bfloat16)
            part = lax.dot_general(
                left, lanes, (((1,), (1,)), ((), ())), preferred_element_type=jnp.float32
            )
            total = part if total is None else total + part
        at = pl.ds(step * block, block)
        out[at] = out[at] + total.reshape(block, cells_z, cells_y)


def open_kernel(
    src_cell, src_wave, onehot, shot_group, rec_cell, rec_data,
    u_prev, u_cur, a_prev, a_cur, low, high,
    base_u, lat_u, dep_u, cross_u, base_a, lat_a, dep_a, cross_a, weight,
    old, now, base, lat, dep, cross, scale_row, rows, pad, first_z, sem_in, sem_out,
):
    cells_x, cells_z, cells_y = lat_u.shape
    masks = lateral_masks(cells_y)
    loads = []
    for j, (before, current) in enumerate(((u_prev, u_cur), (a_prev, a_cur))):
        loads.append(pltpu.make_async_copy(current.at[0], now.at[j], sem_in.at[j, 0]))
        loads.append(pltpu.make_async_copy(before.at[0], old.at[j], sem_in.at[j, 1]))
    for load in loads:
        load.start()
    sends = []

    def send(source, target):
        copy = pltpu.make_async_copy(source, target, sem_out.at[len(sends)])
        copy.start()
        sends.append(copy)

    blocks = onehot.shape[1]
    depth = lax.broadcasted_iota(jnp.int32, weight.shape, 1)
    value = jnp.zeros(weight.shape, jnp.float32)
    for block in range(blocks):
        scale = sum(
            onehot[shot_group[0], block, b].astype(jnp.float32) * 2.0 ** (-b)
            for b in range(onehot.shape[2])
        )
        value = jnp.where(depth // (cells_z // blocks) == block, scale, value)
    scale_row[...] = value
    send(scale_row, weight)

    targets = ((base_u, lat_u, dep_u, cross_u), (base_a, lat_a, dep_a, cross_a))
    for j in range(2):
        loads[2 * j].wait()
        loads[2 * j + 1].wait()
        fill_depth(
            pad,
            lambda at, j=j: now[j, at],
            lambda at, j=j: low[j, at],
            lambda at, j=j: high[j, at],
        )
        depth_pass(pad, first_z, dep.at[j])
        send(dep.at[j], targets[j][2])
        fill_rows(rows, lambda at, j=j: now[j, at])

        @pl.loop(0, cells_x // CHUNK)
        def _(step, j=j):
            x = step * CHUNK
            at = pl.ds(x, CHUNK)
            lat[j, at] = lateral(rows, x, masks)
            cross[j, at] = crossing(first_z, x)
            base[j, at] = 2.0 * now[j, at] - old[j, at]

        send(lat.at[j], targets[j][1])
        send(cross.at[j], targets[j][3])
        if j == 0:
            add_at(base.at[0], src_cell[0], src_wave[0, 0])
        else:
            place_receivers(base.at[1], rec_cell, rec_data)
        send(base.at[j], targets[j][0])
    for copy in sends:
        copy.wait()


def fetch_kernel(*refs):
    count = (len(refs) - 1) // 2
    sources, targets, sem = refs[:count], refs[count:-1], refs[-1]
    copies = [
        pltpu.make_async_copy(source, target, sem.at[i])
        for i, (source, target) in enumerate(zip(sources, targets))
    ]
    for copy in copies:
        copy.start()
    for copy in copies:
        copy.wait()


def first_kernel(
    mine, other, a_cur,
    base_u, lat_u, dep_u, cross_u, base_a, lat_a, dep_a, cross_a,
    u_one, a_one, grad, model, aniso_h, aniso_c, smooth, low, high,
):
    cells_x, cells_z, _ = u_one.shape
    own = position()[1] == 0

    @pl.loop(0, mine.shape[0])
    def _(q):
        for p in range(2):
            rows = pl.ds(q * 4 + p * 2, 2)
            pick = lambda j: jnp.where(own == (p == 0), mine[q, j], other[q, j])
            m, h, c, s = pick(0), pick(1), pick(2), pick(3)
            model[rows], aniso_h[rows], aniso_c[rows], smooth[rows] = m, h, c, s
            k_u = h * lat_u[rows] + dep_u[rows] + c * cross_u[rows]
            k_a = h * lat_a[rows] + dep_a[rows] + c * cross_a[rows]
            grad[rows] = a_cur[0, rows] * k_u
            new = base_u[rows] + m * k_u
            u_one[rows] = new
            a_one[rows] = base_a[rows] + m * k_a
            low[rows] = new[:, :REACH]
            high[rows] = new[:, cells_z - REACH :]
            edge = (pl.ds(cells_x + q, 1), pl.ds(2 * p, 2), slice(None))
            low[edge] = s[:, 0][None]
            high[edge] = s[:, cells_z - 1][None]


def band(cells_y):
    apart = lax.broadcasted_iota(jnp.int32, (cells_y, cells_y), 0)
    apart = apart - lax.broadcasted_iota(jnp.int32, (cells_y, cells_y), 1)
    value = jnp.zeros((cells_y, cells_y), jnp.float32)
    for k in range(1, 5):
        value = jnp.where(jnp.abs(apart) == k, second_coef[k], value)
    return value


def side_part(now, aniso_h, side, rows, also=None):
    cells_x, cells_z, cells_y = now.shape
    matrix = band(cells_y)
    fill_rows(rows, lambda at: now[at])
    block = min(BLOCK, cells_x)

    @pl.loop(0, cells_x // block)
    def _(step):
        x = step * block
        at = pl.ds(x, block)
        v = now[at]
        flat = v.reshape(block * cells_z, cells_y)
        along_y = jnp.dot(
            flat, matrix, precision=lax.Precision.HIGHEST, preferred_element_type=jnp.float32
        )
        total = (2.0 * second_coef[0]) * v + along_y.reshape(v.shape)
        for k in range(1, 5):
            total = total + second_coef[k] * (
                rows[pl.ds(REACH + x + k, block)] + rows[pl.ds(REACH + x - k, block)]
            )
        side[at] = aniso_h[at] * total
        if also is not None:
            also(at, v)


def side_one_kernel(src_cell, src_wave, now, old, aniso_h, base, side, carry, rows):
    def also(at, v):
        base[at] = 2.0 * v - old[at]
        carry[at] = -v

    side_part(now, aniso_h, side, rows, also)
    add_at(base, src_cell[0], src_wave[0, 1])
    add_at(carry, src_cell[0], src_wave[0, 2])


def side_two_kernel(now, aniso_h, low, high, side, low_in, high_in, rows, sem):
    copies = [
        pltpu.make_async_copy(low, low_in, sem.at[0]),
        pltpu.make_async_copy(high, high_in, sem.at[1]),
    ]
    for copy in copies:
        copy.start()
    side_part(now, aniso_h, side, rows)
    for copy in copies:
        copy.wait()


def second_kernel(
    u_one, base, side, a_one, grad, weight, model, aniso_c, low, high,
    u_two, keep, send, pad, first_z, dep,
):
    cells_x = u_two.shape[0]
    fill_depth(pad, lambda at: u_one[at], lambda at: low[at], lambda at: high[at])
    depth_pass(pad, first_z, dep)
    own = position()[1] == 0

    @pl.loop(0, cells_x // CHUNK, unroll=2)
    def _(step):
        x = step * CHUNK
        at = pl.ds(x, CHUNK)
        k_u = side[at] + dep[at] + aniso_c[at] * crossing(first_z, x)
        u_two[at] = base[at] + model[at] * k_u
        total = weight[...] * (grad[at] + a_one[at] * k_u)
        keep[step] = jnp.where(own, total[:2], total[2:])
        send[step] = jnp.where(own, total[2:], total[:2])


def rim_kernel(field, low, high):
    cells_x, cells_z, _ = field.shape

    @pl.loop(0, cells_x // CHUNK, unroll=2)
    def _(step):
        at = pl.ds(step * CHUNK, CHUNK)
        low[at] = field[at, :REACH]
        high[at] = field[at, cells_z - REACH :]


def sum_kernel(parts, out):
    total = parts[0]
    for peer in range(1, parts.shape[0]):
        total = total + parts[peer]
    for peer in range(parts.shape[0]):
        out[peer] = total


def join_kernel(mine, other, summed, low, high):
    cells_z = summed.shape[1]
    count = mine.shape[0]
    own = position()[1] == 0

    @pl.loop(0, count)
    def _(q):
        for p in range(2):
            rows = pl.ds(q * 4 + p * 2, 2)
            g = jnp.where(own == (p == 0), mine[q], other[q])
            summed[rows] = g
            for k in range(2):
                edge = (pl.ds(k * count + q, 1), pl.ds(2 * p, 2), slice(None))
                low[edge] = g[:, k][None]
                high[edge] = g[:, cells_z - 1 - k][None]


def shifted_y(flat):
    cells_y = flat.shape[-1]
    lane = lax.broadcasted_iota(jnp.int32, (1,) * (flat.ndim - 2) + (8, cells_y), flat.ndim - 1)
    axis = flat.ndim - 1
    if flat.ndim == 2:
        lane = lax.broadcasted_iota(jnp.int32, flat.shape, 1)
    right = jnp.where(lane < cells_y - 1, pltpu.roll(flat, cells_y - 1, axis), 0.0)
    left = jnp.where(lane >= 1, pltpu.roll(flat, 1, axis), 0.0)
    return right + left


def relax_kernel(summed, smooth, out, inner, own_g, own_s, own_out, wide, once):
    cells_x, cells_z, cells_y = summed.shape
    for ref in (wide, once):
        blank = jnp.zeros((1, *ref.shape[1:]), jnp.float32)
        ref[pl.ds(0, 1)] = blank
        ref[pl.ds(cells_x + 1, 1)] = blank

    @pl.loop(0, cells_x // CHUNK, unroll=2)
    def _(q):
        at = pl.ds(q * CHUNK + 1, CHUNK)
        blank = jnp.zeros((CHUNK, 1, cells_y), jnp.float32)
        for ref in (wide, once):
            ref[at, pl.ds(MID - 1, 1), :] = blank
            ref[at, pl.ds(MID + cells_z, 1), :] = blank
        wide[at, pl.ds(MID, cells_z), :] = summed[pl.ds(q * CHUNK, CHUNK)]

    def relaxed(ref, x, factor):
        at = lambda dx, dz: ref[pl.ds(x + 1 + dx, CHUNK), pl.ds(MID + dz, cells_z), :]
        v = at(0, 0)
        near = at(1, 0) + at(-1, 0) + at(0, 1) + at(0, -1)
        flat = v.reshape(CHUNK * cells_z // 8, 8, cells_y)
        near = near + shifted_y(flat).reshape(v.shape)
        return v + factor * (near - 6.0 * v)

    @pl.loop(0, cells_x // CHUNK, unroll=2)
    def _(q):
        x = q * CHUNK
        factor = smooth[pl.ds(x, CHUNK)]
        once[pl.ds(x + 1, CHUNK), pl.ds(MID, cells_z), :] = relaxed(wide, x, factor)
        g = summed[pl.ds(x, CHUNK)]
        for i, k in enumerate((0, cells_z - 1)):
            own_g[i, pl.ds(x, CHUNK)] = g[:, k]
        for i, k in enumerate((0, 1, cells_z - 2, cells_z - 1)):
            own_s[i, pl.ds(x, CHUNK)] = factor[:, k]

    depth = lax.broadcasted_iota(jnp.int32, (1, cells_z, cells_y), 1)
    between = (depth >= 2) & (depth < cells_z - 2)

    def sweep(q, total):
        x = q * CHUNK
        value = relaxed(once, x, smooth[pl.ds(x, CHUNK)])
        out[pl.ds(x, CHUNK)] = value
        for i, k in enumerate((0, 1, cells_z - 2, cells_z - 1)):
            own_out[i, pl.ds(x, CHUNK)] = value[:, k]
        squares = jnp.where(between, value * value, 0.0)
        return total + jnp.sum(squares.reshape(CHUNK * cells_z // 8, 8, cells_y), axis=0)

    inner[...] = lax.fori_loop(
        0, cells_x // CHUNK, sweep, jnp.zeros((8, cells_y), jnp.float32), unroll=2
    )


def edge_kernel(
    smoothed_in, inner, own_g, own_s, own_out, low_sum, high_sum, low_one, high_one,
    smoothed, square, planes,
):
    cells_x, cells_z, cells_y = smoothed.shape
    smoothed[...] = smoothed_in[...]
    count = cells_x // 4
    blank = jnp.zeros((8, cells_y), jnp.float32)
    total = inner[...]
    for side, (sums, smooth, present) in enumerate(
        ((low_sum, low_one, has_sides()[0]), (high_sum, high_one, has_sides()[1]))
    ):
        for k in range(4):
            planes[k, pl.ds(0, 8)] = blank
            planes[k, pl.ds(8 + cells_x, 8)] = blank

        @pl.loop(0, count)
        def _(q, sums=sums, smooth=smooth, present=present):
            at = pl.ds(8 + 4 * q, 4)
            for k in range(2):
                planes[k, at] = jnp.where(present, sums[k * count + q], 0.0)
            planes[2, at] = jnp.where(present, smooth[cells_x + q], 0.0)

        def near(k):
            at = lambda dx: planes[k, pl.ds(8 + dx, cells_x)]
            return at(1) + at(-1) + shifted_y(at(0))

        whole = pl.ds(8, cells_x)
        first, second, factor = planes[0, whole], planes[1, whole], planes[2, whole]
        outside = first + factor * (near(0) + second + own_g[side] - 6.0 * first)
        edge, inside = (0, 1) if side == 0 else (3, 2)
        change = own_s[edge] * first
        planes[3, whole] = change
        value = own_out[edge] + change + own_s[edge] * (near(3) - 6.0 * change + outside)
        beside = own_out[inside] + own_s[inside] * change
        squares = value * value + beside * beside
        total = total + jnp.sum(squares.reshape(cells_x // 8, 8, cells_y), axis=0)
        planes[0, whole] = value
        planes[1, whole] = beside
        rows = (0, 1) if side == 0 else (cells_z - 1, cells_z - 2)

        @pl.loop(0, count)
        def _(q, rows=rows):
            for k, z in enumerate(rows):
                smoothed[pl.ds(4 * q, 4), pl.ds(z, 1), :] = planes[k, pl.ds(8 + 4 * q, 4)][:, None]

    row = jnp.sum(total, axis=0, keepdims=True)
    square[...] = jnp.broadcast_to(row[None], square.shape)


def third_kernel(u_two, side, model, aniso_c, low, high, change, pad, first_z, dep):
    cells_x = change.shape[0]
    fill_depth(pad, lambda at: u_two[at], lambda at: low[at], lambda at: high[at])
    depth_pass(pad, first_z, dep)

    @pl.loop(0, cells_x // CHUNK, unroll=2)
    def _(step):
        x = step * CHUNK
        at = pl.ds(x, CHUNK)
        change[at] = model[at] * (side[at] + dep[at] + aniso_c[at] * crossing(first_z, x))


def shifted_y(flat):
    cells_y = flat.shape[-1]
    lane = lax.broadcasted_iota(jnp.int32, (1,) * (flat.ndim - 2) + (8, cells_y), flat.ndim - 1)
    axis = flat.ndim - 1
    if flat.ndim == 2:
        lane = lax.broadcasted_iota(jnp.int32, flat.shape, 1)
    right = jnp.where(lane < cells_y - 1, pltpu.roll(flat, cells_y - 1, axis), 0.0)
    left = jnp.where(lane >= 1, pltpu.roll(flat, 1, axis), 0.0)
    return right + left


def relax_kernel(summed, smooth, out, inner, own_g, own_s, own_out, wide, once):
    cells_x, cells_z, cells_y = summed.shape
    for ref in (wide, once):
        blank = jnp.zeros((1, *ref.shape[1:]), jnp.float32)
        ref[pl.ds(0, 1)] = blank
        ref[pl.ds(cells_x + 1, 1)] = blank

    @pl.loop(0, cells_x // CHUNK, unroll=2)
    def _(q):
        at = pl.ds(q * CHUNK + 1, CHUNK)
        blank = jnp.zeros((CHUNK, 1, cells_y), jnp.float32)
        for ref in (wide, once):
            ref[at, pl.ds(MID - 1, 1), :] = blank
            ref[at, pl.ds(MID + cells_z, 1), :] = blank
        wide[at, pl.ds(MID, cells_z), :] = summed[pl.ds(q * CHUNK, CHUNK)]

    def relaxed(ref, x, factor):
        at = lambda dx, dz: ref[pl.ds(x + 1 + dx, CHUNK), pl.ds(MID + dz, cells_z), :]
        v = at(0, 0)
        near = at(1, 0) + at(-1, 0) + at(0, 1) + at(0, -1)
        flat = v.reshape(CHUNK * cells_z // 8, 8, cells_y)
        near = near + shifted_y(flat).reshape(v.shape)
        return v + factor * (near - 6.0 * v)

    @pl.loop(0, cells_x // CHUNK, unroll=2)
    def _(q):
        x = q * CHUNK
        factor = smooth[pl.ds(x, CHUNK)]
        once[pl.ds(x + 1, CHUNK), pl.ds(MID, cells_z), :] = relaxed(wide, x, factor)
        g = summed[pl.ds(x, CHUNK)]
        for i, k in enumerate((0, cells_z - 1)):
            own_g[i, pl.ds(x, CHUNK)] = g[:, k]
        for i, k in enumerate((0, 1, cells_z - 2, cells_z - 1)):
            own_s[i, pl.ds(x, CHUNK)] = factor[:, k]

    depth = lax.broadcasted_iota(jnp.int32, (1, cells_z, cells_y), 1)
    between = (depth >= 2) & (depth < cells_z - 2)

    def sweep(q, total):
        x = q * CHUNK
        value = relaxed(once, x, smooth[pl.ds(x, CHUNK)])
        out[pl.ds(x, CHUNK)] = value
        for i, k in enumerate((0, 1, cells_z - 2, cells_z - 1)):
            own_out[i, pl.ds(x, CHUNK)] = value[:, k]
        squares = jnp.where(between, value * value, 0.0)
        return total + jnp.sum(squares.reshape(CHUNK * cells_z // 8, 8, cells_y), axis=0)

    inner[...] = lax.fori_loop(
        0, cells_x // CHUNK, sweep, jnp.zeros((8, cells_y), jnp.float32), unroll=2
    )


def edge_kernel(
    smoothed_in, inner, own_g, own_s, own_out, low_sum, high_sum, low_one, high_one,
    smoothed, square, planes,
):
    cells_x, cells_z, cells_y = smoothed.shape
    smoothed[...] = smoothed_in[...]
    count = cells_x // 4
    blank = jnp.zeros((8, cells_y), jnp.float32)
    total = inner[...]
    for side, (sums, smooth, present) in enumerate(
        ((low_sum, low_one, has_sides()[0]), (high_sum, high_one, has_sides()[1]))
    ):
        for k in range(4):
            planes[k, pl.ds(0, 8)] = blank
            planes[k, pl.ds(8 + cells_x, 8)] = blank

        @pl.loop(0, count)
        def _(q, sums=sums, smooth=smooth, present=present):
            at = pl.ds(8 + 4 * q, 4)
            for k in range(2):
                planes[k, at] = jnp.where(present, sums[k * count + q], 0.0)
            planes[2, at] = jnp.where(present, smooth[cells_x + q], 0.0)

        def near(k):
            at = lambda dx: planes[k, pl.ds(8 + dx, cells_x)]
            return at(1) + at(-1) + shifted_y(at(0))

        whole = pl.ds(8, cells_x)
        first, second, factor = planes[0, whole], planes[1, whole], planes[2, whole]
        outside = first + factor * (near(0) + second + own_g[side] - 6.0 * first)
        edge, inside = (0, 1) if side == 0 else (3, 2)
        change = own_s[edge] * first
        planes[3, whole] = change
        value = own_out[edge] + change + own_s[edge] * (near(3) - 6.0 * change + outside)
        beside = own_out[inside] + own_s[inside] * change
        squares = value * value + beside * beside
        total = total + jnp.sum(squares.reshape(cells_x // 8, 8, cells_y), axis=0)
        planes[0, whole] = value
        planes[1, whole] = beside
        rows = (0, 1) if side == 0 else (cells_z - 1, cells_z - 2)

        @pl.loop(0, count)
        def _(q, rows=rows):
            for k, z in enumerate(rows):
                smoothed[pl.ds(4 * q, 4), pl.ds(z, 1), :] = planes[k, pl.ds(8 + 4 * q, 4)][:, None]

    row = jnp.sum(total, axis=0, keepdims=True)
    square[...] = jnp.broadcast_to(row[None], square.shape)


def third_kernel(u_two, side, model, aniso_c, low, high, change, pad, first_z, dep):
    cells_x = change.shape[0]
    fill_depth(pad, lambda at: u_two[at], lambda at: low[at], lambda at: high[at])
    depth_pass(pad, first_z, dep)

    @pl.loop(0, cells_x // CHUNK, unroll=2)
    def _(step):
        x = step * CHUNK
        at = pl.ds(x, CHUNK)
        change[at] = model[at] * (side[at] + dep[at] + aniso_c[at] * crossing(first_z, x))


def close_kernel(squares, smoothed, model, u_two, carry, change, model_next, grad_dir, wave_next):
    cells_x, cells_z, cells_y = smoothed.shape
    rows = grad_dir.shape[0]
    total = jnp.sum(jnp.sum(squares[...], axis=0), axis=1, keepdims=True)
    cells = cells_x * depth_range(cells_z)[1] * cells_y
    scale = lax.rsqrt(total / cells + 1e-06)
    scale = jnp.broadcast_to(scale, (8, cells_y))[None]

    def factor(value):
        flat = value.reshape(value.shape[0] * cells_z // 8, 8, cells_y) * scale
        return flat.reshape(value.shape)

    @pl.loop(0, cells_x // CHUNK)
    def _(step):
        at = pl.ds(step * CHUNK, CHUNK)
        shrink = 1.0 - 0.25 * jnp.tanh(factor(smoothed[at]))
        wave_next[0, at] = 2.0 * u_two[at] + carry[at] + change[at] * shrink

    _, core, chip = position()
    at = pl.ds((2 * chip + core) * rows, rows)
    direction = factor(smoothed[at])
    grad_dir[...] = direction
    model_next[...] = model[at] * (1.0 - 0.25 * jnp.tanh(direction))


def shift(low_edge, high_edge):
    count = lax.axis_size(DEPTH)
    forward = [(i, (i + 1) % count) for i in range(count)]
    backward = [(target, source) for source, target in forward]
    return lax.ppermute(high_edge, DEPTH, forward), lax.ppermute(low_edge, DEPTH, backward)


def body(
    u_prev,
    u_cur,
    a_prev,
    a_cur,
    model,
    aniso_h,
    aniso_c,
    smooth_coef,
    bin_onehot,
    shot_group,
    src_cell,
    rec_cell,
    src_wave,
    rec_data,
):
    _, cells_x, cells_z, cells_y = u_cur.shape
    rows = model.shape[0]
    peers = lax.axis_size(PEERS)
    slab = f32(cells_x, cells_z, cells_y)
    scratch = lambda *shape: pltpu.VMEM(shape, jnp.float32)
    pad = scratch(cells_x, cells_z + 2 * MID, cells_y)
    first_z = scratch(cells_x + 2 * REACH, cells_z, cells_y)
    padded_rows = first_z
    dep = scratch(cells_x, cells_z, cells_y)
    pair = scratch(2, cells_x, cells_z, cells_y)
    work = 80 * cells_x * cells_z * cells_y

    spread = call(
        spread_kernel,
        (model, aniso_h, aniso_c, smooth_coef),
        0,
        f32(peers, 4, rows, cells_z, cells_y),
        (
            scratch(4, rows, cells_z, cells_y),
            pltpu.SemaphoreType.DMA((4,)),
            pltpu.SemaphoreType.DMA((peers,)),
        ),
        hbm_in=range(4),
        hbm_out=(0,),
        grant=62,
    )
    mine = lax.all_to_all(spread, PEERS, 0, 0, tiled=True)

    edges = lambda start: jnp.concatenate(
        [lax.slice_in_dim(v, start, start + REACH, axis=2) for v in (u_cur, a_cur)]
    )
    low, high = shift(edges(0), edges(cells_z - REACH))
    *parts, weight = call(
        open_kernel,
        (src_cell, src_wave, bin_onehot, shot_group, rec_cell, rec_data)
        + (u_prev, u_cur, a_prev, a_cur, low, high),
        4,
        (slab,) * 8 + (f32(1, cells_z, cells_y),),
        (pair,) * 6
        + (scratch(1, cells_z, cells_y), padded_rows, pad, first_z)
        + (pltpu.SemaphoreType.DMA((2, 2)), pltpu.SemaphoreType.DMA((9,))),
        2 * work,
        hbm_in=range(6, 10),
        hbm_out=range(9),
        grant=61,
    )
    other = lax.ppermute(mine, "core", SWAP)
    *parts, weight, adjoint = call(
        fetch_kernel,
        (*parts, weight, a_cur),
        0,
        (slab,) * 8 + (f32(1, cells_z, cells_y), f32(*a_cur.shape)),
        (pltpu.SemaphoreType.DMA((10,)),),
        hbm_in=range(10),
        grant=49,
    )
    payload = f32(cells_x + peers, REACH, cells_y)
    u_one, a_one, grad, model_slab, h_slab, c_slab, smooth_slab, low_edge, high_edge = call(
        first_kernel,
        (mine, other, adjoint, *parts),
        0,
        (slab,) * 7 + (payload, payload),
        (),
        20 * slab.size,
    )
    low_one, high_one = shift(low_edge, high_edge)
    base, side, carry = call(
        side_one_kernel,
        (src_cell, src_wave, u_one, u_cur[0], h_slab),
        2,
        (slab, slab, slab),
        (padded_rows,),
        work // 2,
    )
    split = f32(peers, rows, cells_z, cells_y)
    edge = f32(cells_x, REACH, cells_y)
    u_two, keep, send = call(
        second_kernel,
        (u_one, base, side, a_one, grad, weight, model_slab, c_slab, low_one, high_one),
        0,
        (slab, split, split),
        (pad, first_z, dep),
        work,
    )
    chip_sum = keep + lax.ppermute(send, "core", SWAP)
    shares = lax.all_to_all(chip_sum, PEERS, 0, 0, tiled=True)
    total = call(sum_kernel, (shares,), 0, split)
    mine = lax.all_to_all(total, PEERS, 0, 0, tiled=True)
    other = lax.ppermute(mine, "core", SWAP)
    low_edge, high_edge = call(rim_kernel, (u_two,), 0, (edge, edge))
    low_two, high_two = shift(low_edge, high_edge)
    payload = f32(2 * peers, 4, cells_y)
    summed, low_edge, high_edge = call(
        join_kernel, (mine, other), 0, (slab, payload, payload)
    )
    low_sum, high_sum = shift(low_edge, high_edge)
    side, low_two, high_two = call(
        side_two_kernel,
        (u_two, h_slab, low_two, high_two),
        0,
        (slab, edge, edge),
        (padded_rows, pltpu.SemaphoreType.DMA((2,))),
        work // 2,
        hbm_in=(2, 3),
    )
    edges = f32(4, cells_x, cells_y)
    smoothed, inner, own_g, own_s, own_out = call(
        relax_kernel,
        (summed, smooth_slab),
        0,
        (slab, f32(8, cells_y), f32(2, cells_x, cells_y), edges, edges),
        (scratch(cells_x + 2, cells_z + 2 * MID, cells_y),) * 2,
        40 * slab.size,
    )
    change = call(
        third_kernel,
        (u_two, side, model_slab, c_slab, low_two, high_two),
        0,
        slab,
        (pad, first_z, dep),
        work,
    )
    smoothed, square = call(
        edge_kernel,
        (smoothed, inner, own_g, own_s, own_out, low_sum, high_sum, low_one, high_one),
        0,
        (slab, f32(lax.axis_size(DEPTH), 1, cells_y)),
        (scratch(4, cells_x + 16, cells_y),),
        4 * slab.size,
    )
    squares = lax.all_to_all(square, DEPTH, 0, 0, tiled=True)
    share = f32(rows, cells_z, cells_y)
    return call(
        close_kernel,
        (squares, smoothed, model_slab, u_two, carry, change),
        0,
        (share, share, f32(1, cells_x, cells_z, cells_y)),
        (),
        20 * slab.size,
    )


def solution(mesh):
    mesh = jax.sharding.Mesh(
        mesh.devices.reshape(2, 8, 2, 2, 4), ("xh", "z", "core", "xl", "y")
    )
    return jax.shard_map(
        body,
        mesh=mesh,
        in_specs=(
            P(SHOT, None, DEPTH, None),
            P(SHOT, None, DEPTH, None),
            P(SHOT, None, DEPTH, None),
            P(SHOT, None, DEPTH, None),
            P(SHOT, DEPTH, None),
            P(SHOT, DEPTH, None),
            P(SHOT, DEPTH, None),
            P(SHOT, DEPTH, None),
            P(None, DEPTH, None),
            P(SHOT),
            P(SHOT),
            P(SHOT, None),
            P(SHOT, None),
            P(SHOT, None, None),
        ),
        out_specs=(
            P(SHOT, DEPTH, None),
            P(SHOT, DEPTH, None),
            P(SHOT, None, DEPTH, None),
        ),
        check_vma=False,
    )
```

```python
import jax
import jax.numpy as jnp
from jax import lax
from jax.experimental import pallas as pl
from jax.experimental.pallas import tpu as pltpu
from jax.sharding import PartitionSpec as P


second_coef = (-205.0 / 72.0, 8.0 / 5.0, -1.0 / 5.0, 8.0 / 315.0, -1.0 / 560.0)
first_coef = (0.8, -0.2, 4.0 / 105.0, -1.0 / 280.0)

SHOT = ("xh", "z", "core")
DEPTH = ("xl", "y")
PEERS = ("xh", "z")
SWAP = [(0, 1), (1, 0)]
REACH = 4
MID = 8
CHUNK = 4
BLOCK = 16
VMEM = pl.BlockSpec(memory_space=pltpu.VMEM)
SMEM = pl.BlockSpec(memory_space=pltpu.SMEM)
HBM = pl.BlockSpec(memory_space=pltpu.HBM)


def f32(*shape):
    return jax.ShapeDtypeStruct(shape, jnp.float32)


def call(kernel, args, smem, outs, scratch=(), flops=0, hbm_in=(), hbm_out=(), grant=16):
    bytes_accessed = 4 * sum(a.size for a in args)
    spec = lambda i: SMEM if i < smem else HBM if i in hbm_in else VMEM
    single = not isinstance(outs, tuple)
    out_specs = [HBM if i in hbm_out else VMEM for i in range(1 if single else len(outs))]
    return pl.pallas_call(
        kernel,
        out_shape=outs,
        in_specs=[spec(i) for i in range(len(args))],
        out_specs=out_specs[0] if single else tuple(out_specs),
        scratch_shapes=list(scratch),
        cost_estimate=pl.CostEstimate(
            flops=flops, bytes_accessed=bytes_accessed, transcendentals=0
        ),
        compiler_params=pltpu.CompilerParams(vmem_limit_bytes=grant * 2**20),
    )(*args)


def position():
    layer = lax.axis_index("xl") * lax.axis_size("y") + lax.axis_index("y")
    chip = lax.axis_index("xh") * lax.axis_size("z") + lax.axis_index("z")
    return layer, lax.axis_index("core"), chip


def fill_rows(rows, read):
    cells_x = rows.shape[0] - 2 * REACH
    zeros = jnp.zeros((REACH, *rows.shape[1:]), jnp.float32)
    rows[pl.ds(0, REACH)] = zeros
    rows[pl.ds(REACH + cells_x, REACH)] = zeros

    @pl.loop(0, cells_x // CHUNK)
    def _(step):
        x = step * CHUNK
        rows[pl.ds(REACH + x, CHUNK)] = read(pl.ds(x, CHUNK))


def has_sides():
    layer, _, _ = position()
    return layer > 0, layer < lax.axis_size("xl") * lax.axis_size("y") - 1


def depth_range(cells_z):
    layer, _, _ = position()
    return layer * cells_z, cells_z * lax.axis_size("xl") * lax.axis_size("y")


def fill_depth(pad, read, low, high):
    cells_x, cells_z = pad.shape[0], pad.shape[1] - 2 * MID
    below, above = has_sides()

    @pl.loop(0, cells_x // CHUNK, unroll=2)
    def _(step):
        at = pl.ds(step * CHUNK, CHUNK)
        pad[at, pl.ds(MID, cells_z), :] = read(at)
        pad[at, pl.ds(MID - REACH, REACH), :] = jnp.where(below, low(at), 0.0)
        pad[at, pl.ds(MID + cells_z, REACH), :] = jnp.where(above, high(at), 0.0)


def depth_pass(pad, first_z, second_z):
    cells_x, cells_z = second_z.shape[0], second_z.shape[1]
    zeros = jnp.zeros((REACH, *first_z.shape[1:]), jnp.float32)
    first_z[pl.ds(0, REACH)] = zeros
    first_z[pl.ds(REACH + cells_x, REACH)] = zeros

    @pl.loop(0, cells_x // CHUNK, unroll=4)
    def _(step):
        x = step * CHUNK
        at = lambda k: pad[pl.ds(x, CHUNK), pl.ds(MID + k, cells_z), :]
        two = second_coef[0] * at(0)
        one = None
        for k in range(1, 5):
            above, below = at(k), at(-k)
            two = two + second_coef[k] * (above + below)
            term = first_coef[k - 1] * (above - below)
            one = term if one is None else one + term
        second_z[pl.ds(x, CHUNK)] = two
        first_z[pl.ds(REACH + x, CHUNK)] = one


def lateral_masks(cells_y):
    lane = lax.broadcasted_iota(jnp.int32, (1, 8, cells_y), 2)
    up = [jnp.where(lane < cells_y - k, second_coef[k], 0.0) for k in range(1, 5)]
    down = [jnp.where(lane >= k, second_coef[k], 0.0) for k in range(1, 5)]
    return up, down


def lateral(rows, x, masks):
    up, down = masks
    at = lambda k: rows[pl.ds(REACH + x + k, CHUNK)]
    v = at(0)
    cells_z, cells_y = v.shape[1:]
    total = (2.0 * second_coef[0]) * v
    for k in range(1, 5):
        total = total + second_coef[k] * (at(k) + at(-k))
    flat = v.reshape(CHUNK * cells_z // 8, 8, cells_y)
    along_y = None
    for k in range(1, 5):
        term = up[k - 1] * pltpu.roll(flat, cells_y - k, 2) + down[k - 1] * pltpu.roll(flat, k, 2)
        along_y = term if along_y is None else along_y + term
    return total + along_y.reshape(v.shape)


def crossing(first_z, x):
    at = lambda k: first_z[pl.ds(REACH + x + k, CHUNK)]
    total = None
    for k in range(1, 5):
        term = first_coef[k - 1] * (at(k) - at(-k))
        total = term if total is None else total + term
    return total


def add_at(ref, cell, amount):
    cells_z, cells_y = ref.shape[1], ref.shape[2]
    z_start, depth_cells = depth_range(cells_z)
    row = cell // cells_y
    x, z = row // depth_cells, row % depth_cells - z_start

    @pl.when((z >= 0) & (z < cells_z))
    def _():
        lane = lax.broadcasted_iota(jnp.int32, (1, 1, cells_y), 2)
        at = (pl.ds(x, 1), pl.ds(z, 1), slice(None))
        ref[at] = ref[at] + jnp.where(lane == cell % cells_y, amount, 0.0)


def spread_kernel(model, aniso_h, aniso_c, smooth, out, own, sem_in, sem_out):
    arrays = (model, aniso_h, aniso_c, smooth)
    loads = [pltpu.make_async_copy(ref, own.at[j], sem_in.at[j]) for j, ref in enumerate(arrays)]
    for load in loads:
        load.start()
    for load in loads:
        load.wait()
    sends = [pltpu.make_async_copy(own, out.at[p], sem_out.at[p]) for p in range(out.shape[0])]
    for send in sends:
        send.start()
    for send in sends:
        send.wait()


def place_receivers(out, rec_cell, rec_data):
    cells_x, cells_z, cells_y = out.shape
    z_start, depth_cells = depth_range(cells_z)
    cell = rec_cell[...]
    row = cell // cells_y
    z = row % depth_cells - z_start
    key = jnp.where((z >= 0) & (z < cells_z), row // depth_cells * cells_z + z, -1)
    y = cell % cells_y
    count = cell.shape[1]
    lanes = jnp.where(
        lax.broadcasted_iota(jnp.int32, (cells_y, count), 0) == y, 1.0, 0.0
    ).astype(jnp.bfloat16)
    rest, terms = rec_data[0, pl.ds(0, 1), :], []
    for _ in range(3):
        term = rest.astype(jnp.bfloat16).astype(jnp.float32)
        terms.append(term)
        rest = rest - term
    block = min(16, cells_x)

    @pl.loop(0, cells_x // block)
    def _(step):
        first = step * block * cells_z
        index = first + lax.broadcasted_iota(jnp.int32, (block * cells_z, count), 0)
        hit = index == key
        total = None
        for term in terms:
            left = jnp.where(hit, term, 0.0).astype(jnp.bfloat16)
            part = lax.dot_general(
                left, lanes, (((1,), (1,)), ((), ())), preferred_element_type=jnp.float32
            )
            total = part if total is None else total + part
        at = pl.ds(step * block, block)
        out[at] = out[at] + total.reshape(block, cells_z, cells_y)


def open_kernel(
    src_cell, src_wave, onehot, shot_group, rec_cell, rec_data,
    u_prev, u_cur, a_prev, a_cur, low, high,
    base_u, lat_u, dep_u, cross_u, base_a, lat_a, dep_a, cross_a, weight,
    old, now, base, lat, dep, cross, scale_row, rows, pad, first_z, sem_in, sem_out,
):
    cells_x, cells_z, cells_y = lat_u.shape
    masks = lateral_masks(cells_y)
    loads = []
    for j, (before, current) in enumerate(((u_prev, u_cur), (a_prev, a_cur))):
        loads.append(pltpu.make_async_copy(current.at[0], now.at[j], sem_in.at[j, 0]))
        loads.append(pltpu.make_async_copy(before.at[0], old.at[j], sem_in.at[j, 1]))
    for load in loads:
        load.start()
    sends = []

    def send(source, target):
        copy = pltpu.make_async_copy(source, target, sem_out.at[len(sends)])
        copy.start()
        sends.append(copy)

    blocks = onehot.shape[1]
    depth = lax.broadcasted_iota(jnp.int32, weight.shape, 1)
    value = jnp.zeros(weight.shape, jnp.float32)
    for block in range(blocks):
        scale = sum(
            onehot[shot_group[0], block, b].astype(jnp.float32) * 2.0 ** (-b)
            for b in range(onehot.shape[2])
        )
        value = jnp.where(depth // (cells_z // blocks) == block, scale, value)
    scale_row[...] = value
    send(scale_row, weight)

    targets = ((base_u, lat_u, dep_u, cross_u), (base_a, lat_a, dep_a, cross_a))
    for j in range(2):
        loads[2 * j].wait()
        loads[2 * j + 1].wait()
        fill_depth(
            pad,
            lambda at, j=j: now[j, at],
            lambda at, j=j: low[j, at],
            lambda at, j=j: high[j, at],
        )
        depth_pass(pad, first_z, dep.at[j])
        send(dep.at[j], targets[j][2])
        fill_rows(rows, lambda at, j=j: now[j, at])

        @pl.loop(0, cells_x // CHUNK)
        def _(step, j=j):
            x = step * CHUNK
            at = pl.ds(x, CHUNK)
            lat[j, at] = lateral(rows, x, masks)
            cross[j, at] = crossing(first_z, x)
            base[j, at] = 2.0 * now[j, at] - old[j, at]

        send(lat.at[j], targets[j][1])
        send(cross.at[j], targets[j][3])
        if j == 0:
            add_at(base.at[0], src_cell[0], src_wave[0, 0])
        else:
            place_receivers(base.at[1], rec_cell, rec_data)
        send(base.at[j], targets[j][0])
    for copy in sends:
        copy.wait()


def fetch_kernel(*refs):
    count = (len(refs) - 1) // 2
    sources, targets, sem = refs[:count], refs[count:-1], refs[-1]
    copies = [
        pltpu.make_async_copy(source, target, sem.at[i])
        for i, (source, target) in enumerate(zip(sources, targets))
    ]
    for copy in copies:
        copy.start()
    for copy in copies:
        copy.wait()


def first_kernel(
    mine, other, a_cur,
    base_u, lat_u, dep_u, cross_u, base_a, lat_a, dep_a, cross_a,
    u_one, a_one, grad, model, aniso_h, aniso_c, smooth, low, high,
):
    cells_x, cells_z, _ = u_one.shape
    own = position()[1] == 0

    @pl.loop(0, mine.shape[0], unroll=2)
    def _(q):
        for p in range(2):
            rows = pl.ds(q * 4 + p * 2, 2)
            pick = lambda j: jnp.where(own == (p == 0), mine[q, j], other[q, j])
            m, h, c, s = pick(0), pick(1), pick(2), pick(3)
            model[rows], aniso_h[rows], aniso_c[rows], smooth[rows] = m, h, c, s
            k_u = h * lat_u[rows] + dep_u[rows] + c * cross_u[rows]
            k_a = h * lat_a[rows] + dep_a[rows] + c * cross_a[rows]
            grad[rows] = a_cur[0, rows] * k_u
            new = base_u[rows] + m * k_u
            u_one[rows] = new
            a_one[rows] = base_a[rows] + m * k_a
            low[rows] = new[:, :REACH]
            high[rows] = new[:, cells_z - REACH :]
            edge = (pl.ds(cells_x + q, 1), pl.ds(2 * p, 2), slice(None))
            low[edge] = s[:, 0][None]
            high[edge] = s[:, cells_z - 1][None]


def band(cells_y):
    apart = lax.broadcasted_iota(jnp.int32, (cells_y, cells_y), 0)
    apart = apart - lax.broadcasted_iota(jnp.int32, (cells_y, cells_y), 1)
    value = jnp.zeros((cells_y, cells_y), jnp.float32)
    for k in range(1, 5):
        value = jnp.where(jnp.abs(apart) == k, second_coef[k], value)
    return value


def side_part(now, aniso_h, side, rows, also=None):
    cells_x, cells_z, cells_y = now.shape
    matrix = band(cells_y)
    fill_rows(rows, lambda at: now[at])
    block = min(BLOCK, cells_x)

    @pl.loop(0, cells_x // block)
    def _(step):
        x = step * block
        at = pl.ds(x, block)
        v = now[at]
        flat = v.reshape(block * cells_z, cells_y)
        along_y = jnp.dot(
            flat, matrix, precision=lax.Precision.HIGHEST, preferred_element_type=jnp.float32
        )
        total = (2.0 * second_coef[0]) * v + along_y.reshape(v.shape)
        for k in range(1, 5):
            total = total + second_coef[k] * (
                rows[pl.ds(REACH + x + k, block)] + rows[pl.ds(REACH + x - k, block)]
            )
        side[at] = aniso_h[at] * total
        if also is not None:
            also(at, v)


def side_one_kernel(src_cell, src_wave, now, old, aniso_h, base, side, carry, rows):
    def also(at, v):
        base[at] = 2.0 * v - old[at]
        carry[at] = -v

    side_part(now, aniso_h, side, rows, also)
    add_at(base, src_cell[0], src_wave[0, 1])
    add_at(carry, src_cell[0], src_wave[0, 2])


def side_two_kernel(now, aniso_h, low, high, side, low_in, high_in, rows, sem):
    copies = [
        pltpu.make_async_copy(low, low_in, sem.at[0]),
        pltpu.make_async_copy(high, high_in, sem.at[1]),
    ]
    for copy in copies:
        copy.start()
    side_part(now, aniso_h, side, rows)
    for copy in copies:
        copy.wait()


def second_kernel(
    u_one, base, side, a_one, grad, weight, model, aniso_c, low, high,
    u_two, keep, send, pad, first_z, dep,
):
    cells_x = u_two.shape[0]
    fill_depth(pad, lambda at: u_one[at], lambda at: low[at], lambda at: high[at])
    depth_pass(pad, first_z, dep)
    own = position()[1] == 0

    @pl.loop(0, cells_x // CHUNK, unroll=4)
    def _(step):
        x = step * CHUNK
        at = pl.ds(x, CHUNK)
        k_u = side[at] + dep[at] + aniso_c[at] * crossing(first_z, x)
        u_two[at] = base[at] + model[at] * k_u
        total = weight[...] * (grad[at] + a_one[at] * k_u)
        keep[step] = jnp.where(own, total[:2], total[2:])
        send[step] = jnp.where(own, total[2:], total[:2])


def rim_kernel(field, low, high):
    cells_x, cells_z, _ = field.shape

    @pl.loop(0, cells_x // CHUNK, unroll=2)
    def _(step):
        at = pl.ds(step * CHUNK, CHUNK)
        low[at] = field[at, :REACH]
        high[at] = field[at, cells_z - REACH :]


def sum_kernel(parts, out):
    total = parts[0]
    for peer in range(1, parts.shape[0]):
        total = total + parts[peer]
    for peer in range(parts.shape[0]):
        out[peer] = total


def join_kernel(mine, other, summed, low, high):
    cells_z = summed.shape[1]
    count = mine.shape[0]
    own = position()[1] == 0

    @pl.loop(0, count, unroll=2)
    def _(q):
        for p in range(2):
            rows = pl.ds(q * 4 + p * 2, 2)
            g = jnp.where(own == (p == 0), mine[q], other[q])
            summed[rows] = g
            for k in range(2):
                edge = (pl.ds(k * count + q, 1), pl.ds(2 * p, 2), slice(None))
                low[edge] = g[:, k][None]
                high[edge] = g[:, cells_z - 1 - k][None]


def shifted_y(flat):
    cells_y = flat.shape[-1]
    lane = lax.broadcasted_iota(jnp.int32, (1,) * (flat.ndim - 2) + (8, cells_y), flat.ndim - 1)
    axis = flat.ndim - 1
    if flat.ndim == 2:
        lane = lax.broadcasted_iota(jnp.int32, flat.shape, 1)
    right = jnp.where(lane < cells_y - 1, pltpu.roll(flat, cells_y - 1, axis), 0.0)
    left = jnp.where(lane >= 1, pltpu.roll(flat, 1, axis), 0.0)
    return right + left


def relax_kernel(summed, smooth, out, inner, own_g, own_s, own_out, wide, once):
    cells_x, cells_z, cells_y = summed.shape
    for ref in (wide, once):
        blank = jnp.zeros((1, *ref.shape[1:]), jnp.float32)
        ref[pl.ds(0, 1)] = blank
        ref[pl.ds(cells_x + 1, 1)] = blank

    @pl.loop(0, cells_x // CHUNK, unroll=2)
    def _(q):
        at = pl.ds(q * CHUNK + 1, CHUNK)
        blank = jnp.zeros((CHUNK, 1, cells_y), jnp.float32)
        for ref in (wide, once):
            ref[at, pl.ds(MID - 1, 1), :] = blank
            ref[at, pl.ds(MID + cells_z, 1), :] = blank
        wide[at, pl.ds(MID, cells_z), :] = summed[pl.ds(q * CHUNK, CHUNK)]

    def relaxed(ref, x, factor):
        at = lambda dx, dz: ref[pl.ds(x + 1 + dx, CHUNK), pl.ds(MID + dz, cells_z), :]
        v = at(0, 0)
        near = at(1, 0) + at(-1, 0) + at(0, 1) + at(0, -1)
        flat = v.reshape(CHUNK * cells_z // 8, 8, cells_y)
        near = near + shifted_y(flat).reshape(v.shape)
        return v + factor * (near - 6.0 * v)

    @pl.loop(0, cells_x // CHUNK, unroll=2)
    def _(q):
        x = q * CHUNK
        factor = smooth[pl.ds(x, CHUNK)]
        once[pl.ds(x + 1, CHUNK), pl.ds(MID, cells_z), :] = relaxed(wide, x, factor)
        g = summed[pl.ds(x, CHUNK)]
        for i, k in enumerate((0, cells_z - 1)):
            own_g[i, pl.ds(x, CHUNK)] = g[:, k]
        for i, k in enumerate((0, 1, cells_z - 2, cells_z - 1)):
            own_s[i, pl.ds(x, CHUNK)] = factor[:, k]

    depth = lax.broadcasted_iota(jnp.int32, (1, cells_z, cells_y), 1)
    between = (depth >= 2) & (depth < cells_z - 2)

    def sweep(q, total):
        x = q * CHUNK
        value = relaxed(once, x, smooth[pl.ds(x, CHUNK)])
        out[pl.ds(x, CHUNK)] = value
        for i, k in enumerate((0, 1, cells_z - 2, cells_z - 1)):
            own_out[i, pl.ds(x, CHUNK)] = value[:, k]
        squares = jnp.where(between, value * value, 0.0)
        return total + jnp.sum(squares.reshape(CHUNK * cells_z // 8, 8, cells_y), axis=0)

    inner[...] = lax.fori_loop(
        0, cells_x // CHUNK, sweep, jnp.zeros((8, cells_y), jnp.float32), unroll=2
    )


def edge_kernel(
    smoothed_in, inner, own_g, own_s, own_out, low_sum, high_sum, low_one, high_one,
    smoothed, square, planes,
):
    cells_x, cells_z, cells_y = smoothed.shape
    smoothed[...] = smoothed_in[...]
    count = cells_x // 4
    blank = jnp.zeros((8, cells_y), jnp.float32)
    total = inner[...]
    for side, (sums, smooth, present) in enumerate(
        ((low_sum, low_one, has_sides()[0]), (high_sum, high_one, has_sides()[1]))
    ):
        for k in range(4):
            planes[k, pl.ds(0, 8)] = blank
            planes[k, pl.ds(8 + cells_x, 8)] = blank

        @pl.loop(0, count, unroll=2)
        def _(q, sums=sums, smooth=smooth, present=present):
            at = pl.ds(8 + 4 * q, 4)
            for k in range(2):
                planes[k, at] = jnp.where(present, sums[k * count + q], 0.0)
            planes[2, at] = jnp.where(present, smooth[cells_x + q], 0.0)

        def near(k):
            at = lambda dx: planes[k, pl.ds(8 + dx, cells_x)]
            return at(1) + at(-1) + shifted_y(at(0))

        whole = pl.ds(8, cells_x)
        first, second, factor = planes[0, whole], planes[1, whole], planes[2, whole]
        outside = first + factor * (near(0) + second + own_g[side] - 6.0 * first)
        edge, inside = (0, 1) if side == 0 else (3, 2)
        change = own_s[edge] * first
        planes[3, whole] = change
        value = own_out[edge] + change + own_s[edge] * (near(3) - 6.0 * change + outside)
        beside = own_out[inside] + own_s[inside] * change
        squares = value * value + beside * beside
        total = total + jnp.sum(squares.reshape(cells_x // 8, 8, cells_y), axis=0)
        planes[0, whole] = value
        planes[1, whole] = beside
        rows = (0, 1) if side == 0 else (cells_z - 1, cells_z - 2)

        @pl.loop(0, count, unroll=2)
        def _(q, rows=rows):
            for k, z in enumerate(rows):
                smoothed[pl.ds(4 * q, 4), pl.ds(z, 1), :] = planes[k, pl.ds(8 + 4 * q, 4)][:, None]

    row = jnp.sum(total, axis=0, keepdims=True)
    square[...] = jnp.broadcast_to(row[None], square.shape)


def third_kernel(u_two, side, model, aniso_c, low, high, change, pad, first_z, dep):
    cells_x = change.shape[0]
    fill_depth(pad, lambda at: u_two[at], lambda at: low[at], lambda at: high[at])
    depth_pass(pad, first_z, dep)

    @pl.loop(0, cells_x // CHUNK, unroll=2)
    def _(step):
        x = step * CHUNK
        at = pl.ds(x, CHUNK)
        change[at] = model[at] * (side[at] + dep[at] + aniso_c[at] * crossing(first_z, x))


def shifted_y(flat):
    cells_y = flat.shape[-1]
    lane = lax.broadcasted_iota(jnp.int32, (1,) * (flat.ndim - 2) + (8, cells_y), flat.ndim - 1)
    axis = flat.ndim - 1
    if flat.ndim == 2:
        lane = lax.broadcasted_iota(jnp.int32, flat.shape, 1)
    right = jnp.where(lane < cells_y - 1, pltpu.roll(flat, cells_y - 1, axis), 0.0)
    left = jnp.where(lane >= 1, pltpu.roll(flat, 1, axis), 0.0)
    return right + left


def relax_kernel(summed, smooth, out, inner, own_g, own_s, own_out, wide, once):
    cells_x, cells_z, cells_y = summed.shape
    for ref in (wide, once):
        blank = jnp.zeros((1, *ref.shape[1:]), jnp.float32)
        ref[pl.ds(0, 1)] = blank
        ref[pl.ds(cells_x + 1, 1)] = blank

    @pl.loop(0, cells_x // CHUNK, unroll=2)
    def _(q):
        at = pl.ds(q * CHUNK + 1, CHUNK)
        blank = jnp.zeros((CHUNK, 1, cells_y), jnp.float32)
        for ref in (wide, once):
            ref[at, pl.ds(MID - 1, 1), :] = blank
            ref[at, pl.ds(MID + cells_z, 1), :] = blank
        wide[at, pl.ds(MID, cells_z), :] = summed[pl.ds(q * CHUNK, CHUNK)]

    def relaxed(ref, x, factor):
        at = lambda dx, dz: ref[pl.ds(x + 1 + dx, CHUNK), pl.ds(MID + dz, cells_z), :]
        v = at(0, 0)
        near = at(1, 0) + at(-1, 0) + at(0, 1) + at(0, -1)
        flat = v.reshape(CHUNK * cells_z // 8, 8, cells_y)
        near = near + shifted_y(flat).reshape(v.shape)
        return v + factor * (near - 6.0 * v)

    @pl.loop(0, cells_x // CHUNK, unroll=2)
    def _(q):
        x = q * CHUNK
        factor = smooth[pl.ds(x, CHUNK)]
        once[pl.ds(x + 1, CHUNK), pl.ds(MID, cells_z), :] = relaxed(wide, x, factor)
        g = summed[pl.ds(x, CHUNK)]
        for i, k in enumerate((0, cells_z - 1)):
            own_g[i, pl.ds(x, CHUNK)] = g[:, k]
        for i, k in enumerate((0, 1, cells_z - 2, cells_z - 1)):
            own_s[i, pl.ds(x, CHUNK)] = factor[:, k]

    depth = lax.broadcasted_iota(jnp.int32, (1, cells_z, cells_y), 1)
    between = (depth >= 2) & (depth < cells_z - 2)

    def sweep(q, total):
        x = q * CHUNK
        value = relaxed(once, x, smooth[pl.ds(x, CHUNK)])
        out[pl.ds(x, CHUNK)] = value
        for i, k in enumerate((0, 1, cells_z - 2, cells_z - 1)):
            own_out[i, pl.ds(x, CHUNK)] = value[:, k]
        squares = jnp.where(between, value * value, 0.0)
        return total + jnp.sum(squares.reshape(CHUNK * cells_z // 8, 8, cells_y), axis=0)

    inner[...] = lax.fori_loop(
        0, cells_x // CHUNK, sweep, jnp.zeros((8, cells_y), jnp.float32), unroll=2
    )


def edge_kernel(
    smoothed_in, inner, own_g, own_s, own_out, low_sum, high_sum, low_one, high_one,
    smoothed, square, planes,
):
    cells_x, cells_z, cells_y = smoothed.shape
    smoothed[...] = smoothed_in[...]
    count = cells_x // 4
    blank = jnp.zeros((8, cells_y), jnp.float32)
    total = inner[...]
    for side, (sums, smooth, present) in enumerate(
        ((low_sum, low_one, has_sides()[0]), (high_sum, high_one, has_sides()[1]))
    ):
        for k in range(4):
            planes[k, pl.ds(0, 8)] = blank
            planes[k, pl.ds(8 + cells_x, 8)] = blank

        @pl.loop(0, count)
        def _(q, sums=sums, smooth=smooth, present=present):
            at = pl.ds(8 + 4 * q, 4)
            for k in range(2):
                planes[k, at] = jnp.where(present, sums[k * count + q], 0.0)
            planes[2, at] = jnp.where(present, smooth[cells_x + q], 0.0)

        def near(k):
            at = lambda dx: planes[k, pl.ds(8 + dx, cells_x)]
            return at(1) + at(-1) + shifted_y(at(0))

        whole = pl.ds(8, cells_x)
        first, second, factor = planes[0, whole], planes[1, whole], planes[2, whole]
        outside = first + factor * (near(0) + second + own_g[side] - 6.0 * first)
        edge, inside = (0, 1) if side == 0 else (3, 2)
        change = own_s[edge] * first
        planes[3, whole] = change
        value = own_out[edge] + change + own_s[edge] * (near(3) - 6.0 * change + outside)
        beside = own_out[inside] + own_s[inside] * change
        squares = value * value + beside * beside
        total = total + jnp.sum(squares.reshape(cells_x // 8, 8, cells_y), axis=0)
        planes[0, whole] = value
        planes[1, whole] = beside
        rows = (0, 1) if side == 0 else (cells_z - 1, cells_z - 2)

        @pl.loop(0, count)
        def _(q, rows=rows):
            for k, z in enumerate(rows):
                smoothed[pl.ds(4 * q, 4), pl.ds(z, 1), :] = planes[k, pl.ds(8 + 4 * q, 4)][:, None]

    row = jnp.sum(total, axis=0, keepdims=True)
    square[...] = jnp.broadcast_to(row[None], square.shape)


def third_kernel(u_two, side, model, aniso_c, low, high, change, pad, first_z, dep):
    cells_x = change.shape[0]
    fill_depth(pad, lambda at: u_two[at], lambda at: low[at], lambda at: high[at])
    depth_pass(pad, first_z, dep)

    @pl.loop(0, cells_x // CHUNK, unroll=2)
    def _(step):
        x = step * CHUNK
        at = pl.ds(x, CHUNK)
        change[at] = model[at] * (side[at] + dep[at] + aniso_c[at] * crossing(first_z, x))


def close_kernel(squares, smoothed, model, u_two, carry, change, model_next, grad_dir, wave_next):
    cells_x, cells_z, cells_y = smoothed.shape
    rows = grad_dir.shape[0]
    total = jnp.sum(jnp.sum(squares[...], axis=0), axis=1, keepdims=True)
    cells = cells_x * depth_range(cells_z)[1] * cells_y
    scale = lax.rsqrt(total / cells + 1e-06)
    scale = jnp.broadcast_to(scale, (8, cells_y))[None]

    def factor(value):
        flat = value.reshape(value.shape[0] * cells_z // 8, 8, cells_y) * scale
        return flat.reshape(value.shape)

    @pl.loop(0, cells_x // CHUNK)
    def _(step):
        at = pl.ds(step * CHUNK, CHUNK)
        shrink = 1.0 - 0.25 * jnp.tanh(factor(smoothed[at]))
        wave_next[0, at] = 2.0 * u_two[at] + carry[at] + change[at] * shrink

    _, core, chip = position()
    at = pl.ds((2 * chip + core) * rows, rows)
    direction = factor(smoothed[at])
    grad_dir[...] = direction
    model_next[...] = model[at] * (1.0 - 0.25 * jnp.tanh(direction))


def shift(low_edge, high_edge):
    count = lax.axis_size(DEPTH)
    forward = [(i, (i + 1) % count) for i in range(count)]
    backward = [(target, source) for source, target in forward]
    return lax.ppermute(high_edge, DEPTH, forward), lax.ppermute(low_edge, DEPTH, backward)


def body(
    u_prev,
    u_cur,
    a_prev,
    a_cur,
    model,
    aniso_h,
    aniso_c,
    smooth_coef,
    bin_onehot,
    shot_group,
    src_cell,
    rec_cell,
    src_wave,
    rec_data,
):
    _, cells_x, cells_z, cells_y = u_cur.shape
    rows = model.shape[0]
    peers = lax.axis_size(PEERS)
    slab = f32(cells_x, cells_z, cells_y)
    scratch = lambda *shape: pltpu.VMEM(shape, jnp.float32)
    pad = scratch(cells_x, cells_z + 2 * MID, cells_y)
    first_z = scratch(cells_x + 2 * REACH, cells_z, cells_y)
    padded_rows = first_z
    dep = scratch(cells_x, cells_z, cells_y)
    pair = scratch(2, cells_x, cells_z, cells_y)
    work = 80 * cells_x * cells_z * cells_y

    spread = call(
        spread_kernel,
        (model, aniso_h, aniso_c, smooth_coef),
        0,
        f32(peers, 4, rows, cells_z, cells_y),
        (
            scratch(4, rows, cells_z, cells_y),
            pltpu.SemaphoreType.DMA((4,)),
            pltpu.SemaphoreType.DMA((peers,)),
        ),
        hbm_in=range(4),
        hbm_out=(0,),
        grant=62,
    )
    mine = lax.all_to_all(spread, PEERS, 0, 0, tiled=True)

    edges = lambda start: jnp.concatenate(
        [lax.slice_in_dim(v, start, start + REACH, axis=2) for v in (u_cur, a_cur)]
    )
    low, high = shift(edges(0), edges(cells_z - REACH))
    *parts, weight = call(
        open_kernel,
        (src_cell, src_wave, bin_onehot, shot_group, rec_cell, rec_data)
        + (u_prev, u_cur, a_prev, a_cur, low, high),
        4,
        (slab,) * 8 + (f32(1, cells_z, cells_y),),
        (pair,) * 6
        + (scratch(1, cells_z, cells_y), padded_rows, pad, first_z)
        + (pltpu.SemaphoreType.DMA((2, 2)), pltpu.SemaphoreType.DMA((9,))),
        2 * work,
        hbm_in=range(6, 10),
        hbm_out=range(9),
        grant=61,
    )
    other = lax.ppermute(mine, "core", SWAP)
    *parts, weight, adjoint = call(
        fetch_kernel,
        (*parts, weight, a_cur),
        0,
        (slab,) * 8 + (f32(1, cells_z, cells_y), f32(*a_cur.shape)),
        (pltpu.SemaphoreType.DMA((10,)),),
        hbm_in=range(10),
        grant=49,
    )
    payload = f32(cells_x + peers, REACH, cells_y)
    u_one, a_one, grad, model_slab, h_slab, c_slab, smooth_slab, low_edge, high_edge = call(
        first_kernel,
        (mine, other, adjoint, *parts),
        0,
        (slab,) * 7 + (payload, payload),
        (),
        20 * slab.size,
    )
    low_one, high_one = shift(low_edge, high_edge)
    base, side, carry = call(
        side_one_kernel,
        (src_cell, src_wave, u_one, u_cur[0], h_slab),
        2,
        (slab, slab, slab),
        (padded_rows,),
        work // 2,
    )
    split = f32(peers, rows, cells_z, cells_y)
    edge = f32(cells_x, REACH, cells_y)
    u_two, keep, send = call(
        second_kernel,
        (u_one, base, side, a_one, grad, weight, model_slab, c_slab, low_one, high_one),
        0,
        (slab, split, split),
        (pad, first_z, dep),
        work,
    )
    chip_sum = keep + lax.ppermute(send, "core", SWAP)
    shares = lax.all_to_all(chip_sum, PEERS, 0, 0, tiled=True)
    total = call(sum_kernel, (shares,), 0, split)
    mine = lax.all_to_all(total, PEERS, 0, 0, tiled=True)
    other = lax.ppermute(mine, "core", SWAP)
    low_edge, high_edge = call(rim_kernel, (u_two,), 0, (edge, edge))
    low_two, high_two = shift(low_edge, high_edge)
    payload = f32(2 * peers, 4, cells_y)
    summed, low_edge, high_edge = call(
        join_kernel, (mine, other), 0, (slab, payload, payload)
    )
    low_sum, high_sum = shift(low_edge, high_edge)
    side, low_two, high_two = call(
        side_two_kernel,
        (u_two, h_slab, low_two, high_two),
        0,
        (slab, edge, edge),
        (padded_rows, pltpu.SemaphoreType.DMA((2,))),
        work // 2,
        hbm_in=(2, 3),
    )
    edges = f32(4, cells_x, cells_y)
    smoothed, inner, own_g, own_s, own_out = call(
        relax_kernel,
        (summed, smooth_slab),
        0,
        (slab, f32(8, cells_y), f32(2, cells_x, cells_y), edges, edges),
        (scratch(cells_x + 2, cells_z + 2 * MID, cells_y),) * 2,
        40 * slab.size,
    )
    change = call(
        third_kernel,
        (u_two, side, model_slab, c_slab, low_two, high_two),
        0,
        slab,
        (pad, first_z, dep),
        work,
    )
    smoothed, square = call(
        edge_kernel,
        (smoothed, inner, own_g, own_s, own_out, low_sum, high_sum, low_one, high_one),
        0,
        (slab, f32(lax.axis_size(DEPTH), 1, cells_y)),
        (scratch(4, cells_x + 16, cells_y),),
        4 * slab.size,
    )
    squares = lax.all_to_all(square, DEPTH, 0, 0, tiled=True)
    share = f32(rows, cells_z, cells_y)
    return call(
        close_kernel,
        (squares, smoothed, model_slab, u_two, carry, change),
        0,
        (share, share, f32(1, cells_x, cells_z, cells_y)),
        (),
        20 * slab.size,
    )


def solution(mesh):
    mesh = jax.sharding.Mesh(
        mesh.devices.reshape(2, 8, 2, 2, 4), ("xh", "z", "core", "xl", "y")
    )
    return jax.shard_map(
        body,
        mesh=mesh,
        in_specs=(
            P(SHOT, None, DEPTH, None),
            P(SHOT, None, DEPTH, None),
            P(SHOT, None, DEPTH, None),
            P(SHOT, None, DEPTH, None),
            P(SHOT, DEPTH, None),
            P(SHOT, DEPTH, None),
            P(SHOT, DEPTH, None),
            P(SHOT, DEPTH, None),
            P(None, DEPTH, None),
            P(SHOT),
            P(SHOT),
            P(SHOT, None),
            P(SHOT, None),
            P(SHOT, None, None),
        ),
        out_specs=(
            P(SHOT, DEPTH, None),
            P(SHOT, DEPTH, None),
            P(SHOT, None, DEPTH, None),
        ),
        check_vma=False,
    )
```
